32 devices in a mesh: dp: 8 (over y, x, core), sp: 4 (over z).
Axes of the slice: x: 2, y: 2, z: 4, core: 2. Of those that a mesh axis runs over, the one named last changes fastest.
Arguments:
- inputs: bfloat16 [16, 2048, 768], P('dp', 'sp'), may hold values from -6 to 6
- out_grad: bfloat16 [16, 2048, 768], P('dp', 'sp'), may hold values from -6 to 6
- segment_ids: int32 [16, 2048], P('dp'), may hold values from 0 to 7, as said below
- positions: int32 [16, 2048], P('dp'), may hold values from 0 to 1023, as said below
- norm1_gain: bfloat16 [768], replicated, may hold values from 0.5 to 1.5
- norm1_bias: bfloat16 [768], replicated, may hold values from -1.75 to 1.75
- norm2_gain: bfloat16 [768], replicated, may hold values from 0.5 to 1.5
- norm2_bias: bfloat16 [768], replicated, may hold values from -1.75 to 1.75
- query_weight: bfloat16 [768, 768], replicated, may hold values from -0.21875 to 0.21875
- query_bias: bfloat16 [768], replicated, may hold values from -1.75 to 1.75
- key_weight: bfloat16 [768, 64], replicated, may hold values from -0.21875 to 0.21875
- key_bias: bfloat16 [16], replicated, may hold values from -1.75 to 1.75
- value_weight: bfloat16 [768, 64], replicated, may hold values from -0.21875 to 0.21875
- value_bias: bfloat16 [64], replicated, may hold values from -1.75 to 1.75
- output_weight: bfloat16 [768, 768], replicated, may hold values from -2.5 to 2.5
- output_bias: bfloat16 [768], replicated, may hold values from -1.75 to 1.75
- hidden_weight: bfloat16 [768, 3072], replicated, may hold values from -0.21875 to 0.21875
- hidden_bias: bfloat16 [3072], replicated, may hold values from -1.75 to 1.75
- down_weight: bfloat16 [3072, 768], replicated, may hold values from -0.109375 to 0.109375
- down_bias: bfloat16 [768], replicated, may hold values from -1.75 to 1.75
Outputs:
- layer_out: bfloat16 [16, 2048, 768], P('dp', 'sp')
- input_grad: float32 [16, 2048, 768], P('dp', 'sp')
- norm1_gain_grad: float32 [768], P('sp')
- norm1_bias_grad: float32 [768], P('sp')
- norm2_gain_grad: float32 [768], P('sp')
- norm2_bias_grad: float32 [768], P('sp')
- query_weight_grad: float32 [768, 768], P('sp')
- query_bias_grad: float32 [768], P('sp')
- key_weight_grad: float32 [768, 64], P('sp')
- key_bias_grad: float32 [16], P('sp')
- value_weight_grad: float32 [768, 64], P('sp')
- value_bias_grad: float32 [64], P('sp')
- output_weight_grad: float32 [768, 768], P('sp')
- output_bias_grad: float32 [768], P('sp')
- hidden_weight_grad: float32 [768, 3072], P('sp')
- hidden_bias_grad: float32 [3072], P('sp')
- down_weight_grad: float32 [3072, 768], P('sp')
- down_bias_grad: float32 [768], P('sp')
The draws below stay inside these ranges and needn't reach their ends.
Inputs may be any that keep to these rules, and one draw needn't show every extreme that they name: `segment_ids`: document numbers of a row start at 0 and rise by one at each of its 7 boundaries, so every row holds exactly 8 documents; the first document of every row holds exactly 1024 tokens and each other document fewer. `positions`: each token's place counted from 0 at the first token of its document.
All inputs are finite; a program needn't handle non-finite values.
Results may differ from the reference program's by a relative error of at most 0.0085.
The reference program's roundings to bfloat16 on the way count: a program that leaves them out, or rounds other values in their place, can miss the bound.
Values may be sent and summed in bfloat16 or wider, within the bound.
No kernel may reach another device: no remote copies, remote signals or barrier semaphores. Data moves between devices by JAX's collectives and lax.ppermute only.
A program may use at most 256 MiB of HBM per device.

```python
import jax
import jax.numpy as jnp
from jax import lax

D = 768
HEADS = 12
HEAD_DIM = 64
FF = 3072
ROT = 16
DOCS = 8
LEN = 2048
ROWS = 16


def document_layout(key):
    row_keys = jax.random.split(jax.random.fold_in(key, 7), ROWS)
    half_len = LEN // 2

    def one_row(row_key):
        shuffled = jax.random.permutation(row_key, LEN - half_len - 1) + half_len + 1
        later = jnp.sort(shuffled[:DOCS - 2]).astype(jnp.int32)
        boundaries = jnp.concatenate([jnp.full((1,), half_len, jnp.int32), later])
        token_index = jnp.arange(LEN, dtype=jnp.int32)
        passed = boundaries[None, :] <= token_index[:, None]
        segment = jnp.sum(passed.astype(jnp.int32), 1)
        doc_start = jnp.max(jnp.where(passed, boundaries[None, :], 0), 1)
        return (segment.astype(jnp.int32), (token_index - doc_start).astype(jnp.int32))
    return jax.vmap(one_row)(row_keys)


def draw_segment_ids(key, part):
    return document_layout(key)[0]


def draw_positions(key, part):
    return document_layout(key)[1]


def levels(stream_key, shape, pieces, smallest, largest):
    level = 1.0
    for axis_at, shards_of in pieces:
        steps = jax.random.uniform(jax.random.fold_in(jax.random.fold_in(stream_key, 6), axis_at), (shards_of,), jnp.float32, smallest / len(pieces), largest / len(pieces))
        level = level * jnp.repeat(jnp.exp(steps), shape[axis_at] // shards_of).reshape((-1,) + (1,) * (len(shape) - 1 - axis_at))
    return level


def noise(stream_key, shape, width, limit, cuts=(), kind=jnp.bfloat16):
    values = width * jax.random.normal(stream_key, shape, jnp.float32)
    if cuts:
        values = values * levels(stream_key, shape, cuts, -0.22, 0.18)
    return jnp.clip(values, -limit, limit).astype(kind)


def setup_inputs(seed: int = 0) -> dict:
    key_of = jax.random.split(jax.random.key(seed), 21)
    inputs = noise(key_of[0], (ROWS, LEN, D), 1.0, 6.0, ((0, 8), (1, 4)))
    out_grad = noise(key_of[1], (ROWS, LEN, D), 1.0, 6.0, ((0, 8), (1, 4)))
    segment_ids = draw_segment_ids(jax.random.fold_in(key_of[20], 71), 0)
    positions = draw_positions(jax.random.fold_in(key_of[20], 71), 0)
    norm1_gain = jnp.clip(1.0 + 0.1 * jax.random.normal(key_of[4], (D,), jnp.float32), 0.5, 1.5).astype(jnp.bfloat16)
    norm1_bias = noise(key_of[5], (D,), 0.3, 1.75)
    norm2_gain = jnp.clip(1.0 + 0.1 * jax.random.normal(key_of[6], (D,), jnp.float32), 0.5, 1.5).astype(jnp.bfloat16)
    norm2_bias = noise(key_of[7], (D,), 0.3, 1.75)
    query_weight = noise(key_of[8], (D, D), D ** -0.5, 0.21875)
    query_bias = noise(key_of[9], (D,), 0.3, 1.75)
    key_weight = noise(key_of[10], (D, HEAD_DIM), D ** -0.5, 0.21875)
    key_bias = noise(key_of[11], (ROT,), 0.3, 1.75)
    value_weight = noise(key_of[12], (D, HEAD_DIM), D ** -0.5, 0.21875)
    value_bias = noise(key_of[13], (HEAD_DIM,), 0.3, 1.75)
    output_weight = noise(key_of[14], (D, D), (max(1, D // 128)) ** -0.5, 2.5)
    output_bias = noise(key_of[15], (D,), 0.3, 1.75)
    hidden_weight = noise(key_of[16], (D, FF), D ** -0.5, 0.21875)
    hidden_bias = noise(key_of[17], (FF,), 0.3, 1.75)
    down_weight = noise(key_of[18], (FF, D), FF ** -0.5, 0.109375)
    down_bias = noise(key_of[19], (D,), 0.3, 1.75)
    return dict(inputs=inputs, out_grad=out_grad, segment_ids=segment_ids, positions=positions, norm1_gain=norm1_gain, norm1_bias=norm1_bias, norm2_gain=norm2_gain, norm2_bias=norm2_bias, query_weight=query_weight, query_bias=query_bias, key_weight=key_weight, key_bias=key_bias, value_weight=value_weight, value_bias=value_bias, output_weight=output_weight, output_bias=output_bias, hidden_weight=hidden_weight, hidden_bias=hidden_bias, down_weight=down_weight, down_bias=down_bias)


@jax.custom_vjp
def low(v):
    return lax.optimization_barrier(v.astype(jnp.bfloat16)).astype(jnp.float32)

@jax.custom_vjp
def low_back(v):
    return v

def low_keep(v):
    return (low(v), None)

def low_pass(kept, grad):
    return (grad,)

def back_keep(v):
    return (v, None)

def back_low(kept, grad):
    return (low(grad),)
low.defvjp(low_keep, low_pass)
low_back.defvjp(back_keep, back_low)
EPSILON = 1e-05
HIGHEST_PRECISION = lax.Precision.HIGHEST

def layer_norm(token_rows, gain_vec, offset):
    row_mean = lax.optimization_barrier(jnp.mean(token_rows, -1, keepdims=True))
    centered = token_rows - row_mean
    inverse = lax.rsqrt(lax.optimization_barrier(jnp.mean(centered * centered, -1, keepdims=True)) + EPSILON)
    return centered * inverse * gain_vec + offset

def rope_tables(places):
    half_rot = ROT // 2
    frequency = 10000.0 ** (-(jnp.arange(half_rot, dtype=jnp.float32) * 2.0) / ROT)
    angles = places.astype(jnp.float32)[:, None] * frequency[None, :]
    return (jnp.cos(angles), jnp.sin(angles))

def rotate(values_in, cosine, sine_tab):
    half_rot = ROT // 2
    first_part = values_in[..., :half_rot]
    second_part = values_in[..., half_rot:ROT]
    return jnp.concatenate([first_part * cosine - second_part * sine_tab, second_part * cosine + first_part * sine_tab, values_in[..., ROT:]], -1)

def attend(queries, keys_rot, values_all, segment_row):
    block_rows = min(512, LEN)
    block_count = LEN // block_rows
    token_index = jnp.arange(LEN, dtype=jnp.int32)
    scale_factor = HEAD_DIM ** (-0.5)

    def one_block(block_args):
        query_block, segment_block, index_block = block_args
        scores = low_back(jnp.einsum('qhd,kd->qhk', query_block, keys_rot, precision=HIGHEST_PRECISION) * scale_factor)
        allowed = (segment_block[:, None] == segment_row[None, :]) & (token_index[None, :] <= index_block[:, None])
        masked = jnp.where(allowed[:, None, :], scores, -1e+30)
        top_score = lax.optimization_barrier(jnp.max(masked, -1, keepdims=True))
        exponent = jnp.exp(masked - top_score)
        probs_f = exponent / lax.optimization_barrier(jnp.sum(exponent, -1, keepdims=True))
        return jnp.einsum('qhk,kd->qhd', low(probs_f), values_all, precision=HIGHEST_PRECISION)
    blocks_out = lax.map(jax.checkpoint(one_block), (queries.reshape(block_count, block_rows, HEADS, HEAD_DIM), segment_row.reshape(block_count, block_rows), token_index.reshape(block_count, block_rows)))
    return blocks_out.reshape(LEN, HEADS * HEAD_DIM)

def block_forward(weights_now, token_row, segment_row, place_row):
    attn_gain, attn_shift, mlp_gain, mlp_shift, query_w, query_b, key_w, key_b, value_w, value_b, out_w, out_b, hidden_w, hidden_b, down_w, down_b = weights_now
    cosine, sine_tab = rope_tables(place_row)
    attn_in = low(layer_norm(token_row, attn_gain, attn_shift))
    query_pre = low_back(jnp.dot(attn_in, query_w, precision=HIGHEST_PRECISION) + query_b)
    queries = low(rotate(query_pre.reshape(LEN, HEADS, HEAD_DIM), cosine[:, None, :], sine_tab[:, None, :]))
    key_shift = jnp.concatenate([key_b, jnp.zeros((HEAD_DIM - ROT,), jnp.float32)])
    key_pre = low_back(jnp.dot(attn_in, key_w, precision=HIGHEST_PRECISION) + key_shift)
    keys_rot = low(rotate(key_pre, cosine, sine_tab))
    values_all = low_back(low(jnp.dot(attn_in, value_w, precision=HIGHEST_PRECISION) + value_b))
    heads_out = low_back(low(attend(queries, keys_rot, values_all, segment_row)))
    attn_branch = jnp.dot(heads_out, out_w, precision=HIGHEST_PRECISION) + out_b
    mlp_in = low(layer_norm(token_row, mlp_gain, mlp_shift))
    pre_act = low_back(jnp.dot(mlp_in, hidden_w, precision=HIGHEST_PRECISION) + hidden_b)
    act_low = low(jax.nn.gelu(pre_act, approximate=False))
    mlp_branch = jnp.dot(act_low, down_w, precision=HIGHEST_PRECISION) + down_b
    return token_row + attn_branch + mlp_branch

def reference(inputs, out_grad, segment_ids, positions, norm1_gain, norm1_bias, norm2_gain, norm2_bias, query_weight, query_bias, key_weight, key_bias, value_weight, value_bias, output_weight, output_bias, hidden_weight, hidden_bias, down_weight, down_bias):
    weights_all = tuple((param.astype(jnp.float32) for param in (norm1_gain, norm1_bias, norm2_gain, norm2_bias, query_weight, query_bias, key_weight, key_bias, value_weight, value_bias, output_weight, output_bias, hidden_weight, hidden_bias, down_weight, down_bias)))

    def scan_row(running, row_item):
        token_row, grad_row, segment_row, place_row = row_item
        out_row, pull_back = jax.vjp(lambda weights_now, row_in: block_forward(weights_now, row_in, segment_row, place_row), weights_all, token_row)
        grad_weights, grad_input = pull_back(grad_row)
        return (tuple((total + part for total, part in zip(running, grad_weights))), (out_row.astype(jnp.bfloat16), grad_input))
    start_sums = tuple((jnp.zeros_like(param) for param in weights_all))
    totals, (layer_rows, input_grads) = lax.scan(scan_row, start_sums, (inputs.astype(jnp.float32), out_grad.astype(jnp.float32), segment_ids, positions))
    return (layer_rows, input_grads) + tuple(totals)
```

```python
import functools, jax, jax.numpy as jnp
from jax import lax
from jax.experimental import pallas as pl
from jax.experimental.pallas import tpu as pltpu
EPS=1e-5
NT=(((1,),(1,)),((),()))
TN=(((0,),(0,)),((),()))
def dotf(a,b,dims=(((1,),(0,)),((),()))):
    return lax.dot_general(a,b,dims,preferred_element_type=jnp.float32)
def ln(xv):
    m=jnp.mean(xv,-1,keepdims=True); c=xv-m
    s=lax.rsqrt(jnp.mean(c*c,-1,keepdims=True)+EPS)
    return c*s, s
C1=0.7071067811865476; C2=0.3989422804014327
def mlp_kernel(x_ref,g_ref,w1_ref,w2_ref,b1_ref,gain_ref,bias_ref,
               br_ref,dm_ref,dw1_ref,dw2_ref,db1_ref, mi_ref,mit_ref,act_ref,gp_ref,*,rows):
    j=pl.program_id(0)
    N=x_ref.shape[0]
    @pl.when(j==0)
    def _():
        for r in range(0,N,256):
            n,_s=ln(x_ref[r:r+256,:].astype(jnp.float32))
            mi=(n*gain_ref[...]+bias_ref[...])
            mi_ref[r:r+256,:]=mi.astype(jnp.bfloat16)
            mit_ref[:,r:r+256]=mi.astype(jnp.bfloat16).T
        br_ref[...]=jnp.zeros_like(br_ref); dm_ref[...]=jnp.zeros_like(dm_ref)
    w1=w1_ref[...]; w2=w2_ref[...]; b1=b1_ref[...]
    db=jnp.zeros((1,w1.shape[1]),jnp.float32)
    for r in range(0,N,rows):
        sl=slice(r,r+rows)
        pre=dotf(mi_ref[sl,:],w1)+b1
        da=dotf(g_ref[sl,:],w2,NT)
        phi=0.5*(1.0+lax.erf(pre*C1))
        act=(pre*phi).astype(jnp.bfloat16)
        dg=phi+pre*(jnp.exp(pre*pre*-0.5)*C2)
        gp=(da*dg).astype(jnp.bfloat16)
        act_ref[sl,:]=act
        gp_ref[sl,:]=gp
        db=db+jnp.sum(gp.astype(jnp.float32),0,keepdims=True)
        br_ref[sl,:]+=dotf(act,w2)
        dm_ref[sl,:]+=dotf(gp,w1,NT)
    db1_ref[...]=db
    dw1_ref[...]=dotf(mit_ref[...],gp_ref[...]).astype(dw1_ref.dtype)
    dw2_ref[...]=dotf(act_ref[...],g_ref[...],TN).astype(dw2_ref.dtype)

def mlp(x,g,w1,w2,b1,gain,bias,bw=256,rows=256):
    N,D=x.shape; F=w1.shape[1]
    n=F//bw
    full=lambda s: pl.BlockSpec(s,lambda j:(0,0))
    return pl.pallas_call(functools.partial(mlp_kernel,rows=rows),
      grid=(n,),
      in_specs=[full((N,D)),full((N,D)),pl.BlockSpec((D,bw),lambda j:(0,j)),pl.BlockSpec((bw,D),lambda j:(j,0)),
                pl.BlockSpec((1,bw),lambda j:(0,j)),full((1,D)),full((1,D))],
      out_specs=[full((N,D)),full((N,D)),pl.BlockSpec((D,bw),lambda j:(0,j)),pl.BlockSpec((bw,D),lambda j:(j,0)),pl.BlockSpec((1,bw),lambda j:(0,j))],
      out_shape=[jax.ShapeDtypeStruct((N,D),jnp.float32)]*2+[jax.ShapeDtypeStruct((D,F),jnp.bfloat16),jax.ShapeDtypeStruct((F,D),jnp.bfloat16),jax.ShapeDtypeStruct((1,F),jnp.float32)],
      scratch_shapes=[pltpu.VMEM((N,D),jnp.bfloat16),pltpu.VMEM((D,N),jnp.bfloat16),pltpu.VMEM((N,bw),jnp.bfloat16),pltpu.VMEM((N,bw),jnp.bfloat16)],
      compiler_params=pltpu.CompilerParams(dimension_semantics=("arbitrary",),vmem_limit_bytes=56<<20),
      name="mlp")(x,g,w1,w2,b1,gain,bias)
def lane_iota(shape):
    return lax.broadcasted_iota(jnp.int32,shape,len(shape)-1)
def rope_apply(v,C,S,sign):
    l=lane_iota(v.shape)%64
    sh=jnp.where(l<8,pltpu.roll(v,120,1),jnp.where(l<16,pltpu.roll(v,8,1),0.0))
    return v*C+(sh*S if sign>0 else -(sh*S))
def pre_kernel(x_ref,g_ref,cs_ref,wq_ref,wkv_ref,wo_ref,bq_ref,bkv_ref,gain_ref,bias_ref,
               q_ref,kv_ref,do_ref,tab_ref):
    n,_=ln(x_ref[...].astype(jnp.float32))
    ai=(n*gain_ref[...]+bias_ref[...]).astype(jnp.bfloat16)
    B=ai.shape[0]
    t=cs_ref[...]
    t=jnp.concatenate([t,jnp.zeros((128-t.shape[0],B),jnp.float32)],0).T
    l=lane_iota((B,128))
    co=jnp.where(l<8,t,0.0)
    c2=co+pltpu.roll(co,8,1)
    C=c2+pltpu.roll(c2,64,1)+jnp.where(l%64>=16,1.0,0.0)
    sb=jnp.where((l>=8)&(l<16),t,0.0)
    s2=sb-pltpu.roll(sb,120,1)
    S=s2+pltpu.roll(s2,64,1)
    tab_ref[:,:128]=C
    ds=pltpu.roll(t,111,1)
    tab_ref[:,128:]=jnp.where(l==127,ds,S)
    q=dotf(ai,wq_ref[...])+bq_ref[...]
    for c in range(0,q.shape[1],128):
        q_ref[:,c:c+128]=(rope_apply(q[:,c:c+128],C,S,1)*0.125).astype(jnp.bfloat16)
    kv=dotf(ai,wkv_ref[...])+bkv_ref[...]
    kv_ref[...]=rope_apply(kv,jnp.where(l<64,C,1.0),jnp.where(l<64,S,0.0),1).astype(jnp.bfloat16)
    do_ref[...]=dotf(g_ref[...],wo_ref[...],NT).astype(jnp.bfloat16)
def pre(x,g,cs,wq,wkv,wo,bq,bkv,gain,bias,B=256):
    N,D=x.shape
    f=lambda a: pl.BlockSpec(a.shape,lambda j:(0,0))
    row=lambda w: pl.BlockSpec((B,w),lambda j:(j,0))
    return pl.pallas_call(pre_kernel,grid=(N//B,),
      in_specs=[row(D),row(D),pl.BlockSpec((cs.shape[0],B),lambda j:(0,j)),f(wq),f(wkv),f(wo),f(bq),f(bkv),f(gain),f(bias)],
      out_specs=[row(D),row(128),row(D),row(256)],
      out_shape=[jax.ShapeDtypeStruct((N,D),jnp.bfloat16),jax.ShapeDtypeStruct((N,128),jnp.bfloat16),jax.ShapeDtypeStruct((N,D),jnp.bfloat16),jax.ShapeDtypeStruct((N,256),jnp.float32)],
      compiler_params=pltpu.CompilerParams(dimension_semantics=("arbitrary",),vmem_limit_bytes=48<<20),name="pre")(x,g,cs,wq,wkv,wo,bq,bkv,gain,bias)

NEG=-1e30
def attn_kernel(p0_ref,q_ref,do_ref,kv_ref,kvp_ref,tab_ref,o_ref,dq_ref,dkv_ref,kx_ref,bias_ref,*,QB):
    r=pl.program_id(0); hp=pl.program_id(1)
    T=q_ref.shape[0]
    @pl.when(hp==0)
    def _():
        for i,ref in enumerate((kvp_ref,kv_ref)):
            kv=ref[...].astype(jnp.float32)
            l=lane_iota(kv.shape)
            ke=jnp.where(l<64,kv,0.0); vo=jnp.where(l>=64,kv,0.0)
            sl=slice(i*T,(i+1)*T)
            kx_ref[0,sl,:]=ke.astype(jnp.bfloat16)
            kx_ref[1,sl,:]=pltpu.roll(ke,64,1).astype(jnp.bfloat16)
            kx_ref[2,sl,:]=pltpu.roll(vo,64,1).astype(jnp.bfloat16)
            kx_ref[3,sl,:]=vo.astype(jnp.bfloat16)
        ds=tab_ref[:,255:256]
        kk=(lane_iota((T,2*T))-T)
        qi=lax.broadcasted_iota(jnp.int32,(T,2*T),0)
        ok=(kk.astype(jnp.float32)>=ds)&(kk<=qi)
        bias_ref[...]=jnp.where(ok,0.0,NEG)
        dkv_ref[...]=jnp.zeros_like(dkv_ref)
    def run(lo):
        qT=q_ref[...].T; dT=do_ref[...].T
        for qb in range(0,T,QB):
            hi=T+qb+QB
            rs=slice(qb,qb+QB)
            qv=q_ref[rs,:]; dv=do_ref[rs,:]
            bias=bias_ref[rs,lo:hi]
            o=None; dq=None
            for e in (0,1):
                kx=kx_ref[e,lo:hi,:]; vx=kx_ref[2+e,lo:hi,:]
                s=dotf(qv,kx,NT)+bias
                m=jnp.max(s,-1,keepdims=True)
                p=jnp.exp(s-m)
                p=p*(1.0/jnp.sum(p,-1,keepdims=True))
                pb=p.astype(jnp.bfloat16)
                dp=dotf(dv,vx,NT)
                inner=jnp.sum(p*dp,-1,keepdims=True)
                dsc=(p*(dp-inner)).astype(jnp.bfloat16)
                oh=dotf(pb,vx); dh=dotf(dsc,kx)
                o=oh if o is None else o+oh
                dq=dh if dq is None else dq+dh
                h=slice(e*64,e*64+64)
                dkv_ref[0,:64,lo:hi]+=dotf(qT[h,rs],dsc)
                dkv_ref[0,64:,lo:hi]+=dotf(dT[h,rs],pb)
            o_ref[rs,:]=o.astype(jnp.bfloat16)
            dq_ref[rs,:]=rope_apply(dq*0.125,tab_ref[rs,:128],tab_ref[rs,128:],-1).astype(jnp.bfloat16)
    has=p0_ref[r]>0
    @pl.when(has)
    def _(): run(0)
    @pl.when(jnp.logical_not(has))
    def _(): run(T)
def attn(p0,q,do,kv,kvp,tab,T=512,QB=256):
    N,D=q.shape; R=N//T
    hb=pl.BlockSpec((T,128),lambda r,h,p:(r,h)); rb=lambda w: pl.BlockSpec((T,w),lambda r,h,p:(r,0))
    return pl.pallas_call(functools.partial(attn_kernel,QB=QB),
      grid_spec=pltpu.PrefetchScalarGridSpec(num_scalar_prefetch=1,grid=(R,D//128),
        in_specs=[hb,hb,rb(128),rb(128),rb(256)],
        out_specs=[hb,hb,pl.BlockSpec((1,128,2*T),lambda r,h,p:(r,0,0))],
        scratch_shapes=[pltpu.VMEM((4,2*T,128),jnp.bfloat16),pltpu.VMEM((T,2*T),jnp.float32)]),
      out_shape=[jax.ShapeDtypeStruct((N,D),jnp.bfloat16)]*2+[jax.ShapeDtypeStruct((R,128,2*T),jnp.float32)],
      compiler_params=pltpu.CompilerParams(dimension_semantics=("arbitrary","arbitrary"),vmem_limit_bytes=56<<20),name="attn")(p0,q,do,kv,kvp,tab)
def wgrad_kernel(x_ref,g_ref,o_ref,dq_ref,gain_ref,bias_ref,dwq_ref,dwo_ref,qb_ref,ait_ref,ot_ref):
    j=pl.program_id(0); N=x_ref.shape[0]
    @pl.when(j==0)
    def _():
        for r in range(0,N,256):
            n,_s=ln(x_ref[r:r+256,:].astype(jnp.float32))
            ait_ref[:,r:r+256]=(n*gain_ref[...]+bias_ref[...]).astype(jnp.bfloat16).T
            ot_ref[:,r:r+256]=o_ref[r:r+256,:].T
    dq=dq_ref[...]
    dwq_ref[...]=dotf(ait_ref[...],dq).astype(dwq_ref.dtype)
    dwo_ref[...]=dotf(ot_ref[...],g_ref[...]).astype(dwo_ref.dtype)
    qb_ref[...]=jnp.sum(dq.astype(jnp.float32),0,keepdims=True)
def wgrad(x,g,o,dq,gain,bias,bw=256):
    N,D=x.shape
    full=lambda a: pl.BlockSpec(a.shape,lambda j:(0,0))
    col=pl.BlockSpec((N,bw),lambda j:(0,j)); oc=pl.BlockSpec((D,bw),lambda j:(0,j))
    return pl.pallas_call(wgrad_kernel,grid=(D//bw,),
      in_specs=[full(x),col,full(o),col,full(gain),full(bias)],
      out_specs=[oc,oc,pl.BlockSpec((1,bw),lambda j:(0,j))],
      out_shape=[jax.ShapeDtypeStruct((D,D),jnp.bfloat16)]*2+[jax.ShapeDtypeStruct((1,D),jnp.float32)],
      scratch_shapes=[pltpu.VMEM((D,N),jnp.bfloat16)]*2,
      compiler_params=pltpu.CompilerParams(dimension_semantics=("arbitrary",),vmem_limit_bytes=48<<20),name="wgrad")(x,g,o,dq,gain,bias)
def post_kernel(x_ref,g_ref,o_ref,dq_ref,br_ref,dm_ref,dk_ref,dr_ref,tab_ref,wq_ref,wkv_ref,wo_ref,bo_ref,bd_ref,g1_ref,b1_ref,g2_ref,
                lo_ref,ig_ref,sm_ref,dwkv_ref,kvb_ref):
    j=pl.program_id(0)
    @pl.when(j==0)
    def _():
        sm_ref[...]=jnp.zeros_like(sm_ref); dwkv_ref[...]=jnp.zeros_like(dwkv_ref); kvb_ref[...]=jnp.zeros_like(kvb_ref)
    x=x_ref[...].astype(jnp.float32); g=g_ref[...].astype(jnp.float32)
    n,s=ln(x)
    g1=g1_ref[...]; g2=g2_ref[...]
    ai=(n*g1+b1_ref[...]).astype(jnp.bfloat16)
    dkv=(dk_ref[0]+dr_ref[0].astype(jnp.float32)).T
    l=lane_iota(dkv.shape)
    dkv=rope_apply(dkv,jnp.where(l<64,tab_ref[:,:128],1.0),jnp.where(l<64,tab_ref[:,128:],0.0),-1).astype(jnp.bfloat16)
    kvb_ref[...]+=jnp.sum(dkv.astype(jnp.float32),0,keepdims=True)
    dwkv_ref[...]+=dotf(ai,dkv,TN)
    lo_ref[...]=(x+(dotf(o_ref[...],wo_ref[...])+bo_ref[...])+(br_ref[...]+bd_ref[...])).astype(jnp.bfloat16)
    c1=dotf(dq_ref[...],wq_ref[...],NT)+dotf(dkv,wkv_ref[...],NT)
    c2=dm_ref[...]
    u=c1*g1+c2*g2
    ig_ref[...]=g+s*(u-jnp.mean(u,-1,keepdims=True)-n*jnp.mean(u*n,-1,keepdims=True))
    for i,v in enumerate((c1*n,c1,c2*n,c2,g)):
        sm_ref[i:i+1,:]+=jnp.sum(v,0,keepdims=True)
def post(x,g,o,dq,br,dm,dkv,drecv,tab,wq,wkv,wo,bo,bd,g1,b1,g2,B=256,T=512):
    N,D=x.shape; nb=T//B
    f=lambda a: pl.BlockSpec(a.shape,lambda j:(0,)*a.ndim)
    row=lambda w: pl.BlockSpec((B,w),lambda j:(j,0))
    return pl.pallas_call(post_kernel,grid=(N//B,),
      in_specs=[row(D)]*6+[pl.BlockSpec((1,128,B),lambda j:(j//nb,0,nb+j%nb)),pl.BlockSpec((1,128,B),lambda j:(j//nb,0,j%nb)),row(256)]+[f(a) for a in (wq,wkv,wo,bo,bd,g1,b1,g2)],
      out_specs=[row(D),row(D),pl.BlockSpec((8,D),lambda j:(0,0)),pl.BlockSpec((D,128),lambda j:(0,0)),pl.BlockSpec((1,128),lambda j:(0,0))],
      out_shape=[jax.ShapeDtypeStruct((N,D),jnp.bfloat16),jax.ShapeDtypeStruct((N,D),jnp.float32),jax.ShapeDtypeStruct((8,D),jnp.float32),jax.ShapeDtypeStruct((D,128),jnp.float32),jax.ShapeDtypeStruct((1,128),jnp.float32)],
      compiler_params=pltpu.CompilerParams(dimension_semantics=("arbitrary",),vmem_limit_bytes=56<<20),name="post")(x,g,o,dq,br,dm,dkv,drecv,tab,wq,wkv,wo,bo,bd,g1,b1,g2)
from jax.sharding import PartitionSpec as P
ROT=16
def bits_of(n):
    return n.bit_length()-1
def pair_perm(size,bit):
    return [(i,i^(1<<bit)) for i in range(size)]
def halve(G,axis_name,bit,ax):
    n=lax.axis_size(axis_name)
    my=(lax.axis_index(axis_name)>>bit)&1
    send=lax.dynamic_index_in_dim(G,1-my,ax,keepdims=False)
    keep=lax.dynamic_index_in_dim(G,my,ax,keepdims=False)
    recv=lax.ppermute(send,axis_name,pair_perm(n,bit))
    return (keep.astype(jnp.float32)+recv.astype(jnp.float32)).astype(G.dtype)
def double(own,bit):
    n=lax.axis_size("dp")
    my=(lax.axis_index("dp")>>bit)&1
    recv=lax.ppermute(own,"dp",pair_perm(n,bit))
    buf=jnp.stack([own,own])
    return lax.dynamic_update_index_in_dim(buf,recv,1-my,0)
def reduce_stream(G,order):
    sp=lax.axis_size("sp"); nb=len(order); rows=G.shape[0]//sp; cols=G.shape[1]
    G=G.reshape((sp,)+(2,)*nb+(rows>>nb,cols))
    for b in order: G=halve(G,"dp",b,1)
    G=G.reshape((2,)*bits_of(sp)+G.shape[1:])
    for b in range(bits_of(sp)): G=halve(G,"sp",b,bits_of(sp)-1-b)
    for b in reversed(order): G=double(G,b)
    return G.reshape(rows,cols).astype(jnp.float32)
def on_device(inputs,out_grad,segment_ids,positions,norm1_gain,norm1_bias,norm2_gain,norm2_bias,query_weight,query_bias,key_weight,key_bias,value_weight,value_bias,output_weight,output_bias,hidden_weight,hidden_bias,down_weight,down_bias):
    f32=jnp.float32
    sp=lax.axis_size("sp"); dp=lax.axis_size("dp"); s=lax.axis_index("sp")
    R,T,D=inputs.shape; hd=key_weight.shape[1]; rot=key_bias.shape[0]
    N=R*T
    x=inputs.reshape(N,D); g=out_grad.reshape(N,D)
    vec=lambda v: v.astype(f32)[None,:]
    pos=lax.dynamic_slice_in_dim(positions,s*T,T,1)
    pf=pos.astype(f32).reshape(N)
    freq=10000.0**(-(jnp.arange(rot//2,dtype=f32)*2.0)/rot)
    ang=pf[None,:]*freq[:,None]
    ds=(jnp.arange(T,dtype=f32)[None,:]-pos.astype(f32)).reshape(1,N)
    cs=jnp.concatenate([jnp.cos(ang),jnp.sin(ang),ds,jnp.zeros((7,N),f32)],0)
    wkv=jnp.concatenate([key_weight,value_weight],1)
    bkv=jnp.concatenate([key_bias.astype(f32),jnp.zeros((hd-rot,),f32),value_bias.astype(f32)])[None,:]
    g1,b1,g2,b2=map(vec,(norm1_gain,norm1_bias,norm2_gain,norm2_bias))
    q,kv,do,tab=pre(x,g,cs,query_weight,wkv,output_weight,vec(query_bias),bkv,g1,b1)
    kvp=lax.ppermute(kv,"sp",[(i,i+1) for i in range(0,sp,2)])
    br,dm,dw1,dw2,db1=mlp(x,g,hidden_weight,down_weight,vec(hidden_bias),g2,b2,bw=512,rows=512)
    o,dq,dkv=attn(pos[:,0],q,do,kv,kvp,tab,T=T)
    drecv=lax.ppermute(dkv[:,:,:T].astype(jnp.bfloat16),"sp",[(i+1,i) for i in range(0,sp,2)])
    dwq,dwo,qb=wgrad(x,g,o,dq,g1,b1)
    lo,ig,sm,dwkv,kvb=post(x,g,o,dq,br,dm,dkv,drecv,tab,query_weight,wkv,output_weight,vec(output_bias),vec(down_bias),g1,b1,g2,T=T)
    nb=bits_of(dp)
    A=tuple(range(nb)); B=(0,)+tuple(range(nb-1,0,-1))
    rw1=reduce_stream(dw1,A); rw2=reduce_stream(dw2,B)
    rq=reduce_stream(dwq,A); ro=reduce_stream(dwo,B)
    rkv=reduce_stream(dwkv.astype(jnp.bfloat16),A)
    small=jnp.concatenate([sm[0],sm[1],sm[2],sm[3],sm[4],qb[0],db1[0],kvb[0]])
    small=lax.psum(small,("dp","sp"))
    def piece(a,n): return lax.dynamic_slice_in_dim(a,s*(n//sp),n//sp)
    n1g,n1b,n2g,n2b,ob,qbg=[piece(small[i*D:(i+1)*D],D) for i in range(6)]
    F=hidden_weight.shape[1]
    hb=piece(small[6*D:6*D+F],F)
    kb=piece(small[6*D+F:6*D+F+rot],rot)
    vb=piece(small[6*D+F+hd:6*D+F+2*hd],hd)
    return (lo.reshape(R,T,D),ig.reshape(R,T,D),n1g,n1b,n2g,n2b,rq,qbg,rkv[:,:hd],kb,rkv[:,hd:],vb,ro,ob,rw1,hb,rw2,ob)
def solution(mesh):
    t=P("dp","sp",None); m=P("dp",None); w=P()
    v=P("sp"); v2=P("sp",None)
    return jax.shard_map(on_device,mesh=mesh,in_specs=(t,t,m,m)+(w,)*16,
        out_specs=(t,t,v,v,v,v,v2,v,v2,v,v2,v,v2,v,v2,v,v2,v),check_vma=False)
```

```python
import functools
import jax
import jax.numpy as jnp
from jax import lax
from jax.experimental import pallas as pl
from jax.experimental.pallas import tpu as pltpu
from jax.sharding import PartitionSpec as P
EPS=1e-5
VMEM_ALL=67043328
NN=(((1,),(0,)),((),()))
NT=(((1,),(1,)),((),()))
TN=(((0,),(0,)),((),()))
BF=jnp.bfloat16
F32=jnp.float32
NEG=-1e30
C1=0.7071067811865476
C2=0.3989422804014327
def dotf(a,b,dims=NN):
    return lax.dot_general(a,b,dims,preferred_element_type=F32)
def ln(xv):
    m=jnp.mean(xv,-1,keepdims=True); c=xv-m
    s=lax.rsqrt(jnp.mean(c*c,-1,keepdims=True)+EPS)
    return c*s,s
def cost(flops,bytes_):
    return pl.CostEstimate(flops=int(flops),bytes_accessed=int(bytes_),transcendentals=0)
def params(n,mb):
    return pltpu.CompilerParams(dimension_semantics=("arbitrary",)*n,vmem_limit_bytes=VMEM_ALL if mb is None else mb<<20)
ANY=pl.BlockSpec(memory_space=pl.ANY)
hs=jax.ShapeDtypeStruct
def whole(a):
    z=(0,)*len(a.shape)
    return pl.BlockSpec(a.shape,lambda *_: z)
def lane_iota(shape):
    return lax.broadcasted_iota(jnp.int32,shape,len(shape)-1)
V_G1,V_B1,V_G2,V_B2,V_Q,V_KV,V_O,V_D,V_H=range(9)
def table_kernel(*refs):
    *vs,kb_ref,vb_ref,hb_ref,out_ref=refs
    D=out_ref.shape[1]
    for k,ref in zip((V_G1,V_B1,V_G2,V_B2,V_Q,V_O,V_D),vs):
        out_ref[k:k+1,:]=ref[...].astype(F32).reshape(1,D)
    n=kb_ref.shape[0]; h=vb_ref.shape[0]
    out_ref[V_KV:V_KV+1,:]=jnp.zeros((1,D),F32)
    out_ref[V_KV:V_KV+1,:n]=kb_ref[...].astype(F32).reshape(1,n)
    out_ref[V_KV:V_KV+1,h:2*h]=vb_ref[...].astype(F32).reshape(1,h)
    for i in range(4):
        out_ref[V_H+i:V_H+i+1,:]=hb_ref[i*D:(i+1)*D].astype(F32).reshape(1,D)
def table(*vs):
    return pl.pallas_call(table_kernel,out_shape=hs((V_H+4,vs[0].shape[0]),F32),compiler_params=params(0,None),name="table")(*vs)
def rope_apply(v,C,S,sign):
    l=lane_iota(v.shape)&63
    sh=jnp.where(l<8,pltpu.roll(v,120,1),jnp.where(l<16,pltpu.roll(v,8,1),0.0))
    return v*C+S*sh if sign>0 else v*C-S*sh
def rope_kv(v,C,S,sign):
    l=lane_iota(v.shape)
    return rope_apply(v,jnp.where(l<64,C,1.0),jnp.where(l<64,S,0.0),sign)
def pre_kernel(x_ref,g_ref,cs_ref,wq_ref,wk_ref,wv_ref,wo_ref,vec_ref,q_ref,kv_ref,do_ref,tab_ref,ai_ref):
    B=x_ref.shape[0]
    row=lambda k: vec_ref[k:k+1,:]
    n,_=ln(x_ref[...].astype(F32))
    ai=(n*row(V_G1)+row(V_B1)).astype(BF)
    ai_ref[...]=ai.T
    t=cs_ref[...]
    t=jnp.concatenate([t,jnp.zeros((128-t.shape[0],B),F32)],0).T
    l=lane_iota((B,128))
    co=jnp.where(l<8,t,0.0)
    c2=co+pltpu.roll(co,8,1)
    C=c2+pltpu.roll(c2,64,1)+jnp.where((l&63)>=16,1.0,0.0)
    sb=jnp.where((l>=8)&(l<16),t,0.0)
    s2=sb-pltpu.roll(sb,120,1)
    S=s2+pltpu.roll(s2,64,1)
    tab_ref[:,:128]=C
    tab_ref[:,128:]=jnp.where(l==127,pltpu.roll(t,111,1),S)
    q=dotf(ai,wq_ref[...])+row(V_Q)
    do=dotf(g_ref[...],wo_ref[...],NT)
    for k in range(q.shape[1]//128):
        c=slice(k*128,k*128+128)
        q_ref[k]=(rope_apply(q[:,c],C,S,1)*0.125).astype(BF)
        do_ref[k]=do[:,c].astype(BF)
    kv=jnp.concatenate([dotf(ai,wk_ref[...],NT),dotf(ai,wv_ref[...],NT)],1)+row(V_KV)[:,:128]
    kv_ref[...]=rope_kv(kv,C,S,1).astype(BF)
def pre(x,g,cs,wq,wk,wv,wo,vec,B=256):
    N,D=x.shape; NP=D//128
    row=lambda w: pl.BlockSpec((B,w),lambda j:(j,0))
    pair=pl.BlockSpec((NP,B,128),lambda j:(0,j,0)); col=lambda h: pl.BlockSpec((h,B),lambda j:(0,j))
    return pl.pallas_call(pre_kernel,grid=(N//B,),
      in_specs=[row(D),row(D),col(cs.shape[0])]+[whole(a) for a in (wq,wk,wv,wo,vec)],
      out_specs=[pair,row(128),pair,row(256),col(D)],
      out_shape=[hs((NP,N,128),BF),hs((N,128),BF),hs((NP,N,128),BF),hs((N,256),F32),hs((D,N),BF)],
      cost_estimate=cost(4e9,1e7),compiler_params=params(1,None),name="pre")(x,g,cs,wq,wk,wv,wo,vec)
def mlp_kernel(last,rows,*refs):
    if last:
        (sc,x_ref,g_ref,wa_ref,wb_ref,va_ref,vb_ref,vec_ref,r2_ref,r1_ref,dbs_ref,_a,_g,
         keep_ref,send_ref,act_hbm,gp_hbm,db_ref,w1_ref,w2_ref,b_ref,act_ref,gp_ref,sem)=refs
        mi_ref=x_ref
    else:
        (sc,x_ref,g_ref,wa_ref,wb_ref,va_ref,vb_ref,vec_ref,
         out_ref,act_hbm,gp_hbm,db_ref,mi_ref,w1_ref,w2_ref,b_ref,act_ref,gp_ref,sem)=refs
    j=pl.program_id(0); N,D=x_ref.shape; W=wa_ref.shape[1]
    h=sc[0]
    def copies(jj):
        out=[]
        for i,(scr,hbm) in enumerate(((act_ref,act_hbm),(gp_ref,gp_hbm))):
            for k in (0,1):
                off=pl.multiple_of((2*(2*jj+k)+h)*W,W)
                out.append(pltpu.make_async_copy(scr.at[:,k*W:(k+1)*W],hbm.at[:,pl.ds(off,W)],sem.at[i,k]))
        return out
    if not last:
        @pl.when(j==0)
        def _():
            def body(i,_):
                r=pl.ds(pl.multiple_of(i*256,256),256)
                n,_s=ln(x_ref[r,:].astype(F32))
                mi_ref[r,:]=(n*vec_ref[V_G2:V_G2+1,:]+vec_ref[V_B2:V_B2+1,:]).astype(BF)
                return 0
            lax.fori_loop(0,N//256,body,0)
    w1_ref[:,:W]=wa_ref[...]; w1_ref[:,W:]=wb_ref[...]
    w2_ref[:W,:]=va_ref[...]; w2_ref[W:,:]=vb_ref[...]
    lane=pl.ds(pl.multiple_of(h*W,128),W)
    b_ref[:,:W]=vec_ref[pl.ds(V_H+2*j,1),lane]; b_ref[:,W:]=vec_ref[pl.ds(V_H+2*j+1,1),lane]
    @pl.when(j>0)
    def _():
        for c in copies(j-1): c.wait()
    for r in range(0,N,rows):
        sl=slice(r,r+rows)
        pre_=dotf(mi_ref[sl,:],w1_ref[...])+b_ref[...]
        da=dotf(g_ref[sl,:],w2_ref[...],NT)
        phi=0.5*(1.0+lax.erf(pre_*C1))
        act_ref[sl,:]=(pre_*phi).astype(BF)
        gp_ref[sl,:]=(da*(phi+pre_*(jnp.exp(pre_*pre_*-0.5)*C2))).astype(BF)
    for c in copies(j): c.start()
    db=jnp.sum(gp_ref[...].astype(F32),0,keepdims=True)
    if last:
        other=pl.ds(pl.multiple_of((1-h)*W,128),W)
        for k in (0,1):
            db_ref[pl.ds(2*j+k,1),lane]=db[:,k*W:(k+1)*W]
            db_ref[pl.ds(2*j+k,1),other]=dbs_ref[j][:,k*W:(k+1)*W]
    else: db_ref[0]=db
    d1=dotf(mi_ref[...],gp_ref[...],TN).reshape(4,D//4,2*W)
    d2=dotf(act_ref[...],g_ref[...],TN).reshape(2,W,D)
    q=D//4
    if last:
        d1=(d1+r1_ref[...].astype(F32)).astype(BF)
        d2=(d2+r2_ref[...].astype(F32)).astype(BF)
        bit=sc[1]
        @pl.when(bit==0)
        def _():
            keep_ref[pl.ds(2*j,2)]=d2
            send_ref[:,pl.ds(pl.multiple_of(j*q,q),q),:]=d1
        @pl.when(bit!=0)
        def _():
            send_ref[pl.ds(2*j,2)]=d2
            keep_ref[:,pl.ds(pl.multiple_of(j*q,q),q),:]=d1
    else:
        out_ref[pl.ds(2*j,2),:W,:]=d2.astype(BF)
        out_ref[:,pl.ds(pl.multiple_of(W+j*q,q),q),:]=d1.astype(BF)
    @pl.when(j==pl.num_programs(0)-1)
    def _():
        for c in copies(j): c.wait()
def mlp_half(sc,x,g,w1,w2,vec,recv=None,dbs=None,act=None,gp=None,rows=512):
    N,D=x.shape; F=w1.shape[1]; W=F//8
    last=recv is not None
    cb=lambda sh,k,ax: pl.BlockSpec(sh,(lambda j,s:(0,2*(2*j+k)+s[0])) if ax else (lambda j,s:(2*(2*j+k)+s[0],0)))
    ins=[whole(x),whole(g),cb((D,W),0,1),cb((D,W),1,1),cb((W,D),0,0),cb((W,D),1,0),whole(vec)]
    args=[x,g,w1,w1,w2,w2,vec]
    ag=[hs((N,F),BF),hs((N,F),BF),hs((2,1,2*W),F32)]
    ags=[ANY,ANY,pl.BlockSpec((1,1,2*W),lambda j,s:(j,0,0))]
    alias={}; scr=[]
    if last:
        ins+=[pl.BlockSpec((2,W,D),lambda j,s:(j,0,0)),pl.BlockSpec((4,D//4,D),lambda j,s:(0,W//(D//4)+j,0)),whole(dbs),ANY,ANY]
        args+=[recv,recv,dbs,act,gp]
        outs=[hs((4,W,D),BF)]*2+ag[:2]+[hs((4,2*W),F32)]
        ospec=[whole(outs[0])]*2+ags[:2]+[whole(outs[-1])]
        alias={1+10:2,1+11:3}
    else:
        outs=[hs((4,2*W,D),BF)]+ag+[hs((N,D),BF)]
        ospec=[whole(outs[0])]+ags+[whole(outs[-1])]
    return pl.pallas_call(functools.partial(mlp_kernel,last,rows),
        grid_spec=pltpu.PrefetchScalarGridSpec(num_scalar_prefetch=1,grid=(2,),in_specs=ins,out_specs=ospec,
            scratch_shapes=[pltpu.VMEM((D,2*W),BF),pltpu.VMEM((2*W,D),BF),pltpu.VMEM((1,2*W),F32),
                            pltpu.VMEM((N,2*W),BF),pltpu.VMEM((N,2*W),BF),pltpu.SemaphoreType.DMA((2,2))]),
        out_shape=outs,input_output_aliases=alias,cost_estimate=cost(4*N*D*F*1.3,20e6),
        compiler_params=params(1,None),name="mlp_keep" if last else "mlp_send")(sc,*args)

def attn_kernel(row,RB,p0_ref,q_ref,do_ref,kv_ref,kvp_ref,tab_ref,o_ref,dq_ref,dk_ref,dp_out,kx_ref,bias_ref,s_ref,d_ref,p_ref,ds_ref,acc_ref,qt_ref,oa_ref):
    step=pl.program_id(0)
    T=q_ref.shape[1]; QB=T//2
    @pl.when(step==0)
    def _():
        for i,ref in enumerate((kvp_ref,kv_ref)):
            kv=ref[...].astype(F32)
            l=lane_iota(kv.shape)
            ke=jnp.where(l<64,kv,0.0); vo=jnp.where(l>=64,kv,0.0)
            sl=slice(i*T,(i+1)*T)
            kx_ref[0,sl,:]=ke.astype(BF)
            kx_ref[1,sl,:]=pltpu.roll(ke,64,1).astype(BF)
            kx_ref[2,sl,:]=pltpu.roll(vo,64,1).astype(BF)
            kx_ref[3,sl,:]=vo.astype(BF)
        for r in range(0,T,128):
            ds=tab_ref[r:r+128,255:256]
            kk=(lane_iota((128,2*T))-T)
            qi=lax.broadcasted_iota(jnp.int32,(128,2*T),0)+r
            ok=(kk.astype(F32)>=ds)&(kk<=qi)
            bias_ref[r:r+128,:]=jnp.where(ok,0.0,NEG)
        acc_ref[...]=jnp.zeros_like(acc_ref)
    def run(lo):
        units=[(qb,e) for qb in (0,1) for e in (0,1)]
        rng=lambda qb: (lo,T+(qb+1)*QB)
        def mm1(u):
            qb,e=units[u]; a,b=rng(qb); n=b-a; z=u%2; rs=slice(qb*QB,(qb+1)*QB)
            qs=q_ref[:,rs,:].reshape(2*QB,128); dv=do_ref[:,rs,:].reshape(2*QB,128)
            if e==0:
                qt_ref[0,qb]=qs.T; qt_ref[1,qb]=dv.T
            s_ref[z,:,:n]=dotf(qs,kx_ref[e,a:b,:],NT)
            d_ref[z,:,:n]=dotf(dv,kx_ref[2+e,a:b,:],NT)
        def vp(u):
            qb,e=units[u]; a,b=rng(qb); n=b-a; z=u%2
            for r in range(0,2*QB,RB):
                rr=slice(r,r+RB); br=qb*QB+r%QB
                s=s_ref[z,rr,:n]+bias_ref[br:br+RB,a:b]
                m=jnp.max(s,-1,keepdims=True)
                p=jnp.exp(s-m)
                p=p*(1.0/jnp.sum(p,-1,keepdims=True))
                p_ref[z,rr,:n]=p.astype(BF)
                t=p*d_ref[z,rr,:n]
                ds_ref[z,rr,:n]=(t-p*jnp.sum(t,-1,keepdims=True)).astype(BF)
        def mm2(u):
            qb,e=units[u]; a,b=rng(qb); n=b-a; z=u%2; rs=slice(qb*QB,(qb+1)*QB)
            pb=p_ref[z,:,:n]; dsb=ds_ref[z,:,:n]
            o=dotf(pb,kx_ref[2+e,a:b,:]); dq=dotf(dsb,kx_ref[e,a:b,:])
            h=slice(e*64,e*64+64)
            acc_ref[:64,a:b]+=dotf(qt_ref[0,qb,h,:],dsb)
            acc_ref[64:,a:b]+=dotf(qt_ref[1,qb,h,:],pb)
            if e==0:
                oa_ref[0]=o; oa_ref[1]=dq
            else:
                oo=(oa_ref[0]+o).astype(BF)
                dq=((oa_ref[1]+dq)*0.125)
                C=tab_ref[rs,:128]; S=tab_ref[rs,128:]
                for k in (0,1):
                    o_ref[rs,k*128:(k+1)*128]=oo[k*QB:(k+1)*QB]
                    dq_ref[rs,k*128:(k+1)*128]=rope_apply(dq[k*QB:(k+1)*QB],C,S,-1).astype(BF)
        mm1(0)
        mm1(1); vp(0)
        mm2(0); mm1(2); vp(1)
        mm2(1); mm1(3); vp(2)
        mm2(2); vp(3)
        mm2(3)
    def short():
        for qb in (0,1):
            a,b=T,T+(qb+1)*QB; n=b-a; rs=slice(qb*QB,(qb+1)*QB)
            both=lambda ref: ref[:,rs,:].reshape(2*QB,128)
            qt_ref[0,qb]=both(q_ref).T; qt_ref[1,qb]=both(do_ref).T
            oa_ref[...]=jnp.zeros_like(oa_ref)
            def unit(e,_):
                kx=kx_ref[e,a:b,:]; vx=kx_ref[2+e,a:b,:]
                s_ref[0,:,:n]=dotf(both(q_ref),kx,NT)
                d_ref[0,:,:n]=dotf(both(do_ref),vx,NT)
                for k in range(0,2*QB,RB):
                    r=slice(k,k+RB); br=slice(qb*QB+k%QB,qb*QB+k%QB+RB)
                    s=s_ref[0,r,:n]+bias_ref[br,a:b]
                    p=jnp.exp(s-jnp.max(s,-1,keepdims=True))
                    p=p*(1.0/jnp.sum(p,-1,keepdims=True))
                    p_ref[0,r,:n]=p.astype(BF)
                    w=p*d_ref[0,r,:n]
                    ds_ref[0,r,:n]=(w-p*jnp.sum(w,-1,keepdims=True)).astype(BF)
                pb=p_ref[0,:,:n]; dsb=ds_ref[0,:,:n]
                oa_ref[0]+=dotf(pb,vx); oa_ref[1]+=dotf(dsb,kx)
                h=pl.ds(pl.multiple_of(e*64,64),64)
                acc_ref[:64,a:b]+=dotf(qt_ref[0,qb,h,:],dsb)
                acc_ref[64:,a:b]+=dotf(qt_ref[1,qb,h,:],pb)
                return 0
            lax.fori_loop(0,2,unit,0)
            for k in (0,1):
                r=slice(k*QB,(k+1)*QB); c=slice(k*128,(k+1)*128)
                o_ref[rs,c]=oa_ref[0,r].astype(BF)
                dq_ref[rs,c]=rope_apply(oa_ref[1,r]*0.125,tab_ref[rs,:128],tab_ref[rs,128:],-1).astype(BF)
    has=p0_ref[row]>0
    @pl.when(has)
    def _(): run(0)
    @pl.when(jnp.logical_not(has))
    def _(): short()
    @pl.when(step==pl.num_programs(0)-1)
    def _():
        dp_out[...]=acc_ref[:,:T].astype(BF)
        dk_ref[...]=acc_ref[:,T:]
def attn_row(row,p0,q,do,kv,kvp,tab,prev=None,T=512,RB=32):
    NP,N,_=q.shape; QB=T//2
    bf=BF; f=F32
    hb=pl.BlockSpec((2,T,128),lambda h,p:(h,row,0)); rb=lambda w: pl.BlockSpec((T,w),lambda h,p:(row,0))
    def body(p0_ref,q_ref,do_ref,kv_ref,kvp_ref,tab_ref,*rest):
        if prev is not None: rest=rest[2:]
        attn_kernel(row,RB,p0_ref,q_ref,do_ref,kv_ref,kvp_ref,tab_ref,*rest)
    ins=[hb,hb,rb(128),rb(128),rb(256)]; args=[q,do,kv,kvp,tab]; alias={}
    if prev is not None:
        ins+=[ANY,ANY]; args+=list(prev); alias={6:0,7:1}
    c=lambda: pl.BlockSpec((128,T),lambda h,p:(0,0)); ob=pl.BlockSpec((T,256),lambda h,p:(row,h))
    return pl.pallas_call(body,
      grid_spec=pltpu.PrefetchScalarGridSpec(num_scalar_prefetch=1,grid=(NP//2,),in_specs=ins,
        out_specs=[ob,ob,c(),c()],
        scratch_shapes=[pltpu.VMEM((4,2*T,128),bf),pltpu.VMEM((T,2*T),f),pltpu.VMEM((2,2*QB,2*T),f),pltpu.VMEM((2,2*QB,2*T),f),
                        pltpu.VMEM((2,2*QB,2*T),bf),pltpu.VMEM((2,2*QB,2*T),bf),pltpu.VMEM((128,2*T),f),pltpu.VMEM((2,2,128,2*QB),bf),pltpu.VMEM((2,2*QB,128),f)]),
      out_shape=[hs((N,NP*128),bf)]*2+[hs((128,T),f),hs((128,T),bf)],
      input_output_aliases=alias,cost_estimate=cost(2.4e10,4e6),
      compiler_params=params(1,28),name=f"attn{row}")(p0,*args)
def wgrad_kernel(sc,g_ref,o_ref,dq_ref,ai_ref,keep_ref,send_ref,qb_ref,ot_ref,so_ref,sa_ref):
    N,D=o_ref.shape; hr=D//8
    for r in range(0,N,256): ot_ref[:,r:r+256]=o_ref[r:r+256,:].T
    for i,c in enumerate((1-sc[0],sc[0])):
        for s in range(4):
            src=pl.ds(pl.multiple_of(s*2*hr+c*hr,hr),hr); to=slice((4*i+s)*hr,(4*i+s+1)*hr)
            so_ref[to,:]=ot_ref[src,:]; sa_ref[to,:]=ai_ref[src,:]
    for k,(a,b) in enumerate(((so_ref,g_ref),(sa_ref,dq_ref))):
        w=dotf(a[...],b[...]).astype(BF).reshape(8,hr,D)
        send_ref[:,:,k*D:(k+1)*D]=w[:4]; keep_ref[:,:,k*D:(k+1)*D]=w[4:]
    qb_ref[...]=jnp.sum(dq_ref[...].astype(F32),0,keepdims=True)
def wgrad(sc,g,o,dq,ai):
    N,D=g.shape
    args=(g,o,dq,ai)
    part=pl.BlockSpec((4,D//8,2*D),lambda j,s:(0,0,0)); out=hs((4,D//8,2*D+128),BF)
    return pl.pallas_call(wgrad_kernel,
        grid_spec=pltpu.PrefetchScalarGridSpec(num_scalar_prefetch=1,grid=(1,),in_specs=[whole(a) for a in args],out_specs=[part,part,pl.BlockSpec((1,D),lambda j,s:(0,0))],
            scratch_shapes=[pltpu.VMEM((D,N),BF)]*3),
        out_shape=[out,out,hs((1,D),F32)],cost_estimate=cost(2.6e9,9e6),compiler_params=params(1,30),name="wgrad")(sc,*args)
def kvgrad_kernel(sc,da_ref,db_ref,ra_ref,rb_ref,tab_ref,ai_ref,_k,_s,keep_ref,send_ref,dkv_ref,kvb_ref,w_ref):
    D,N=ai_ref.shape; T=N//2; hr=D//8
    for i,(ref,rr) in enumerate(((da_ref,ra_ref),(db_ref,rb_ref))):
        sl=slice(i*T,(i+1)*T)
        dkv_ref[sl,:]=rope_kv((ref[...]+rr[...].astype(F32)).T,tab_ref[sl,:128],tab_ref[sl,128:],-1).astype(BF)
    kvb_ref[...]=jnp.sum(dkv_ref[...].astype(F32),0,keepdims=True)
    w_ref[...]=dotf(ai_ref[...],dkv_ref[...])
    for dst,c in ((send_ref,1-sc[0]),(keep_ref,sc[0])):
        for s in range(4):
            dst[s]=w_ref[pl.ds(pl.multiple_of(s*2*hr+c*hr,hr),hr),:].astype(BF)
def kvgrad(sc,d0,d1,r0,r1,tab,ai,keep,send):
    D,N=ai.shape
    args=(d0,d1,r0,r1,tab,ai)
    col=pl.BlockSpec((4,D//8,128),lambda j,s:(0,0,2*D//128))
    outs=[hs(keep.shape,BF),hs(send.shape,BF),hs((N,128),BF),hs((1,128),F32)]
    return pl.pallas_call(kvgrad_kernel,
        grid_spec=pltpu.PrefetchScalarGridSpec(num_scalar_prefetch=1,grid=(1,),in_specs=[whole(a) for a in args]+[ANY,ANY],out_specs=[col,col,whole(outs[2]),whole(outs[3])],
            scratch_shapes=[pltpu.VMEM((D,128),F32)]),
        out_shape=outs,input_output_aliases={7:0,8:1},cost_estimate=cost(2e8,4e6),compiler_params=params(1,16),name="kvgrad")(sc,*args,keep,send)
def rows_of(w,B): return pl.BlockSpec((B,w),lambda j:(j,0))
def product_kernel(dims,a_ref,w_ref,out_ref):
    @pl.when(pl.program_id(0)==0)
    def _(): out_ref[...]=dotf(a_ref[...],w_ref[...],dims)
    @pl.when(pl.program_id(0)>0)
    def _(): out_ref[...]+=dotf(a_ref[...],w_ref[...],dims)
def product(a,w,across,name):
    N,F=a.shape; D=w.shape[0] if across else w.shape[1]
    ws=pl.BlockSpec((D,D),(lambda j:(0,j)) if across else (lambda j:(j,0)))
    return pl.pallas_call(functools.partial(product_kernel,NT if across else NN),grid=(F//D,),
      in_specs=[pl.BlockSpec((N,D),lambda j:(0,j)),ws],out_specs=pl.BlockSpec((N,D),lambda j:(0,0)),out_shape=hs((N,D),F32),
      cost_estimate=cost(4.8e9,1.4e7),compiler_params=params(1,None),name=name)(a,w)
def postb_kernel(x_ref,g_ref,dq_ref,dkv_ref,c2_ref,wq_ref,wk_ref,wv_ref,vec_ref,ig_ref,sm_ref):
    j=pl.program_id(0)
    @pl.when(j==0)
    def _(): sm_ref[...]=jnp.zeros_like(sm_ref)
    g=g_ref[...].astype(F32)
    n,s=ln(x_ref[...].astype(F32))
    dkv=dkv_ref[...]
    c1=dotf(dq_ref[...],wq_ref[...],NT)+dotf(dkv[:,:64],wk_ref[...])+dotf(dkv[:,64:],wv_ref[...])
    c2=c2_ref[...]
    u=c1*vec_ref[V_G1:V_G1+1,:]+c2*vec_ref[V_G2:V_G2+1,:]
    ig_ref[...]=g+s*(u-jnp.mean(u,-1,keepdims=True)-n*jnp.mean(u*n,-1,keepdims=True))
    for i,v in enumerate((c1*n,c1,c2*n,c2,g)):
        sm_ref[i:i+1,:]+=jnp.sum(v,0,keepdims=True)
def postb(x,g,dq,dkv,c2,wq,wk,wv,vec,B=256):
    N,D=x.shape
    return pl.pallas_call(postb_kernel,grid=(N//B,),
      in_specs=[rows_of(D,B)]*3+[rows_of(128,B),rows_of(D,B)]+[whole(a) for a in (wq,wk,wv,vec)],
      out_specs=[rows_of(D,B),pl.BlockSpec((8,D),lambda j:(0,0))],
      out_shape=[hs((N,D),F32),hs((8,D),F32)],
      cost_estimate=cost(2e9,1.2e7),compiler_params=params(1,None),name="postb")(x,g,dq,dkv,c2,wq,wk,wv,vec)
def posta_kernel(x_ref,o_ref,mb_ref,wo_ref,vec_ref,lo_ref):
    lo_ref[...]=(x_ref[...].astype(F32)+(dotf(o_ref[...],wo_ref[...])+vec_ref[V_O:V_O+1,:])+(mb_ref[...]+vec_ref[V_D:V_D+1,:])).astype(BF)
def posta(x,o,mb,wo,vec,B=256):
    N,D=x.shape
    return pl.pallas_call(posta_kernel,grid=(N//B,),
      in_specs=[rows_of(D,B)]*3+[whole(a) for a in (wo,vec)],
      out_specs=rows_of(D,B),out_shape=hs((N,D),BF),
      cost_estimate=cost(2e9,9e6),compiler_params=params(1,None),name="posta")(x,o,mb,wo,vec)
def final_kernel(sc,m_ref,mr_ref,a_ref,ar_ref,s_ref,sr_ref,w1_ref,w2_ref,wo_ref,wq_ref,wk_ref,wv_ref,
                 n1g_ref,n1b_ref,n2g_ref,n2b_ref,ob_ref,qb_ref,hb_ref,kb_ref,vb_ref,kv_ref):
    W=w2_ref.shape[0]//2; D=m_ref.shape[1]; q=D//4; hr=a_ref.shape[0]; pr=hr//4; mr=m_ref.shape[0]//4
    for r0,(m,a) in enumerate(((m_ref,a_ref),(mr_ref,ar_ref))):
        h=sc[0]^r0
        for r1 in (0,1):
            for r2 in (0,1):
                i=sc[2+2*r0]^r1; j=sc[3+2*r0]^r2; k=r1*2+r2
                src=slice(k*mr,(k+1)*mr)
                @pl.when(i==0)
                def _(): w2_ref[pl.ds(pl.multiple_of(h*W+j*mr,mr),mr),:]=m[src,:].astype(F32)
                @pl.when(i!=0)
                def _():
                    for c in (0,1):
                        w1_ref[:,pl.ds(pl.multiple_of((2*j+c)*2*W+h*W,W),W)]=m[src,c*W:(c+1)*W].astype(F32)
                to=pl.ds(pl.multiple_of(h*hr+i*2*pr+j*pr,pr),pr)
                wo_ref[to,:]=a[k*pr:(k+1)*pr,:D].astype(F32)
                wq_ref[to,:]=a[k*pr:(k+1)*pr,D:2*D].astype(F32)
                kv_ref[to,:]=a[k*pr:(k+1)*pr,2*D:].astype(F32)
    keys=kv_ref[...].T
    wk_ref[...]=keys[:64]; wv_ref[...]=keys[64:]
    t=s_ref[...]+sr_ref[...]
    for s in range(4):
        @pl.when(sc[1]==s)
        def _():
            for k,ref in enumerate((n1g_ref,n1b_ref,n2g_ref,n2b_ref,ob_ref,qb_ref)):
                ref[...]=t[k:k+1,s*q:(s+1)*q].reshape(q)
            hb_ref[...]=t[6+s:7+s,:].reshape(D)
            n=kb_ref.shape[0]; kb_ref[...]=t[10:11,s*n:(s+1)*n].reshape(n)
            n=vb_ref.shape[0]; vb_ref[...]=t[10:11,64+s*n:64+(s+1)*n].reshape(n)
def final(sc,m,mr,a,ar,s,sr,F,rotd):
    D=m.shape[1]; f=F32; v=hs((D//4,),f)
    outs=[hs((D//4,F),f),hs((F//4,D),f),hs((D//4,D),f),hs((D//4,D),f),hs((64,D//4),f),hs((64,D//4),f)]+[v]*6+[hs((D,),f),hs((rotd//4,),f),hs((16,),f)]
    return pl.pallas_call(final_kernel,
        grid_spec=pltpu.PrefetchScalarGridSpec(num_scalar_prefetch=1,grid=(1,),in_specs=[whole(u) for u in (m,mr,a,ar,s,sr)],out_specs=[whole(u) for u in outs],
            scratch_shapes=[pltpu.VMEM((D//4,128),F32)]),
        out_shape=outs,cost_estimate=cost(1e6,9e6),compiler_params=params(1,24),name="final")(sc,m,mr,a,ar,s,sr)
def bits_of(n):
    return n.bit_length()-1
def after(xs,*deps):
    out=lax.optimization_barrier(tuple(xs)+tuple(deps))
    return out[:len(xs)]
def dp_stages():
    dp=lax.axis_size("dp"); nb=bits_of(dp); i=lax.axis_index("dp")
    core=i&1
    st=[(core,[(k,k^1) for k in range(dp)],core)]
    for t in range(1,nb):
        up,down=t,nb-t
        a,b=(i>>up)&1,(i>>down)&1
        st.append((jnp.where(core==0,a,b),[(k,k^((1<<up) if k%2==0 else (1<<down))) for k in range(dp)],jnp.where(core==0,b,a)))
    return st
def pick(G,bit,ax): return lax.dynamic_index_in_dim(G,bit,ax,keepdims=False)
def add(a,b): return (a.astype(F32)+b.astype(F32)).astype(a.dtype)
class Stream:
    def __init__(self,stages,at,send,keep):
        self.st=stages; self.at=at; self.send=send; self.keep=keep; self.left=len(stages)
    def go(self):
        n=len(self.st)
        if self.at<n: axis,pairs="dp",self.st[self.at][1]
        else: axis="sp"; pairs=[(k,k^(1<<(self.at-n))) for k in range(lax.axis_size("sp"))]
        self.recv=lax.ppermute(self.send,axis,pairs)
        return self.recv
    def land(self):
        k,r=self.keep,self.recv; self.at+=1
        n=len(self.st); s=lax.axis_index("sp")
        if self.at<n:
            split=lambda t: t.reshape(t.shape[0],2,t.shape[1]//2,t.shape[2]); bit=self.st[self.at][0]; ax=1
        elif self.at==n:
            split=lambda t: t.reshape(2,2,t.shape[1],t.shape[2]); bit=s&1; ax=1
        elif self.at==n+1:
            split=lambda t: t; bit=s>>1; ax=0
        else:
            self.own=add(k,r); self.left=n
            return
        k,r=split(k),split(r)
        self.send=add(pick(k,1-bit,ax),pick(r,1-bit,ax))
        self.keep=add(pick(k,bit,ax),pick(r,bit,ax))
    def gather_go(self):
        self.left-=1
        self.recv=lax.ppermute(self.own,"dp",self.st[self.left][1])
        return self.recv
    def gather_land(self):
        self.own=jnp.concatenate([self.own,self.recv],0)
    def settle(self,x,of):
        n=len(self.st)
        if n<=3: return x
        g=x.reshape((4,)+(2,)*(n-3)+(-1,x.shape[1]))
        for t in range(3,n): g=jnp.where(self.st[t][of]==0,g,jnp.flip(g,t-2))
        return g.reshape(x.shape)
def on_device(inputs,out_grad,segment_ids,positions,norm1_gain,norm1_bias,norm2_gain,norm2_bias,query_weight,query_bias,key_weight,key_bias,value_weight,value_bias,output_weight,output_bias,hidden_weight,hidden_bias,down_weight,down_bias):
    sp=lax.axis_size("sp"); s=lax.axis_index("sp")
    R,T,D=inputs.shape; hd=key_weight.shape[1]; rotd=key_bias.shape[0]
    F=hidden_weight.shape[1]
    N=R*T
    x=inputs.reshape(N,D); g=out_grad.reshape(N,D)
    vec=table(norm1_gain,norm1_bias,norm2_gain,norm2_bias,query_bias,output_bias,down_bias,key_bias,value_bias,hidden_bias)
    pos=lax.dynamic_slice_in_dim(positions,s*T,T,1)
    p0=pos[:,0]
    st=dp_stages(); core=st[0][0]; bit1=st[1][0]
    back=[(i+1,i) for i in range(0,sp,2)]
    Ms,act,gp,dbs,mi=mlp_half(jnp.stack([1-core,bit1]),x,g,hidden_weight,down_weight,vec)
    Mr=lax.ppermute(Ms,"dp",st[0][1])
    pf=pos.astype(F32).reshape(N)
    freq=10000.0**(-(jnp.arange(rotd//2,dtype=F32)*2.0)/rotd)
    ang=pf[None,:]*freq[:,None]
    ds=(jnp.arange(T,dtype=F32)[None,:]-pos.astype(F32)).reshape(1,N)
    cs=jnp.concatenate([jnp.cos(ang),jnp.sin(ang),ds,jnp.zeros((7,N),F32)],0)
    xq,=after([x],dbs)
    q,kv,do,tab,ai=pre(xq,g,cs,query_weight,key_weight.T,value_weight.T,output_weight,vec)
    kv,Mr=after([kv,Mr],q)
    kvp=lax.ppermute(kv,"sp",[(i,i+1) for i in range(0,sp,2)])
    mi,=after([mi],q)
    keep,send,act,gp,dbk=mlp_half(jnp.stack([core,bit1]),mi,g,hidden_weight,down_weight,vec,recv=Mr,dbs=dbs,act=act,gp=gp)
    M=Stream(st,1,send,keep)
    M.send,kvp=after([M.send,kvp],dbk)
    M.go()
    q,=after([q],dbk)
    o,dq,d0,k0=attn_row(0,p0,q,do,kv,kvp,tab,T=T)
    M.recv,k0=after([M.recv,k0],dq)
    M.land()
    r0=lax.ppermute(k0,"sp",back); M.go()
    o,dq=after([o,dq],M.send,k0)
    o,dq,d1,k1=attn_row(1,p0,q,do,kv,kvp,tab,prev=(o,dq),T=T)
    k1,M.recv,r0=after([k1,M.recv,r0],dq)
    r1=lax.ppermute(k1,"sp",back)
    while True:
        M.land()
        if M.at>=len(st): break
        M.go()
    o_,=after([o],M.send,k1)
    sc=core.reshape(1)
    wkeep,wsend,qb=wgrad(sc,g,o_,dq,ai)
    M.send,wkeep,wsend,r1=after([M.send,wkeep,wsend,r1],qb)
    M.send,=after([M.send],r1)
    M.go()
    r1,=after([r1],M.send)
    wkeep,wsend,dkv,kvb=kvgrad(sc,d0,d1,r0,r1,tab,ai,wkeep,wsend)
    A=Stream(st,0,wsend,wkeep)
    small=None
    todo=[("dp",p) for _,p,_o in st]+[("sp",[(i,i^(1<<k)) for i in range(sp)]) for k in range(bits_of(sp))]
    c2=mb=ig=lo=None
    fill=["c2","ig","mb","lo"]
    moved=[A.send]
    first=True
    while A.at<len(st)+2 or A.left>1 or len(todo)>1 or M.left>1:
        rs=A.at<len(st)+2
        ag=not rs and A.left>1
        if rs: A.go()
        elif ag: A.gather_go()
        mg=mz=False
        if not first:
            if M.at<len(st)+2: M.go(); mz=True
            elif M.left>1: M.gather_go(); mg=True
        sr=None
        if small is not None and len(todo)>1: axis,pairs=todo.pop(0); sr=lax.ppermute(small,axis,pairs)
        deps=[]
        if fill:
            k=fill.pop(0)
            if k=="c2": gk,=after([gp],*moved); c2=product(gk,hidden_weight,True,"back"); deps=[c2]
            if k=="ig": xk,=after([x],*moved); ig,sm=postb(xk,g,dq,dkv,c2,query_weight,key_weight.T,value_weight.T,vec); deps=[ig]
            if k=="mb": ak,=after([act],*moved); mb=product(ak,down_weight,False,"down"); deps=[mb]
            if k=="lo": xk,=after([x],*moved); lo=posta(xk,o,mb,output_weight,vec); deps=[lo]
        got=([A.recv] if rs or ag else [])+([M.recv] if mz or mg or first else [])+([sr] if sr is not None else [])
        got=list(after(got,*deps))
        if rs or ag: A.recv=got.pop(0)
        if mz or mg or first: M.recv=got.pop(0)
        if sr is not None: small=small+got.pop(0)
        if rs: A.land()
        elif ag: A.gather_land()
        if mz or first: M.land()
        elif mg: M.gather_land()
        first=False
        if small is None and ig is not None:
            small=jnp.concatenate([sm[:5],qb,dbk,jnp.pad(kvb,((0,5),(0,D-kvb.shape[1])))],0)
        moved=[A.send if A.at<len(st)+2 else A.own]+([M.send] if M.at<len(st)+2 else [M.own])+([small] if small is not None else [])
    Mr=lax.ppermute(M.own,"dp",st[0][1])
    Ar=lax.ppermute(A.own,"dp",st[0][1])
    axis,pairs=todo.pop(0)
    sr=lax.ppermute(small,axis,pairs)
    zero=jnp.zeros_like(core)
    where=jnp.stack([core,s]+[st[t][of] if len(st)>t else zero for of in (0,2) for t in (1,2)])
    rw1,rw2,ro,rq,rk,rv,n1g,n1b,n2g,n2b,ob,qbg,hb,kb,vb=final(where,M.settle(M.own,0),M.settle(Mr,2),A.settle(A.own,0),A.settle(Ar,2),small,sr,F,rotd)
    return (lo.reshape(R,T,D),ig.reshape(R,T,D),n1g,n1b,n2g,n2b,rq,qbg,rk.T,kb,rv.T,vb,ro,ob,rw1,hb,rw2,ob)
def solution(mesh):
    t=P("dp","sp",None); m=P("dp",None); w=P()
    v=P("sp"); v2=P("sp",None)
    return jax.shard_map(on_device,mesh=mesh,in_specs=(t,t,m,m)+(w,)*16,
        out_specs=(t,t,v,v,v,v,v2,v,v2,v,v2,v,v2,v,v2,v,v2,v),check_vma=False)
```

```python
import functools
import jax
import jax.numpy as jnp
from jax import lax
from jax.experimental import pallas as pl
from jax.experimental.pallas import tpu as pltpu
from jax.sharding import PartitionSpec as P
EPS=1e-5
VMEM_ALL=67043328
NN=(((1,),(0,)),((),()))
NT=(((1,),(1,)),((),()))
TN=(((0,),(0,)),((),()))
BF=jnp.bfloat16
F32=jnp.float32
NEG=-1e30
C1=0.7071067811865476
C2=0.3989422804014327
def dotf(a,b,dims=NN):
    return lax.dot_general(a,b,dims,preferred_element_type=F32)
def ln(xv):
    m=jnp.mean(xv,-1,keepdims=True); c=xv-m
    s=lax.rsqrt(jnp.mean(c*c,-1,keepdims=True)+EPS)
    return c*s,s
def cost(flops,bytes_):
    return pl.CostEstimate(flops=int(flops),bytes_accessed=int(bytes_),transcendentals=0)
def params(n,mb):
    return pltpu.CompilerParams(dimension_semantics=("arbitrary",)*n,vmem_limit_bytes=VMEM_ALL if mb is None else mb<<20)
ANY=pl.BlockSpec(memory_space=pl.ANY)
hs=jax.ShapeDtypeStruct
def whole(a):
    z=(0,)*len(a.shape)
    return pl.BlockSpec(a.shape,lambda *_: z)
def lane_iota(shape):
    return lax.broadcasted_iota(jnp.int32,shape,len(shape)-1)
V_G1,V_B1,V_G2,V_B2,V_Q,V_KV,V_O,V_D,V_H=range(9)
def table_kernel(*refs):
    *vs,kb_ref,vb_ref,hb_ref,out_ref=refs
    D=out_ref.shape[1]
    for k,ref in zip((V_G1,V_B1,V_G2,V_B2,V_Q,V_O,V_D),vs):
        out_ref[k:k+1,:]=ref[...].astype(F32).reshape(1,D)
    n=kb_ref.shape[0]; h=vb_ref.shape[0]
    out_ref[V_KV:V_KV+1,:]=jnp.zeros((1,D),F32)
    out_ref[V_KV:V_KV+1,:n]=kb_ref[...].astype(F32).reshape(1,n)
    out_ref[V_KV:V_KV+1,h:2*h]=vb_ref[...].astype(F32).reshape(1,h)
    for i in range(4):
        out_ref[V_H+i:V_H+i+1,:]=hb_ref[i*D:(i+1)*D].astype(F32).reshape(1,D)
def table(*vs):
    return pl.pallas_call(table_kernel,out_shape=hs((V_H+4,vs[0].shape[0]),F32),compiler_params=params(0,None),name="table")(*vs)
def rope_apply(v,C,S,sign):
    l=lane_iota(v.shape)&63
    sh=jnp.where(l<8,pltpu.roll(v,120,1),jnp.where(l<16,pltpu.roll(v,8,1),0.0))
    return v*C+S*sh if sign>0 else v*C-S*sh
def rope_kv(v,C,S,sign):
    l=lane_iota(v.shape)
    return rope_apply(v,jnp.where(l<64,C,1.0),jnp.where(l<64,S,0.0),sign)
def pre_kernel(x_ref,g_ref,cs_ref,wq_ref,wk_ref,wv_ref,wo_ref,vec_ref,q_ref,kv_ref,do_ref,tab_ref,ai_ref):
    B=x_ref.shape[0]
    row=lambda k: vec_ref[k:k+1,:]
    n,_=ln(x_ref[...].astype(F32))
    ai=(n*row(V_G1)+row(V_B1)).astype(BF)
    ai_ref[...]=ai.T
    t=cs_ref[...]
    t=jnp.concatenate([t,jnp.zeros((128-t.shape[0],B),F32)],0).T
    l=lane_iota((B,128))
    co=jnp.where(l<8,t,0.0)
    c2=co+pltpu.roll(co,8,1)
    C=c2+pltpu.roll(c2,64,1)+jnp.where((l&63)>=16,1.0,0.0)
    sb=jnp.where((l>=8)&(l<16),t,0.0)
    s2=sb-pltpu.roll(sb,120,1)
    S=s2+pltpu.roll(s2,64,1)
    tab_ref[:,:128]=C
    tab_ref[:,128:]=jnp.where(l==127,pltpu.roll(t,111,1),S)
    q=dotf(ai,wq_ref[...])+row(V_Q)
    do=dotf(g_ref[...],wo_ref[...],NT)
    for k in range(q.shape[1]//128):
        c=slice(k*128,k*128+128)
        q_ref[k]=(rope_apply(q[:,c],C,S,1)*0.125).astype(BF)
        do_ref[k]=do[:,c].astype(BF)
    kv=jnp.concatenate([dotf(ai,wk_ref[...],NT),dotf(ai,wv_ref[...],NT)],1)+row(V_KV)[:,:128]
    kv_ref[...]=rope_kv(kv,C,S,1).astype(BF)
def pre(x,g,cs,wq,wk,wv,wo,vec,B=256):
    N,D=x.shape; NP=D//128
    row=lambda w: pl.BlockSpec((B,w),lambda j:(j,0))
    pair=pl.BlockSpec((NP,B,128),lambda j:(0,j,0)); col=lambda h: pl.BlockSpec((h,B),lambda j:(0,j))
    return pl.pallas_call(pre_kernel,grid=(N//B,),
      in_specs=[row(D),row(D),col(cs.shape[0])]+[whole(a) for a in (wq,wk,wv,wo,vec)],
      out_specs=[pair,row(128),pair,row(256),col(D)],
      out_shape=[hs((NP,N,128),BF),hs((N,128),BF),hs((NP,N,128),BF),hs((N,256),F32),hs((D,N),BF)],
      cost_estimate=cost(4e9,1e7),compiler_params=params(1,None),name="pre")(x,g,cs,wq,wk,wv,wo,vec)
def mlp_kernel(last,rows,*refs):
    if last:
        (sc,x_ref,g_ref,wa_ref,wb_ref,va_ref,vb_ref,vec_ref,r2_ref,r1_ref,dbs_ref,_a,_g,
         keep_ref,send_ref,act_hbm,gp_hbm,db_ref,w1_ref,w2_ref,b_ref,act_ref,gp_ref,sem)=refs
        mi_ref=x_ref
    else:
        (sc,x_ref,g_ref,wa_ref,wb_ref,va_ref,vb_ref,vec_ref,
         out_ref,act_hbm,gp_hbm,db_ref,mi_ref,w1_ref,w2_ref,b_ref,act_ref,gp_ref,sem)=refs
    j=pl.program_id(0); N,D=x_ref.shape; W=wa_ref.shape[1]
    h=sc[0]
    def copies(jj):
        out=[]
        for i,(scr,hbm) in enumerate(((act_ref,act_hbm),(gp_ref,gp_hbm))):
            for k in (0,1):
                off=pl.multiple_of((2*(2*jj+k)+h)*W,W)
                out.append(pltpu.make_async_copy(scr.at[:,k*W:(k+1)*W],hbm.at[:,pl.ds(off,W)],sem.at[i,k]))
        return out
    if not last:
        @pl.when(j==0)
        def _():
            def body(i,_):
                r=pl.ds(pl.multiple_of(i*256,256),256)
                n,_s=ln(x_ref[r,:].astype(F32))
                mi_ref[r,:]=(n*vec_ref[V_G2:V_G2+1,:]+vec_ref[V_B2:V_B2+1,:]).astype(BF)
                return 0
            lax.fori_loop(0,N//256,body,0)
    w1_ref[:,:W]=wa_ref[...]; w1_ref[:,W:]=wb_ref[...]
    w2_ref[:W,:]=va_ref[...]; w2_ref[W:,:]=vb_ref[...]
    lane=pl.ds(pl.multiple_of(h*W,128),W)
    b_ref[:,:W]=vec_ref[pl.ds(V_H+2*j,1),lane]; b_ref[:,W:]=vec_ref[pl.ds(V_H+2*j+1,1),lane]
    @pl.when(j>0)
    def _():
        for c in copies(j-1): c.wait()
    for r in range(0,N,rows):
        sl=slice(r,r+rows)
        pre_=dotf(mi_ref[sl,:],w1_ref[...])+b_ref[...]
        da=dotf(g_ref[sl,:],w2_ref[...],NT)
        phi=0.5*(1.0+lax.erf(pre_*C1))
        act_ref[sl,:]=(pre_*phi).astype(BF)
        gp_ref[sl,:]=(da*(phi+pre_*(jnp.exp(pre_*pre_*-0.5)*C2))).astype(BF)
    for c in copies(j): c.start()
    db=jnp.sum(gp_ref[...].astype(F32),0,keepdims=True)
    if last:
        other=pl.ds(pl.multiple_of((1-h)*W,128),W)
        for k in (0,1):
            db_ref[pl.ds(2*j+k,1),lane]=db[:,k*W:(k+1)*W]
            db_ref[pl.ds(2*j+k,1),other]=dbs_ref[j][:,k*W:(k+1)*W]
    else: db_ref[0]=db
    q=D//4
    to=pl.ds(pl.multiple_of(j*q,q),q)
    if last: bit=sc[1]
    def part(i,_):
        c=pl.ds(pl.multiple_of(i*256,256),256)
        d2=dotf(act_ref[...],g_ref[:,c],TN).reshape(2,W,256)
        d1=dotf(mi_ref[...],gp_ref[:,c],TN).reshape(4,q,256)
        if last:
            d2=(d2+r2_ref[:,:,c].astype(F32)).astype(BF)
            d1=(d1+r1_ref[:,:,c].astype(F32)).astype(BF)
            @pl.when(bit==0)
            def _():
                keep_ref[pl.ds(2*j,2),:,c]=d2; send_ref[:,to,c]=d1
            @pl.when(bit!=0)
            def _():
                send_ref[pl.ds(2*j,2),:,c]=d2; keep_ref[:,to,c]=d1
        else:
            out_ref[pl.ds(2*j,2),:W,c]=d2.astype(BF)
            out_ref[:,pl.ds(pl.multiple_of(W+j*q,q),q),c]=d1.astype(BF)
        return 0
    lax.fori_loop(0,2*W//256,part,0)
    @pl.when(j==pl.num_programs(0)-1)
    def _():
        for c in copies(j): c.wait()
def mlp_half(sc,x,g,w1,w2,vec,recv=None,dbs=None,act=None,gp=None,rows=256):
    N,D=x.shape; F=w1.shape[1]; W=F//8
    last=recv is not None
    cb=lambda sh,k,ax: pl.BlockSpec(sh,(lambda j,s:(0,2*(2*j+k)+s[0])) if ax else (lambda j,s:(2*(2*j+k)+s[0],0)))
    ins=[whole(x),whole(g),cb((D,W),0,1),cb((D,W),1,1),cb((W,D),0,0),cb((W,D),1,0),whole(vec)]
    args=[x,g,w1,w1,w2,w2,vec]
    ag=[hs((N,F),BF),hs((N,F),BF),hs((2,1,2*W),F32)]
    ags=[ANY,ANY,pl.BlockSpec((1,1,2*W),lambda j,s:(j,0,0))]
    alias={}; scr=[]
    if last:
        ins+=[pl.BlockSpec((2,W,D),lambda j,s:(j,0,0)),pl.BlockSpec((4,D//4,D),lambda j,s:(0,W//(D//4)+j,0)),whole(dbs),ANY,ANY]
        args+=[recv,recv,dbs,act,gp]
        outs=[hs((4,W,D),BF)]*2+ag[:2]+[hs((4,2*W),F32)]
        ospec=[whole(outs[0])]*2+ags[:2]+[whole(outs[-1])]
        alias={1+10:2,1+11:3}
    else:
        outs=[hs((4,2*W,D),BF)]+ag+[hs((N,D),BF)]
        ospec=[whole(outs[0])]+ags+[whole(outs[-1])]
    return pl.pallas_call(functools.partial(mlp_kernel,last,rows),
        grid_spec=pltpu.PrefetchScalarGridSpec(num_scalar_prefetch=1,grid=(2,),in_specs=ins,out_specs=ospec,
            scratch_shapes=[pltpu.VMEM((D,2*W),BF),pltpu.VMEM((2*W,D),BF),pltpu.VMEM((1,2*W),F32),
                            pltpu.VMEM((N,2*W),BF),pltpu.VMEM((N,2*W),BF),pltpu.SemaphoreType.DMA((2,2))]),
        out_shape=outs,input_output_aliases=alias,cost_estimate=cost(4*N*D*F*1.3,20e6),
        compiler_params=params(1,None),name="mlp_keep" if last else "mlp_send")(sc,*args)

def attn_kernel(RB,q_ref,do_ref,kv_ref,kvp_ref,tab_ref,o_ref,dq_ref,dk_ref,dp_out,kx_ref,bias_ref,s_ref,d_ref,p_ref,ds_ref,acc_ref,qt_ref,oa_ref):
    step=pl.program_id(0)
    T=q_ref.shape[1]; QB=T//2
    @pl.when(step==0)
    def _():
        for i,ref in enumerate((kvp_ref,kv_ref)):
            kv=ref[...].astype(F32)
            l=lane_iota(kv.shape)
            ke=jnp.where(l<64,kv,0.0); vo=jnp.where(l>=64,kv,0.0)
            sl=slice(i*T,(i+1)*T)
            kx_ref[0,sl,:]=ke.astype(BF)
            kx_ref[1,sl,:]=pltpu.roll(ke,64,1).astype(BF)
            kx_ref[2,sl,:]=pltpu.roll(vo,64,1).astype(BF)
            kx_ref[3,sl,:]=vo.astype(BF)
        def mask(i,_):
            r=pl.ds(pl.multiple_of(i*64,64),64)
            kk=lane_iota((64,2*T))-T
            qi=lax.broadcasted_iota(jnp.int32,(64,2*T),0)+i*64
            ok=(kk.astype(F32)>=tab_ref[r,255:256])&(kk<=qi)
            bias_ref[r,:]=jnp.where(ok,0.0,NEG)
            return 0
        lax.fori_loop(0,T//64,mask,0)
        acc_ref[...]=jnp.zeros_like(acc_ref)
    def run(lo):
        units=[(qb,e) for qb in (0,1) for e in (0,1)]
        rng=lambda qb: (lo,T+(qb+1)*QB)
        def mm1(u):
            qb,e=units[u]; a,b=rng(qb); n=b-a; z=u%2; rs=slice(qb*QB,(qb+1)*QB)
            qs=q_ref[:,rs,:].reshape(2*QB,128); dv=do_ref[:,rs,:].reshape(2*QB,128)
            if e==0:
                qt_ref[0,qb]=qs.T; qt_ref[1,qb]=dv.T
            s_ref[z,:,:n]=dotf(qs,kx_ref[e,a:b,:],NT)
            d_ref[z,:,:n]=dotf(dv,kx_ref[2+e,a:b,:],NT)
        def vp(u):
            qb,e=units[u]; a,b=rng(qb); n=b-a; z=u%2
            for r in range(0,2*QB,RB):
                rr=slice(r,r+RB); br=qb*QB+r%QB
                s=s_ref[z,rr,:n]+bias_ref[br:br+RB,a:b]
                m=jnp.max(s,-1,keepdims=True)
                p=jnp.exp(s-m)
                p=p*(1.0/jnp.sum(p,-1,keepdims=True))
                p_ref[z,rr,:n]=p.astype(BF)
                t=p*d_ref[z,rr,:n]
                ds_ref[z,rr,:n]=(t-p*jnp.sum(t,-1,keepdims=True)).astype(BF)
        def mm2(u):
            qb,e=units[u]; a,b=rng(qb); n=b-a; z=u%2; rs=slice(qb*QB,(qb+1)*QB)
            pb=p_ref[z,:,:n]; dsb=ds_ref[z,:,:n]
            o=dotf(pb,kx_ref[2+e,a:b,:]); dq=dotf(dsb,kx_ref[e,a:b,:])
            h=slice(e*64,e*64+64)
            acc_ref[:64,a:b]+=dotf(qt_ref[0,qb,h,:],dsb)
            acc_ref[64:,a:b]+=dotf(qt_ref[1,qb,h,:],pb)
            if e==0:
                oa_ref[0]=o; oa_ref[1]=dq
            else:
                oo=(oa_ref[0]+o).astype(BF)
                dq=((oa_ref[1]+dq)*0.125)
                C=tab_ref[rs,:128]; S=tab_ref[rs,128:]
                for k in (0,1):
                    o_ref[rs,k*128:(k+1)*128]=oo[k*QB:(k+1)*QB]
                    dq_ref[rs,k*128:(k+1)*128]=rope_apply(dq[k*QB:(k+1)*QB],C,S,-1).astype(BF)
        mm1(0)
        mm1(1); vp(0)
        mm2(0); mm1(2); vp(1)
        mm2(1); mm1(3); vp(2)
        mm2(2); vp(3)
        mm2(3)
    run(0)
    @pl.when(step==pl.num_programs(0)-1)
    def _():
        dp_out[...]=acc_ref[:,:T].astype(BF)
        dk_ref[...]=acc_ref[:,T:]
def attn_row(row,q,do,kv,kvp,tab,prev=None,T=512,RB=32):
    NP,N,_=q.shape; QB=T//2
    bf=BF; f=F32
    hb=pl.BlockSpec((2,T,128),lambda h:(h,row,0)); rb=lambda w: pl.BlockSpec((T,w),lambda h:(row,0))
    def body(q_ref,do_ref,kv_ref,kvp_ref,tab_ref,*rest):
        if prev is not None: rest=rest[2:]
        attn_kernel(RB,q_ref,do_ref,kv_ref,kvp_ref,tab_ref,*rest)
    ins=[hb,hb,rb(128),rb(128),rb(256)]; args=[q,do,kv,kvp,tab]; alias={}
    if prev is not None:
        ins+=[ANY,ANY]; args+=list(prev); alias={5:0,6:1}
    c=lambda: pl.BlockSpec((128,T),lambda h:(0,0)); ob=pl.BlockSpec((T,256),lambda h:(row,h))
    return pl.pallas_call(body,
      grid=(NP//2,),in_specs=ins,out_specs=[ob,ob,c(),c()],
        scratch_shapes=[pltpu.VMEM((4,2*T,128),bf),pltpu.VMEM((T,2*T),f),pltpu.VMEM((2,2*QB,2*T),f),pltpu.VMEM((2,2*QB,2*T),f),
                        pltpu.VMEM((2,2*QB,2*T),bf),pltpu.VMEM((2,2*QB,2*T),bf),pltpu.VMEM((128,2*T),f),pltpu.VMEM((2,2,128,2*QB),bf),pltpu.VMEM((2,2*QB,128),f)],
      out_shape=[hs((N,NP*128),bf)]*2+[hs((128,T),f),hs((128,T),bf)],
      input_output_aliases=alias,cost_estimate=cost(2.4e10,4e6),
      compiler_params=params(1,28),name=f"attn{row}")(*args)
def wgrad_kernel(sc,g_ref,o_ref,dq_ref,ai_ref,keep_ref,send_ref,qb_ref,ot_ref,so_ref,sa_ref):
    N,D=o_ref.shape; hr=D//8
    def turn(i,_):
        r=pl.ds(pl.multiple_of(i*256,256),256); ot_ref[:,r]=o_ref[r,:].T
        return 0
    lax.fori_loop(0,N//256,turn,0)
    for i,c in enumerate((1-sc[0],sc[0])):
        def move(s,_):
            src=pl.ds(pl.multiple_of(s*2*hr+c*hr,hr),hr); to=pl.ds(pl.multiple_of((4*i+s)*hr,hr),hr)
            so_ref[to,:]=ot_ref[src,:]; sa_ref[to,:]=ai_ref[src,:]
            return 0
        lax.fori_loop(0,4,move,0)
    def part(i,_):
        c=pl.ds(pl.multiple_of(i*256,256),256)
        for k,(a,b) in enumerate(((so_ref,g_ref),(sa_ref,dq_ref))):
            w=dotf(a[...],b[:,c]).astype(BF).reshape(8,hr,256); to=pl.ds(pl.multiple_of(k*D+i*256,256),256)
            send_ref[:,:,to]=w[:4]; keep_ref[:,:,to]=w[4:]
        return 0
    lax.fori_loop(0,D//256,part,0)
    qb_ref[...]=jnp.sum(dq_ref[...].astype(F32),0,keepdims=True)
def wgrad(sc,g,o,dq,ai):
    N,D=g.shape
    args=(g,o,dq,ai)
    part=pl.BlockSpec((4,D//8,2*D),lambda j,s:(0,0,0)); out=hs((4,D//8,2*D+128),BF)
    return pl.pallas_call(wgrad_kernel,
        grid_spec=pltpu.PrefetchScalarGridSpec(num_scalar_prefetch=1,grid=(1,),in_specs=[whole(a) for a in args],out_specs=[part,part,pl.BlockSpec((1,D),lambda j,s:(0,0))],
            scratch_shapes=[pltpu.VMEM((D,N),BF)]*3),
        out_shape=[out,out,hs((1,D),F32)],cost_estimate=cost(2.6e9,9e6),compiler_params=params(1,30),name="wgrad")(sc,*args)
def kvgrad_kernel(sc,da_ref,db_ref,ra_ref,rb_ref,tab_ref,ai_ref,_k,_s,keep_ref,send_ref,dkv_ref,kvb_ref,w_ref):
    D,N=ai_ref.shape; T=N//2; hr=D//8
    for i,(ref,rr) in enumerate(((da_ref,ra_ref),(db_ref,rb_ref))):
        sl=slice(i*T,(i+1)*T)
        dkv_ref[sl,:]=rope_kv((ref[...]+rr[...].astype(F32)).T,tab_ref[sl,:128],tab_ref[sl,128:],-1).astype(BF)
    kvb_ref[...]=jnp.sum(dkv_ref[...].astype(F32),0,keepdims=True)
    w_ref[...]=dotf(ai_ref[...],dkv_ref[...])
    for dst,c in ((send_ref,1-sc[0]),(keep_ref,sc[0])):
        for s in range(4):
            dst[s]=w_ref[pl.ds(pl.multiple_of(s*2*hr+c*hr,hr),hr),:].astype(BF)
def kvgrad(sc,d0,d1,r0,r1,tab,ai,keep,send):
    D,N=ai.shape
    args=(d0,d1,r0,r1,tab,ai)
    col=pl.BlockSpec((4,D//8,128),lambda j,s:(0,0,2*D//128))
    outs=[hs(keep.shape,BF),hs(send.shape,BF),hs((N,128),BF),hs((1,128),F32)]
    return pl.pallas_call(kvgrad_kernel,
        grid_spec=pltpu.PrefetchScalarGridSpec(num_scalar_prefetch=1,grid=(1,),in_specs=[whole(a) for a in args]+[ANY,ANY],out_specs=[col,col,whole(outs[2]),whole(outs[3])],
            scratch_shapes=[pltpu.VMEM((D,128),F32)]),
        out_shape=outs,input_output_aliases={7:0,8:1},cost_estimate=cost(2e8,4e6),compiler_params=params(1,16),name="kvgrad")(sc,*args,keep,send)
def rows_of(w,B): return pl.BlockSpec((B,w),lambda j:(j,0))
def product_kernel(dims,a_ref,w_ref,out_ref):
    @pl.when(pl.program_id(0)==0)
    def _(): out_ref[...]=jnp.zeros_like(out_ref)
    out_ref[...]+=dotf(a_ref[...],w_ref[...],dims)
def product(a,w,across,name):
    N,F=a.shape; D=w.shape[0] if across else w.shape[1]
    ws=pl.BlockSpec((D,D),(lambda j:(0,j)) if across else (lambda j:(j,0)))
    return pl.pallas_call(functools.partial(product_kernel,NT if across else NN),grid=(F//D,),
      in_specs=[pl.BlockSpec((N,D),lambda j:(0,j)),ws],out_specs=pl.BlockSpec((N,D),lambda j:(0,0)),out_shape=hs((N,D),F32),
      cost_estimate=cost(4.8e9,1.4e7),compiler_params=params(1,None),name=name)(a,w)
def postb_kernel(x_ref,g_ref,dq_ref,dkv_ref,c2_ref,wq_ref,wk_ref,wv_ref,vec_ref,ig_ref,sm_ref):
    j=pl.program_id(0)
    @pl.when(j==0)
    def _(): sm_ref[...]=jnp.zeros_like(sm_ref)
    g=g_ref[...].astype(F32)
    n,s=ln(x_ref[...].astype(F32))
    dkv=dkv_ref[...]
    c1=dotf(dq_ref[...],wq_ref[...],NT)+dotf(dkv[:,:64],wk_ref[...])+dotf(dkv[:,64:],wv_ref[...])
    c2=c2_ref[...]
    u=c1*vec_ref[V_G1:V_G1+1,:]+c2*vec_ref[V_G2:V_G2+1,:]
    ig_ref[...]=g+s*(u-jnp.mean(u,-1,keepdims=True)-n*jnp.mean(u*n,-1,keepdims=True))
    for i,v in enumerate((c1*n,c1,c2*n,c2,g)):
        sm_ref[i:i+1,:]+=jnp.sum(v,0,keepdims=True)
def postb(x,g,dq,dkv,c2,wq,wk,wv,vec,B=256):
    N,D=x.shape
    return pl.pallas_call(postb_kernel,grid=(N//B,),
      in_specs=[rows_of(D,B)]*3+[rows_of(128,B),rows_of(D,B)]+[whole(a) for a in (wq,wk,wv,vec)],
      out_specs=[rows_of(D,B),pl.BlockSpec((8,D),lambda j:(0,0))],
      out_shape=[hs((N,D),F32),hs((8,D),F32)],
      cost_estimate=cost(2e9,1.2e7),compiler_params=params(1,None),name="postb")(x,g,dq,dkv,c2,wq,wk,wv,vec)
def posta_kernel(x_ref,o_ref,mb_ref,wo_ref,vec_ref,lo_ref):
    lo_ref[...]=(x_ref[...].astype(F32)+(dotf(o_ref[...],wo_ref[...])+vec_ref[V_O:V_O+1,:])+(mb_ref[...]+vec_ref[V_D:V_D+1,:])).astype(BF)
def posta(x,o,mb,wo,vec,B=256):
    N,D=x.shape
    return pl.pallas_call(posta_kernel,grid=(N//B,),
      in_specs=[rows_of(D,B)]*3+[whole(a) for a in (wo,vec)],
      out_specs=rows_of(D,B),out_shape=hs((N,D),BF),
      cost_estimate=cost(2e9,9e6),compiler_params=params(1,None),name="posta")(x,o,mb,wo,vec)
def final_kernel(sc,m_ref,mr_ref,a_ref,ar_ref,s_ref,sr_ref,w1_ref,w2_ref,wo_ref,wq_ref,wk_ref,wv_ref,
                 n1g_ref,n1b_ref,n2g_ref,n2b_ref,ob_ref,qb_ref,hb_ref,kb_ref,vb_ref,kv_ref):
    W=w2_ref.shape[0]//2; D=m_ref.shape[1]; q=D//4; hr=a_ref.shape[0]; pr=hr//4; mr=m_ref.shape[0]//4
    for r0,(m,a) in enumerate(((m_ref,a_ref),(mr_ref,ar_ref))):
        h=sc[0]^r0
        def piece(k,_):
            i=sc[2+2*r0]^(k>>1); j=sc[3+2*r0]^(k&1)
            src=pl.ds(pl.multiple_of(k*mr,mr),mr)
            @pl.when(i==0)
            def _(): w2_ref[pl.ds(pl.multiple_of(h*W+j*mr,mr),mr),:]=m[src,:].astype(F32)
            @pl.when(i!=0)
            def _():
                for c in (0,1):
                    w1_ref[:,pl.ds(pl.multiple_of((2*j+c)*2*W+h*W,W),W)]=m[src,c*W:(c+1)*W].astype(F32)
            return 0
        lax.fori_loop(0,4,piece,0)
        for k in range(4):
            i=sc[2+2*r0]^(k>>1); j=sc[3+2*r0]^(k&1)
            to=pl.ds(pl.multiple_of(h*hr+i*2*pr+j*pr,pr),pr)
            wo_ref[to,:]=a[k*pr:(k+1)*pr,:D].astype(F32)
            wq_ref[to,:]=a[k*pr:(k+1)*pr,D:2*D].astype(F32)
            kv_ref[to,:]=a[k*pr:(k+1)*pr,2*D:].astype(F32)
    keys=kv_ref[...].T
    wk_ref[...]=keys[:64]; wv_ref[...]=keys[64:]
    t=s_ref[...]+sr_ref[...]
    for s in range(4):
        @pl.when(sc[1]==s)
        def _():
            for k,ref in enumerate((n1g_ref,n1b_ref,n2g_ref,n2b_ref,ob_ref,qb_ref)):
                ref[...]=t[k:k+1,s*q:(s+1)*q].reshape(q)
            hb_ref[...]=t[6+s:7+s,:].reshape(D)
            n=kb_ref.shape[0]; kb_ref[...]=t[10:11,s*n:(s+1)*n].reshape(n)
            n=vb_ref.shape[0]; vb_ref[...]=t[10:11,64+s*n:64+(s+1)*n].reshape(n)
def final(sc,m,mr,a,ar,s,sr,F,rotd):
    D=m.shape[1]; f=F32; v=hs((D//4,),f)
    outs=[hs((D//4,F),f),hs((F//4,D),f),hs((D//4,D),f),hs((D//4,D),f),hs((64,D//4),f),hs((64,D//4),f)]+[v]*6+[hs((D,),f),hs((rotd//4,),f),hs((16,),f)]
    return pl.pallas_call(final_kernel,
        grid_spec=pltpu.PrefetchScalarGridSpec(num_scalar_prefetch=1,grid=(1,),in_specs=[whole(u) for u in (m,mr,a,ar,s,sr)],out_specs=[whole(u) for u in outs],
            scratch_shapes=[pltpu.VMEM((D//4,128),F32)]),
        out_shape=outs,cost_estimate=cost(1e6,9e6),compiler_params=params(1,24),name="final")(sc,m,mr,a,ar,s,sr)
def bits_of(n):
    return n.bit_length()-1
def after(xs,*deps):
    out=lax.optimization_barrier(tuple(xs)+tuple(deps))
    return out[:len(xs)]
def dp_stages():
    dp=lax.axis_size("dp"); nb=bits_of(dp); i=lax.axis_index("dp")
    core=i&1
    st=[(core,[(k,k^1) for k in range(dp)],core)]
    for t in range(1,nb):
        up,down=t,nb-t
        a,b=(i>>up)&1,(i>>down)&1
        st.append((jnp.where(core==0,a,b),[(k,k^((1<<up) if k%2==0 else (1<<down))) for k in range(dp)],jnp.where(core==0,b,a)))
    return st
def pick(G,bit,ax): return lax.dynamic_index_in_dim(G,bit,ax,keepdims=False)
def add(a,b): return (a.astype(F32)+b.astype(F32)).astype(a.dtype)
class Stream:
    def __init__(self,stages,at,send,keep):
        self.st=stages; self.at=at; self.send=send; self.keep=keep; self.left=len(stages)
    def go(self):
        n=len(self.st)
        if self.at<n: axis,pairs="dp",self.st[self.at][1]
        else: axis="sp"; pairs=[(k,k^(1<<(self.at-n))) for k in range(lax.axis_size("sp"))]
        self.recv=lax.ppermute(self.send,axis,pairs)
        return self.recv
    def land(self):
        k,r=self.keep,self.recv; self.at+=1
        n=len(self.st); s=lax.axis_index("sp")
        if self.at<n:
            split=lambda t: t.reshape(t.shape[0],2,t.shape[1]//2,t.shape[2]); bit=self.st[self.at][0]; ax=1
        elif self.at==n:
            split=lambda t: t.reshape(2,2,t.shape[1],t.shape[2]); bit=s&1; ax=1
        elif self.at==n+1:
            split=lambda t: t; bit=s>>1; ax=0
        else:
            self.own=add(k,r); self.left=n
            return
        k,r=split(k),split(r)
        self.send=add(pick(k,1-bit,ax),pick(r,1-bit,ax))
        self.keep=add(pick(k,bit,ax),pick(r,bit,ax))
    def gather_go(self):
        self.left-=1
        self.recv=lax.ppermute(self.own,"dp",self.st[self.left][1])
        return self.recv
    def gather_land(self):
        self.own=jnp.concatenate([self.own,self.recv],0)
    def settle(self,x,of):
        n=len(self.st)
        if n<=3: return x
        g=x.reshape((4,)+(2,)*(n-3)+(-1,x.shape[1]))
        for t in range(3,n): g=jnp.where(self.st[t][of]==0,g,jnp.flip(g,t-2))
        return g.reshape(x.shape)
def on_device(inputs,out_grad,segment_ids,positions,norm1_gain,norm1_bias,norm2_gain,norm2_bias,query_weight,query_bias,key_weight,key_bias,value_weight,value_bias,output_weight,output_bias,hidden_weight,hidden_bias,down_weight,down_bias):
    sp=lax.axis_size("sp"); s=lax.axis_index("sp")
    R,T,D=inputs.shape; hd=key_weight.shape[1]; rotd=key_bias.shape[0]
    F=hidden_weight.shape[1]
    N=R*T
    x=inputs.reshape(N,D); g=out_grad.reshape(N,D)
    vec=table(norm1_gain,norm1_bias,norm2_gain,norm2_bias,query_bias,output_bias,down_bias,key_bias,value_bias,hidden_bias)
    pos=lax.dynamic_slice_in_dim(positions,s*T,T,1)
    st=dp_stages(); core=st[0][0]; bit1=st[1][0]
    back=[(i+1,i) for i in range(0,sp,2)]
    Ms,act,gp,dbs,mi=mlp_half(jnp.stack([1-core,bit1]),x,g,hidden_weight,down_weight,vec)
    Mr=lax.ppermute(Ms,"dp",st[0][1])
    pf=pos.astype(F32).reshape(N)
    freq=10000.0**(-(jnp.arange(rotd//2,dtype=F32)*2.0)/rotd)
    ang=pf[None,:]*freq[:,None]
    ds=(jnp.arange(T,dtype=F32)[None,:]-pos.astype(F32)).reshape(1,N)
    cs=jnp.concatenate([jnp.cos(ang),jnp.sin(ang),ds,jnp.zeros((7,N),F32)],0)
    xq,=after([x],dbs)
    q,kv,do,tab,ai=pre(xq,g,cs,query_weight,key_weight.T,value_weight.T,output_weight,vec)
    kv,Mr=after([kv,Mr],q)
    kvp=lax.ppermute(kv,"sp",[(i,i+1) for i in range(0,sp,2)])
    mi,=after([mi],q)
    keep,send,act,gp,dbk=mlp_half(jnp.stack([core,bit1]),mi,g,hidden_weight,down_weight,vec,recv=Mr,dbs=dbs,act=act,gp=gp)
    M=Stream(st,1,send,keep)
    M.send,kvp=after([M.send,kvp],dbk)
    M.go()
    q,=after([q],dbk)
    o,dq,d0,k0=attn_row(0,q,do,kv,kvp,tab,T=T)
    M.recv,k0=after([M.recv,k0],dq)
    M.land()
    r0=lax.ppermute(k0,"sp",back); M.go()
    o,dq=after([o,dq],M.send,k0)
    o,dq,d1,k1=attn_row(1,q,do,kv,kvp,tab,prev=(o,dq),T=T)
    k1,M.recv,r0=after([k1,M.recv,r0],dq)
    r1=lax.ppermute(k1,"sp",back)
    while True:
        M.land()
        if M.at>=len(st): break
        M.go()
    o_,=after([o],M.send,k1)
    sc=core.reshape(1)
    wkeep,wsend,qb=wgrad(sc,g,o_,dq,ai)
    M.send,wkeep,wsend,r1=after([M.send,wkeep,wsend,r1],qb)
    M.send,=after([M.send],r1)
    M.go()
    r1,=after([r1],M.send)
    wkeep,wsend,dkv,kvb=kvgrad(sc,d0,d1,r0,r1,tab,ai,wkeep,wsend)
    A=Stream(st,0,wsend,wkeep)
    small=None
    todo=[("dp",p) for _,p,_o in st]+[("sp",[(i,i^(1<<k)) for i in range(sp)]) for k in range(bits_of(sp))]
    c2=mb=ig=lo=sm=None
    fill=["c2","ig","mb","lo"]
    held=1
    busy=True
    while True:
        rs=A.at<len(st)+2
        ag=not rs and A.left>1
        if not (rs or ag or busy or M.left>1 or len(todo)>1): break
        if rs: A.go(); moved=[A.send]
        elif ag: A.gather_go(); moved=[A.own]
        else: moved=[]
        if not busy:
            if M.at<len(st)+2: M.go(); busy=True; held=1; moved.append(M.send)
            elif M.left>1: moved.append(M.own); M.gather_go(); busy=True; held=0 if M.left>1 else 1
        sr=None
        if small is not None and len(todo)>1: axis,pairs=todo.pop(0); sr=lax.ppermute(small,axis,pairs); moved.append(small)
        deps=[]
        if fill:
            k=fill.pop(0)
            if k=="c2": gk,=after([gp],*moved); c2=product(gk,hidden_weight,True,"back"); deps=[c2]
            if k=="ig": xk,=after([x],*moved); ig,sm=postb(xk,g,dq,dkv,c2,query_weight,key_weight.T,value_weight.T,vec); deps=[ig]
            if k=="mb": ak,=after([act],*moved); mb=product(ak,down_weight,False,"down"); deps=[mb]
            if k=="lo": xk,=after([x],*moved); lo=posta(xk,o,mb,output_weight,vec); deps=[lo]
        lands=busy and held==0
        got=([A.recv] if rs or ag else [])+([M.recv] if lands else [])+([sr] if sr is not None else [])
        got=list(after(got,*deps))
        if rs or ag: A.recv=got.pop(0)
        if lands: M.recv=got.pop(0)
        if sr is not None: small=small+got.pop(0)
        if rs: A.land()
        elif ag: A.gather_land()
        if lands:
            busy=False
            if M.at<len(st)+2: M.land()
            else: M.gather_land()
        held-=1
        if small is None and ig is not None:
            small=jnp.concatenate([sm[:5],qb,dbk,jnp.pad(kvb,((0,5),(0,D-kvb.shape[1])))],0)
    Mr=lax.ppermute(M.own,"dp",st[0][1])
    Ar=lax.ppermute(A.own,"dp",st[0][1])
    axis,pairs=todo.pop(0)
    sr=lax.ppermute(small,axis,pairs)
    zero=jnp.zeros_like(core)
    where=jnp.stack([core,s]+[st[t][of] if len(st)>t else zero for of in (0,2) for t in (1,2)])
    rw1,rw2,ro,rq,rk,rv,n1g,n1b,n2g,n2b,ob,qbg,hb,kb,vb=final(where,M.settle(M.own,0),M.settle(Mr,2),A.settle(A.own,0),A.settle(Ar,2),small,sr,F,rotd)
    return (lo.reshape(R,T,D),ig.reshape(R,T,D),n1g,n1b,n2g,n2b,rq,qbg,rk.T,kb,rv.T,vb,ro,ob,rw1,hb,rw2,ob)
def solution(mesh):
    t=P("dp","sp",None); m=P("dp",None); w=P()
    v=P("sp"); v2=P("sp",None)
    return jax.shard_map(on_device,mesh=mesh,in_specs=(t,t,m,m)+(w,)*16,
        out_specs=(t,t,v,v,v,v,v2,v,v2,v,v2,v,v2,v,v2,v,v2,v),check_vma=False)
```

```python
import functools
import jax
import jax.numpy as jnp
from jax import lax
from jax.experimental import pallas as pl
from jax.experimental.pallas import tpu as pltpu
from jax.sharding import PartitionSpec as P
EPS=1e-5
VMEM_ALL=67043328
NN=(((1,),(0,)),((),()))
NT=(((1,),(1,)),((),()))
TN=(((0,),(0,)),((),()))
BF=jnp.bfloat16
F32=jnp.float32
NEG=-1e30
C1=0.7071067811865476
C2=0.3989422804014327
def dotf(a,b,dims=NN):
    return lax.dot_general(a,b,dims,preferred_element_type=F32)
def ln(xv):
    m=jnp.mean(xv,-1,keepdims=True); c=xv-m
    s=lax.rsqrt(jnp.mean(c*c,-1,keepdims=True)+EPS)
    return c*s,s
def cost(flops,bytes_):
    return pl.CostEstimate(flops=int(flops),bytes_accessed=int(bytes_),transcendentals=0)
def params(n,mb):
    return pltpu.CompilerParams(dimension_semantics=("arbitrary",)*n,vmem_limit_bytes=VMEM_ALL if mb is None else mb<<20)
ANY=pl.BlockSpec(memory_space=pl.ANY)
hs=jax.ShapeDtypeStruct
def stay(v):
    return pltpu.with_memory_space_constraint(v,pltpu.HBM)
def whole(a):
    z=(0,)*len(a.shape)
    return pl.BlockSpec(a.shape,lambda *_: z)
def lane_iota(shape):
    return lax.broadcasted_iota(jnp.int32,shape,len(shape)-1)
V_G1,V_B1,V_G2,V_B2,V_Q,V_KV,V_O,V_D,V_H=range(9)
def table_kernel(*refs):
    *vs,kb_ref,vb_ref,hb_ref,out_ref=refs
    D=out_ref.shape[1]
    for k,ref in zip((V_G1,V_B1,V_G2,V_B2,V_Q,V_O,V_D),vs):
        out_ref[k:k+1,:]=ref[...].astype(F32).reshape(1,D)
    n=kb_ref.shape[0]; h=vb_ref.shape[0]
    out_ref[V_KV:V_KV+1,:]=jnp.zeros((1,D),F32)
    out_ref[V_KV:V_KV+1,:n]=kb_ref[...].astype(F32).reshape(1,n)
    out_ref[V_KV:V_KV+1,h:2*h]=vb_ref[...].astype(F32).reshape(1,h)
    for i in range(4):
        out_ref[V_H+i:V_H+i+1,:]=hb_ref[i*D:(i+1)*D].astype(F32).reshape(1,D)
def table(*vs):
    return pl.pallas_call(table_kernel,out_shape=hs((V_H+4,vs[0].shape[0]),F32),compiler_params=params(0,None),name="table")(*vs)
def rope_apply(v,C,S,sign):
    l=lane_iota(v.shape)&63
    sh=jnp.where(l<8,pltpu.roll(v,120,1),jnp.where(l<16,pltpu.roll(v,8,1),0.0))
    return v*C+S*sh if sign>0 else v*C-S*sh
def rope_kv(v,C,S,sign):
    l=lane_iota(v.shape)
    return rope_apply(v,jnp.where(l<64,C,1.0),jnp.where(l<64,S,0.0),sign)
def pre_kernel(x_ref,g_ref,cs_ref,wq_ref,wk_ref,wv_ref,wo_ref,vec_ref,q_ref,kv_ref,do_ref,tab_ref,ai_ref):
    B=x_ref.shape[0]
    row=lambda k: vec_ref[k:k+1,:]
    n,_=ln(x_ref[...].astype(F32))
    ai=(n*row(V_G1)+row(V_B1)).astype(BF)
    ai_ref[...]=ai.T
    t=cs_ref[...]
    t=jnp.concatenate([t,jnp.zeros((128-t.shape[0],B),F32)],0).T
    l=lane_iota((B,128))
    co=jnp.where(l<8,t,0.0)
    c2=co+pltpu.roll(co,8,1)
    C=c2+pltpu.roll(c2,64,1)+jnp.where((l&63)>=16,1.0,0.0)
    sb=jnp.where((l>=8)&(l<16),t,0.0)
    s2=sb-pltpu.roll(sb,120,1)
    S=s2+pltpu.roll(s2,64,1)
    tab_ref[:,:128]=C
    tab_ref[:,128:]=jnp.where(l==127,pltpu.roll(t,111,1),S)
    q=dotf(ai,wq_ref[...])+row(V_Q)
    do=dotf(g_ref[...],wo_ref[...],NT)
    for k in range(q.shape[1]//128):
        c=slice(k*128,k*128+128)
        q_ref[k]=(rope_apply(q[:,c],C,S,1)*0.125).astype(BF)
        do_ref[k]=do[:,c].astype(BF)
    kv=jnp.concatenate([dotf(ai,wk_ref[...],NT),dotf(ai,wv_ref[...],NT)],1)+row(V_KV)[:,:128]
    kv_ref[...]=rope_kv(kv,C,S,1).astype(BF)
def pre(x,g,cs,wq,wk,wv,wo,vec,B=256):
    N,D=x.shape; NP=D//128
    row=lambda w: pl.BlockSpec((B,w),lambda j:(j,0))
    pair=pl.BlockSpec((NP,B,128),lambda j:(0,j,0)); col=lambda h: pl.BlockSpec((h,B),lambda j:(0,j))
    return pl.pallas_call(pre_kernel,grid=(N//B,),
      in_specs=[row(D),row(D),col(cs.shape[0])]+[whole(a) for a in (wq,wk,wv,wo,vec)],
      out_specs=[pair,row(128),pair,row(256),col(D)],
      out_shape=[hs((NP,N,128),BF),hs((N,128),BF),hs((NP,N,128),BF),hs((N,256),F32),hs((D,N),BF)],
      cost_estimate=cost(4e9,1e7),compiler_params=params(1,None),name="pre")(x,g,cs,wq,wk,wv,wo,vec)
def mlp_kernel(last,rows,*refs):
    if last:
        (sc,x_ref,g_ref,wa_ref,wb_ref,va_ref,vb_ref,vec_ref,r2_ref,r1_ref,dbs_ref,_a,_g,
         keep_ref,send_ref,act_hbm,gp_hbm,db_ref,w1_ref,w2_ref,b_ref,act_ref,gp_ref,sem)=refs
        mi_ref=x_ref
    else:
        (sc,x_ref,g_ref,wa_ref,wb_ref,va_ref,vb_ref,vec_ref,
         out_ref,act_hbm,gp_hbm,db_ref,mi_ref,w1_ref,w2_ref,b_ref,act_ref,gp_ref,sem)=refs
    j=pl.program_id(0); N,D=x_ref.shape; W=wa_ref.shape[1]
    h=sc[0]
    def copies(jj):
        out=[]
        for i,(scr,hbm) in enumerate(((act_ref,act_hbm),(gp_ref,gp_hbm))):
            for k in (0,1):
                off=pl.multiple_of((2*(2*jj+k)+h)*W,W)
                out.append(pltpu.make_async_copy(scr.at[:,k*W:(k+1)*W],hbm.at[:,pl.ds(off,W)],sem.at[i,k]))
        return out
    if not last:
        @pl.when(j==0)
        def _():
            def body(i,_):
                r=pl.ds(pl.multiple_of(i*256,256),256)
                n,_s=ln(x_ref[r,:].astype(F32))
                mi_ref[r,:]=(n*vec_ref[V_G2:V_G2+1,:]+vec_ref[V_B2:V_B2+1,:]).astype(BF)
                return 0
            lax.fori_loop(0,N//256,body,0)
    w1_ref[:,:W]=wa_ref[...]; w1_ref[:,W:]=wb_ref[...]
    w2_ref[:W,:]=va_ref[...]; w2_ref[W:,:]=vb_ref[...]
    lane=pl.ds(pl.multiple_of(h*W,128),W)
    b_ref[:,:W]=vec_ref[pl.ds(V_H+2*j,1),lane]; b_ref[:,W:]=vec_ref[pl.ds(V_H+2*j+1,1),lane]
    @pl.when(j>0)
    def _():
        for c in copies(j-1): c.wait()
    for r in range(0,N,rows):
        sl=slice(r,r+rows)
        pre_=dotf(mi_ref[sl,:],w1_ref[...])+b_ref[...]
        da=dotf(g_ref[sl,:],w2_ref[...],NT)
        phi=0.5*(1.0+lax.erf(pre_*C1))
        act_ref[sl,:]=(pre_*phi).astype(BF)
        gp_ref[sl,:]=(da*(phi+pre_*(jnp.exp(pre_*pre_*-0.5)*C2))).astype(BF)
    for c in copies(j): c.start()
    db=jnp.sum(gp_ref[...].astype(F32),0,keepdims=True)
    if last:
        other=pl.ds(pl.multiple_of((1-h)*W,128),W)
        for k in (0,1):
            db_ref[pl.ds(2*j+k,1),lane]=db[:,k*W:(k+1)*W]
            db_ref[pl.ds(2*j+k,1),other]=dbs_ref[j][:,k*W:(k+1)*W]
    else: db_ref[0]=db
    q=D//4
    to=pl.ds(pl.multiple_of(j*q,q),q)
    if last: bit=sc[1]
    def part(i,_):
        c=pl.ds(pl.multiple_of(i*256,256),256)
        d2=dotf(act_ref[...],g_ref[:,c],TN).reshape(2,W,256)
        d1=dotf(mi_ref[...],gp_ref[:,c],TN).reshape(4,q,256)
        if last:
            d2=(d2+r2_ref[:,:,c].astype(F32)).astype(BF)
            d1=(d1+r1_ref[:,:,c].astype(F32)).astype(BF)
            @pl.when(bit==0)
            def _():
                keep_ref[pl.ds(2*j,2),:,c]=d2; send_ref[:,to,c]=d1
            @pl.when(bit!=0)
            def _():
                send_ref[pl.ds(2*j,2),:,c]=d2; keep_ref[:,to,c]=d1
        else:
            out_ref[pl.ds(2*j,2),:W,c]=d2.astype(BF)
            out_ref[:,pl.ds(pl.multiple_of(W+j*q,q),q),c]=d1.astype(BF)
        return 0
    lax.fori_loop(0,2*W//256,part,0)
    @pl.when(j==pl.num_programs(0)-1)
    def _():
        for c in copies(j): c.wait()
def mlp_half(sc,x,g,w1,w2,vec,recv=None,dbs=None,act=None,gp=None,rows=256):
    N,D=x.shape; F=w1.shape[1]; W=F//8
    last=recv is not None
    cb=lambda sh,k,ax: pl.BlockSpec(sh,(lambda j,s:(0,2*(2*j+k)+s[0])) if ax else (lambda j,s:(2*(2*j+k)+s[0],0)))
    ins=[whole(x),whole(g),cb((D,W),0,1),cb((D,W),1,1),cb((W,D),0,0),cb((W,D),1,0),whole(vec)]
    args=[x,g,w1,w1,w2,w2,vec]
    ag=[hs((N,F),BF),hs((N,F),BF),hs((2,1,2*W),F32)]
    ags=[ANY,ANY,pl.BlockSpec((1,1,2*W),lambda j,s:(j,0,0))]
    alias={}; scr=[]
    if last:
        ins+=[pl.BlockSpec((2,W,D),lambda j,s:(j,0,0)),pl.BlockSpec((4,D//4,D),lambda j,s:(0,W//(D//4)+j,0)),whole(dbs),ANY,ANY]
        args+=[recv,recv,dbs,act,gp]
        outs=[hs((4,W,D),BF)]*2+ag[:2]+[hs((4,2*W),F32)]
        ospec=[whole(outs[0])]*2+ags[:2]+[whole(outs[-1])]
        alias={1+10:2,1+11:3}
    else:
        outs=[hs((4,2*W,D),BF)]+ag+[hs((N,D),BF)]
        ospec=[whole(outs[0])]+ags+[whole(outs[-1])]
    return pl.pallas_call(functools.partial(mlp_kernel,last,rows),
        grid_spec=pltpu.PrefetchScalarGridSpec(num_scalar_prefetch=1,grid=(2,),in_specs=ins,out_specs=ospec,
            scratch_shapes=[pltpu.VMEM((D,2*W),BF),pltpu.VMEM((2*W,D),BF),pltpu.VMEM((1,2*W),F32),
                            pltpu.VMEM((N,2*W),BF),pltpu.VMEM((N,2*W),BF),pltpu.SemaphoreType.DMA((2,2))]),
        out_shape=outs,input_output_aliases=alias,cost_estimate=cost(4*N*D*F*1.3,20e6),
        compiler_params=params(1,None),name="mlp_keep" if last else "mlp_send")(sc,*args)

def attn_kernel(base,per,RB,acc_in,q_ref,do_ref,kv_ref,kvp_ref,tab_ref,o_ref,dq_ref,own_ref,prev_ref,rest_ref,kx_ref,bias_ref,s_ref,d_ref,p_ref,ds_ref,acc_ref,qt_ref,oa_ref):
    first=pl.program_id(0)==0
    step=lax.rem(pl.program_id(0)+base,per)
    T=q_ref.shape[1]; QB=T//2
    @pl.when(first|(step==0))
    def _():
        for i,ref in enumerate((kvp_ref,kv_ref)):
            kv=ref[...].astype(F32)
            l=lane_iota(kv.shape)
            ke=jnp.where(l<64,kv,0.0); vo=jnp.where(l>=64,kv,0.0)
            sl=slice(i*T,(i+1)*T)
            kx_ref[0,sl,:]=ke.astype(BF)
            kx_ref[1,sl,:]=pltpu.roll(ke,64,1).astype(BF)
            kx_ref[2,sl,:]=pltpu.roll(vo,64,1).astype(BF)
            kx_ref[3,sl,:]=vo.astype(BF)
        def mask(i,_):
            r=pl.ds(pl.multiple_of(i*64,64),64)
            kk=lane_iota((64,2*T))-T
            qi=lax.broadcasted_iota(jnp.int32,(64,2*T),0)+i*64
            ok=(kk.astype(F32)>=tab_ref[r,255:256])&(kk<=qi)
            bias_ref[r,:]=jnp.where(ok,0.0,NEG)
            return 0
        lax.fori_loop(0,T//64,mask,0)
        if acc_in is None: acc_ref[...]=jnp.zeros_like(acc_ref)
        else: acc_ref[...]=acc_in[...]
    def run(lo):
        units=[(qb,e) for qb in (0,1) for e in (0,1)]
        rng=lambda qb: (lo,T+(qb+1)*QB)
        def mm1(u):
            qb,e=units[u]; a,b=rng(qb); n=b-a; z=u%2; rs=slice(qb*QB,(qb+1)*QB)
            qs=q_ref[:,rs,:].reshape(2*QB,128); dv=do_ref[:,rs,:].reshape(2*QB,128)
            if e==0:
                qt_ref[0,qb]=qs.T; qt_ref[1,qb]=dv.T
            s_ref[z,:,:n]=dotf(qs,kx_ref[e,a:b,:],NT)
            d_ref[z,:,:n]=dotf(dv,kx_ref[2+e,a:b,:],NT)
        def vp(u):
            qb,e=units[u]; a,b=rng(qb); n=b-a; z=u%2
            for r in range(0,2*QB,RB):
                rr=slice(r,r+RB); br=qb*QB+r%QB
                s=s_ref[z,rr,:n]+bias_ref[br:br+RB,a:b]
                m=jnp.max(s,-1,keepdims=True)
                p=jnp.exp(s-m)
                p=p*(1.0/jnp.sum(p,-1,keepdims=True))
                p_ref[z,rr,:n]=p.astype(BF)
                t=p*d_ref[z,rr,:n]
                ds_ref[z,rr,:n]=(t-p*jnp.sum(t,-1,keepdims=True)).astype(BF)
        def mm2(u):
            qb,e=units[u]; a,b=rng(qb); n=b-a; z=u%2; rs=slice(qb*QB,(qb+1)*QB)
            pb=p_ref[z,:,:n]; dsb=ds_ref[z,:,:n]
            o=dotf(pb,kx_ref[2+e,a:b,:]); dq=dotf(dsb,kx_ref[e,a:b,:])
            h=slice(e*64,e*64+64)
            acc_ref[:64,a:b]+=dotf(qt_ref[0,qb,h,:],dsb)
            acc_ref[64:,a:b]+=dotf(qt_ref[1,qb,h,:],pb)
            if e==0:
                oa_ref[0]=o; oa_ref[1]=dq
            else:
                oo=(oa_ref[0]+o).astype(BF)
                dq=((oa_ref[1]+dq)*0.125)
                C=tab_ref[rs,:128]; S=tab_ref[rs,128:]
                for k in (0,1):
                    o_ref[rs,k*128:(k+1)*128]=oo[k*QB:(k+1)*QB]
                    dq_ref[rs,k*128:(k+1)*128]=rope_apply(dq[k*QB:(k+1)*QB],C,S,-1).astype(BF)
        mm1(0)
        mm1(1); vp(0)
        mm2(0); mm1(2); vp(1)
        mm2(1); mm1(3); vp(2)
        mm2(2); vp(3)
        mm2(3)
    run(0)
    @pl.when(step==per-1)
    def _():
        prev_ref[...]=acc_ref[:,:T].astype(BF)
        own_ref[...]=acc_ref[:,T:]
    if rest_ref is not None:
        @pl.when(pl.program_id(0)==pl.num_programs(0)-1)
        def _(): rest_ref[...]=acc_ref[...]
def attn_part(base,count,q,do,kv,kvp,tab,prev=None,T=512,RB=32):
    NP,N,_=q.shape; QB=T//2; per=NP//2
    bf=BF; f=F32
    row=lambda h: lax.div(h+base,per); col=lambda h: lax.rem(h+base,per)
    hb=pl.BlockSpec((2,T,128),lambda h:(col(h),row(h),0)); rb=lambda w: pl.BlockSpec((T,w),lambda h:(row(h),0))
    c=lambda w: pl.BlockSpec((128,w),lambda h:(0,0)); ob=pl.BlockSpec((T,256),lambda h:(row(h),col(h)))
    more=prev is not None
    def body(q_ref,do_ref,kv_ref,kvp_ref,tab_ref,*refs):
        acc_in=None
        if more: acc_in=refs[0]; refs=refs[3:]
        o_ref,dq_ref,own_ref,prev_ref,*refs=refs
        rest_ref=None
        if not more: rest_ref,*refs=refs
        attn_kernel(base,per,RB,acc_in,q_ref,do_ref,kv_ref,kvp_ref,tab_ref,o_ref,dq_ref,own_ref,prev_ref,rest_ref,*refs)
    ins=[hb,hb,rb(128),rb(128),rb(256)]; args=[stay(v) for v in (q,do,kv,kvp,tab)]; alias={}
    outs=[hs((N,NP*128),bf)]*2+[hs((128,T),f),hs((128,T),bf)]; specs=[ob,ob,c(T),c(T)]
    if more:
        ins+=[c(2*T),ANY,ANY]; args+=[prev[2],prev[0],prev[1]]; alias={6:0,7:1}
    else:
        outs+=[hs((128,2*T),f)]; specs+=[c(2*T)]
    return pl.pallas_call(body,
      grid=(count,),in_specs=ins,out_specs=specs,
        scratch_shapes=[pltpu.VMEM((4,2*T,128),bf),pltpu.VMEM((T,2*T),f),pltpu.VMEM((2,2*QB,2*T),f),pltpu.VMEM((2,2*QB,2*T),f),
                        pltpu.VMEM((2,2*QB,2*T),bf),pltpu.VMEM((2,2*QB,2*T),bf),pltpu.VMEM((128,2*T),f),pltpu.VMEM((2,2,128,2*QB),bf),pltpu.VMEM((2,2*QB,128),f)],
      out_shape=outs,input_output_aliases=alias,cost_estimate=cost(8e9*count,1.4e6*count),
      compiler_params=params(1,28),name="attn_b" if more else "attn_a")(*args)
def wgrad_kernel(sc,g_ref,o_ref,dq_ref,ai_ref,keep_ref,send_ref,qb_ref,ot_ref,so_ref,sa_ref):
    N,D=o_ref.shape; hr=D//8
    def turn(i,_):
        r=pl.ds(pl.multiple_of(i*256,256),256); ot_ref[:,r]=o_ref[r,:].T
        return 0
    lax.fori_loop(0,N//256,turn,0)
    for i,c in enumerate((1-sc[0],sc[0])):
        def move(s,_):
            src=pl.ds(pl.multiple_of(s*2*hr+c*hr,hr),hr); to=pl.ds(pl.multiple_of((4*i+s)*hr,hr),hr)
            so_ref[to,:]=ot_ref[src,:]; sa_ref[to,:]=ai_ref[src,:]
            return 0
        lax.fori_loop(0,4,move,0)
    def part(i,_):
        c=pl.ds(pl.multiple_of(i*256,256),256)
        for k,(a,b) in enumerate(((so_ref,g_ref),(sa_ref,dq_ref))):
            w=dotf(a[...],b[:,c]).astype(BF).reshape(8,hr,256); to=pl.ds(pl.multiple_of(k*D+i*256,256),256)
            send_ref[:,:,to]=w[:4]; keep_ref[:,:,to]=w[4:]
        return 0
    lax.fori_loop(0,D//256,part,0)
    qb_ref[...]=jnp.sum(dq_ref[...].astype(F32),0,keepdims=True)
def wgrad(sc,g,o,dq,ai):
    N,D=g.shape
    args=(g,o,dq,ai)
    part=pl.BlockSpec((4,D//8,2*D),lambda j,s:(0,0,0)); out=hs((4,D//8,2*D+128),BF)
    return pl.pallas_call(wgrad_kernel,
        grid_spec=pltpu.PrefetchScalarGridSpec(num_scalar_prefetch=1,grid=(1,),in_specs=[whole(a) for a in args],out_specs=[part,part,pl.BlockSpec((1,D),lambda j,s:(0,0))],
            scratch_shapes=[pltpu.VMEM((D,N),BF)]*3),
        out_shape=[out,out,hs((1,D),F32)],cost_estimate=cost(2.6e9,9e6),compiler_params=params(1,30),name="wgrad")(sc,*args)
def kvgrad_kernel(sc,da_ref,db_ref,ra_ref,rb_ref,tab_ref,ai_ref,_k,_s,keep_ref,send_ref,dkv_ref,kvb_ref,w_ref):
    D,N=ai_ref.shape; T=N//2; hr=D//8
    for i,(ref,rr) in enumerate(((da_ref,ra_ref),(db_ref,rb_ref))):
        sl=slice(i*T,(i+1)*T)
        dkv_ref[sl,:]=rope_kv((ref[...]+rr[...].astype(F32)).T,tab_ref[sl,:128],tab_ref[sl,128:],-1).astype(BF)
    kvb_ref[...]=jnp.sum(dkv_ref[...].astype(F32),0,keepdims=True)
    w_ref[...]=dotf(ai_ref[...],dkv_ref[...])
    for dst,c in ((send_ref,1-sc[0]),(keep_ref,sc[0])):
        for s in range(4):
            dst[s]=w_ref[pl.ds(pl.multiple_of(s*2*hr+c*hr,hr),hr),:].astype(BF)
def kvgrad(sc,d0,d1,r0,r1,tab,ai,keep,send):
    D,N=ai.shape
    args=(d0,d1,r0,r1,tab,ai)
    col=pl.BlockSpec((4,D//8,128),lambda j,s:(0,0,2*D//128))
    outs=[hs(keep.shape,BF),hs(send.shape,BF),hs((N,128),BF),hs((1,128),F32)]
    return pl.pallas_call(kvgrad_kernel,
        grid_spec=pltpu.PrefetchScalarGridSpec(num_scalar_prefetch=1,grid=(1,),in_specs=[whole(a) for a in args]+[ANY,ANY],out_specs=[col,col,whole(outs[2]),whole(outs[3])],
            scratch_shapes=[pltpu.VMEM((D,128),F32)]),
        out_shape=outs,input_output_aliases={7:0,8:1},cost_estimate=cost(2e8,4e6),compiler_params=params(1,16),name="kvgrad")(sc,*args,keep,send)
def rows_of(w,B): return pl.BlockSpec((B,w),lambda j:(j,0))
def product_kernel(dims,a_ref,w_ref,out_ref):
    @pl.when(pl.program_id(0)==0)
    def _(): out_ref[...]=jnp.zeros_like(out_ref)
    out_ref[...]+=dotf(a_ref[...],w_ref[...],dims)
def product(a,w,across,name):
    N,F=a.shape; D=w.shape[0] if across else w.shape[1]
    ws=pl.BlockSpec((D,D),(lambda j:(0,j)) if across else (lambda j:(j,0)))
    return pl.pallas_call(functools.partial(product_kernel,NT if across else NN),grid=(F//D,),
      in_specs=[pl.BlockSpec((N,D),lambda j:(0,j)),ws],out_specs=pl.BlockSpec((N,D),lambda j:(0,0)),out_shape=hs((N,D),F32),
      cost_estimate=cost(4.8e9,1.4e7),compiler_params=params(1,None),name=name)(a,w)
def postb_kernel(x_ref,g_ref,dq_ref,dkv_ref,c2_ref,wq_ref,wk_ref,wv_ref,vec_ref,qb_ref,hb_ref,kvb_ref,ig_ref,sm_ref):
    j=pl.program_id(0)
    @pl.when(j==0)
    def _():
        sm_ref[...]=jnp.zeros_like(sm_ref)
        sm_ref[5:6,:]=qb_ref[...]; sm_ref[6:10,:]=hb_ref[...]; sm_ref[10:11,:kvb_ref.shape[1]]=kvb_ref[...]
    g=g_ref[...].astype(F32)
    n,s=ln(x_ref[...].astype(F32))
    dkv=dkv_ref[...]
    c1=dotf(dq_ref[...],wq_ref[...],NT)+dotf(dkv[:,:64],wk_ref[...])+dotf(dkv[:,64:],wv_ref[...])
    c2=c2_ref[...]
    u=c1*vec_ref[V_G1:V_G1+1,:]+c2*vec_ref[V_G2:V_G2+1,:]
    ig_ref[...]=g+s*(u-jnp.mean(u,-1,keepdims=True)-n*jnp.mean(u*n,-1,keepdims=True))
    for i,v in enumerate((c1*n,c1,c2*n,c2,g)):
        sm_ref[i:i+1,:]+=jnp.sum(v,0,keepdims=True)
def postb(x,g,dq,dkv,c2,wq,wk,wv,vec,qb,hb,kvb,B=256):
    N,D=x.shape
    return pl.pallas_call(postb_kernel,grid=(N//B,),
      in_specs=[rows_of(D,B)]*3+[rows_of(128,B),rows_of(D,B)]+[whole(a) for a in (wq,wk,wv,vec,qb,hb,kvb)],
      out_specs=[rows_of(D,B),pl.BlockSpec((16,D),lambda j:(0,0))],
      out_shape=[hs((N,D),F32),hs((16,D),F32)],
      cost_estimate=cost(2e9,1.2e7),compiler_params=params(1,None),name="postb")(x,g,dq,dkv,c2,wq,wk,wv,vec,qb,hb,kvb)
def posta_kernel(x_ref,o_ref,mb_ref,wo_ref,vec_ref,lo_ref):
    lo_ref[...]=(x_ref[...].astype(F32)+(dotf(o_ref[...],wo_ref[...])+vec_ref[V_O:V_O+1,:])+(mb_ref[...]+vec_ref[V_D:V_D+1,:])).astype(BF)
def posta(x,o,mb,wo,vec,B=256):
    N,D=x.shape
    return pl.pallas_call(posta_kernel,grid=(N//B,),
      in_specs=[rows_of(D,B)]*3+[whole(a) for a in (wo,vec)],
      out_specs=rows_of(D,B),out_shape=hs((N,D),BF),
      cost_estimate=cost(2e9,9e6),compiler_params=params(1,None),name="posta")(x,o,mb,wo,vec)
def final_kernel(sc,m_ref,mr_ref,a_ref,ar_ref,s_ref,sr_ref,w1_ref,w2_ref,wo_ref,wq_ref,wk_ref,wv_ref,
                 n1g_ref,n1b_ref,n2g_ref,n2b_ref,ob_ref,qb_ref,db_ref,hb_ref,kb_ref,vb_ref,kv_ref):
    W=w2_ref.shape[0]//2; D=m_ref.shape[1]; q=D//4; hr=a_ref.shape[0]; pr=hr//4; mr=m_ref.shape[0]//4
    for r0,(m,a) in enumerate(((m_ref,a_ref),(mr_ref,ar_ref))):
        h=sc[0]^r0
        def piece(k,_):
            i=sc[2+2*r0]^(k>>1); j=sc[3+2*r0]^(k&1)
            src=pl.ds(pl.multiple_of(k*mr,mr),mr)
            @pl.when(i==0)
            def _(): w2_ref[pl.ds(pl.multiple_of(h*W+j*mr,mr),mr),:]=m[src,:].astype(F32)
            @pl.when(i!=0)
            def _():
                for c in (0,1):
                    w1_ref[:,pl.ds(pl.multiple_of((2*j+c)*2*W+h*W,W),W)]=m[src,c*W:(c+1)*W].astype(F32)
            return 0
        lax.fori_loop(0,4,piece,0)
        for k in range(4):
            i=sc[2+2*r0]^(k>>1); j=sc[3+2*r0]^(k&1)
            to=pl.ds(pl.multiple_of(h*hr+i*2*pr+j*pr,pr),pr)
            wo_ref[to,:]=a[k*pr:(k+1)*pr,:D].astype(F32)
            wq_ref[to,:]=a[k*pr:(k+1)*pr,D:2*D].astype(F32)
            kv_ref[to,:]=a[k*pr:(k+1)*pr,2*D:].astype(F32)
    keys=kv_ref[...].T
    wk_ref[...]=keys[:64]; wv_ref[...]=keys[64:]
    t=s_ref[...]+sr_ref[...]
    for s in range(4):
        @pl.when(sc[1]==s)
        def _():
            for k,ref in enumerate((n1g_ref,n1b_ref,n2g_ref,n2b_ref,ob_ref,qb_ref)):
                ref[...]=t[k:k+1,s*q:(s+1)*q].reshape(q)
            db_ref[...]=t[4:5,s*q:(s+1)*q].reshape(q)
            hb_ref[...]=t[6+s:7+s,:].reshape(D)
            n=kb_ref.shape[0]; kb_ref[...]=t[10:11,s*n:(s+1)*n].reshape(n)
            n=vb_ref.shape[0]; vb_ref[...]=t[10:11,64+s*n:64+(s+1)*n].reshape(n)
def final(sc,m,mr,a,ar,s,sr,F,rotd):
    D=m.shape[1]; f=F32; v=hs((D//4,),f)
    outs=[hs((D//4,F),f),hs((F//4,D),f),hs((D//4,D),f),hs((D//4,D),f),hs((64,D//4),f),hs((64,D//4),f)]+[v]*7+[hs((D,),f),hs((rotd//4,),f),hs((16,),f)]
    return pl.pallas_call(final_kernel,
        grid_spec=pltpu.PrefetchScalarGridSpec(num_scalar_prefetch=1,grid=(1,),in_specs=[whole(u) for u in (m,mr,a,ar,s,sr)],out_specs=[whole(u) for u in outs],
            scratch_shapes=[pltpu.VMEM((D//4,128),F32)]),
        out_shape=outs,cost_estimate=cost(1e6,9e6),compiler_params=params(1,24),name="final")(sc,m,mr,a,ar,s,sr)
def bits_of(n):
    return n.bit_length()-1
def after(xs,*deps):
    out=lax.optimization_barrier(tuple(xs)+tuple(deps))
    return out[:len(xs)]
def dp_stages():
    dp=lax.axis_size("dp"); nb=bits_of(dp); i=lax.axis_index("dp")
    core=i&1
    st=[(core,[(k,k^1) for k in range(dp)],core)]
    for t in range(1,nb):
        up,down=t,nb-t
        a,b=(i>>up)&1,(i>>down)&1
        st.append((jnp.where(core==0,a,b),[(k,k^((1<<up) if k%2==0 else (1<<down))) for k in range(dp)],jnp.where(core==0,b,a)))
    return st
def pick(G,bit,ax): return lax.dynamic_index_in_dim(G,bit,ax,keepdims=False)
def add(a,b): return (a.astype(F32)+b.astype(F32)).astype(a.dtype)
class Stream:
    def __init__(self,stages,at,send,keep):
        self.st=stages; self.at=at; self.send=send; self.keep=keep; self.left=len(stages)
    def go(self):
        n=len(self.st)
        if self.at<n: axis,pairs="dp",self.st[self.at][1]
        else: axis="sp"; pairs=[(k,k^(1<<(self.at-n))) for k in range(lax.axis_size("sp"))]
        self.recv=lax.ppermute(self.send,axis,pairs)
        return self.recv
    def land(self):
        k,r=self.keep,self.recv; self.at+=1
        n=len(self.st); s=lax.axis_index("sp")
        if self.at<n:
            split=lambda t: t.reshape(t.shape[0],2,t.shape[1]//2,t.shape[2]); bit=self.st[self.at][0]; ax=1
        elif self.at==n:
            split=lambda t: t.reshape(2,2,t.shape[1],t.shape[2]); bit=s&1; ax=1
        elif self.at==n+1:
            split=lambda t: t; bit=s>>1; ax=0
        else:
            self.own=add(k,r); self.left=n
            return
        k,r=split(k),split(r)
        self.send=add(pick(k,1-bit,ax),pick(r,1-bit,ax))
        self.keep=add(pick(k,bit,ax),pick(r,bit,ax))
    def gather_go(self):
        self.left-=1
        self.recv=lax.ppermute(self.own,"dp",self.st[self.left][1])
        return self.recv
    def gather_land(self):
        self.own=jnp.concatenate([self.own,self.recv],0)
    def settle(self,x,of):
        n=len(self.st)
        if n<=3: return x
        g=x.reshape((4,)+(2,)*(n-3)+(-1,x.shape[1]))
        for t in range(3,n): g=jnp.where(self.st[t][of]==0,g,jnp.flip(g,t-2))
        return g.reshape(x.shape)
def on_device(inputs,out_grad,segment_ids,positions,norm1_gain,norm1_bias,norm2_gain,norm2_bias,query_weight,query_bias,key_weight,key_bias,value_weight,value_bias,output_weight,output_bias,hidden_weight,hidden_bias,down_weight,down_bias):
    sp=lax.axis_size("sp"); s=lax.axis_index("sp")
    R,T,D=inputs.shape; hd=key_weight.shape[1]; rotd=key_bias.shape[0]
    F=hidden_weight.shape[1]
    N=R*T
    x=inputs.reshape(N,D); g=out_grad.reshape(N,D)
    vec=table(norm1_gain,norm1_bias,norm2_gain,norm2_bias,query_bias,output_bias,down_bias,key_bias,value_bias,hidden_bias)
    pos=lax.dynamic_slice_in_dim(positions,s*T,T,1)
    st=dp_stages(); core=st[0][0]; bit1=st[1][0]
    both=[(i,i^1) for i in range(sp)]
    Ms,act,gp,dbs,mi=mlp_half(jnp.stack([1-core,bit1]),x,g,hidden_weight,down_weight,vec)
    Mr=lax.ppermute(Ms,"dp",st[0][1])
    pf=pos.astype(F32).reshape(N)
    freq=10000.0**(-(jnp.arange(rotd//2,dtype=F32)*2.0)/rotd)
    ang=pf[None,:]*freq[:,None]
    ds=(jnp.arange(T,dtype=F32)[None,:]-pos.astype(F32)).reshape(1,N)
    cs=jnp.concatenate([jnp.cos(ang),jnp.sin(ang),ds,jnp.zeros((7,N),F32)],0)
    xq,=after([x],dbs)
    q,kv,do,tab,ai=pre(xq,g,cs,query_weight,key_weight.T,value_weight.T,output_weight,vec)
    kv,Mr=after([kv,Mr],q)
    kvp=lax.ppermute(kv,"sp",both)
    mi,=after([mi],q)
    keep,send,act,gp,dbk=mlp_half(jnp.stack([core,bit1]),mi,g,hidden_weight,down_weight,vec,recv=Mr,dbs=dbs,act=act,gp=gp)
    M=Stream(st,1,send,keep)
    M.send,kvp=after([M.send,kvp],dbk)
    M.go()
    q,=after([q],dbk)
    o,dq,d0,k0,part=attn_part(0,2*(D//256)*2//3,q,do,kv,kvp,tab,T=T)
    M.recv,k0=after([M.recv,k0],dq)
    M.land()
    r0=lax.ppermute(k0,"sp",both); M.go()
    o,dq=after([o,dq],M.send,k0)
    o,dq,d1,k1=attn_part(2*(D//256)*2//3,2*(D//256)-2*(D//256)*2//3,q,do,kv,kvp,tab,prev=(o,dq,part),T=T)
    k1,M.recv,r0=after([k1,M.recv,r0],dq)
    r1=lax.ppermute(k1,"sp",both)
    while True:
        M.land()
        if M.at>=len(st): break
        M.go()
    o_,=after([o],M.send,k1)
    sc=core.reshape(1)
    wkeep,wsend,qb=wgrad(sc,g,o_,dq,ai)
    M.send,wkeep,wsend,r1=after([M.send,wkeep,wsend,r1],qb)
    M.send,=after([M.send],r1)
    M.go()
    r1,=after([r1],M.send)
    wkeep,wsend,dkv,kvb=kvgrad(sc,d0,d1,r0,r1,tab,ai,wkeep,wsend)
    A=Stream(st,0,wsend,wkeep)
    small=None
    todo=[("dp",p) for _,p,_o in st]+[("sp",[(i,i^(1<<k)) for i in range(sp)]) for k in range(bits_of(sp))]
    c2=mb=ig=lo=sm=None
    fill=["c2","ig","mb","lo"]
    held=1
    busy=True
    while True:
        rs=A.at<len(st)+2
        ag=not rs and A.left>1
        if not (rs or ag or busy or M.left>1 or len(todo)>1): break
        if rs: A.go(); moved=[A.send]
        elif ag: A.gather_go(); moved=[A.own]
        else: moved=[]
        if not busy:
            if M.at<len(st)+2: M.go(); busy=True; held=1; moved.append(M.send)
            elif M.left>1: moved.append(M.own); M.gather_go(); busy=True; held=0 if M.left>1 else 1
        sr=None
        if small is not None and len(todo)>1: axis,pairs=todo.pop(0); sr=lax.ppermute(small,axis,pairs); moved.append(small)
        deps=[]
        if fill:
            k=fill.pop(0)
            if k=="c2": gk,=after([gp],*moved); c2=product(gk,hidden_weight,True,"back"); deps=[c2]
            if k=="ig": xk,=after([x],*moved); ig,sm=postb(xk,g,dq,dkv,c2,query_weight,key_weight.T,value_weight.T,vec,qb,dbk,kvb); deps=[ig]
            if k=="mb": ak,=after([act],*moved); mb=product(ak,down_weight,False,"down"); deps=[mb]
            if k=="lo": xk,=after([x],*moved); lo=posta(xk,o,mb,output_weight,vec); deps=[lo]
        lands=busy and held==0
        got=([A.recv] if rs or ag else [])+([M.recv] if lands else [])+([sr] if sr is not None else [])
        got=list(after(got,*deps))
        if rs or ag: A.recv=got.pop(0)
        if lands: M.recv=got.pop(0)
        if sr is not None: small=small+got.pop(0)
        if rs: A.land()
        elif ag: A.gather_land()
        if lands:
            busy=False
            if M.at<len(st)+2: M.land()
            else: M.gather_land()
        held-=1
        if small is None and ig is not None:
            small=sm
    Mr=lax.ppermute(M.own,"dp",st[0][1])
    Ar=lax.ppermute(A.own,"dp",st[0][1])
    axis,pairs=todo.pop(0)
    sr=lax.ppermute(small,axis,pairs)
    zero=jnp.zeros_like(core)
    where=jnp.stack([core,s]+[st[t][of] if len(st)>t else zero for of in (0,2) for t in (1,2)])
    rw1,rw2,ro,rq,rk,rv,n1g,n1b,n2g,n2b,ob,qbg,db,hb,kb,vb=final(where,M.settle(M.own,0),M.settle(Mr,2),A.settle(A.own,0),A.settle(Ar,2),small,sr,F,rotd)
    return (lo.reshape(R,T,D),ig.reshape(R,T,D),n1g,n1b,n2g,n2b,rq,qbg,rk.T,kb,rv.T,vb,ro,ob,rw1,hb,rw2,db)
def solution(mesh):
    t=P("dp","sp",None); m=P("dp",None); w=P()
    v=P("sp"); v2=P("sp",None)
    return jax.shard_map(on_device,mesh=mesh,in_specs=(t,t,m,m)+(w,)*16,
        out_specs=(t,t,v,v,v,v,v2,v,v2,v,v2,v,v2,v,v2,v,v2,v),check_vma=False)
```

```python
import functools
import jax
import jax.numpy as jnp
from jax import lax
from jax.experimental import pallas as pl
from jax.experimental.pallas import tpu as pltpu
from jax.sharding import PartitionSpec as P
EPS=1e-5
VMEM_ALL=67043328
NN=(((1,),(0,)),((),()))
NT=(((1,),(1,)),((),()))
TN=(((0,),(0,)),((),()))
BF=jnp.bfloat16
F32=jnp.float32
NEG=-1e30
C1=0.7071067811865476
C2=0.3989422804014327
def dotf(a,b,dims=NN):
    return lax.dot_general(a,b,dims,preferred_element_type=F32)
def ln(xv):
    m=jnp.mean(xv,-1,keepdims=True); c=xv-m
    s=lax.rsqrt(jnp.mean(c*c,-1,keepdims=True)+EPS)
    return c*s,s
def cost(flops,bytes_):
    return pl.CostEstimate(flops=int(flops),bytes_accessed=int(bytes_),transcendentals=0)
def params(n,mb):
    return pltpu.CompilerParams(dimension_semantics=("arbitrary",)*n,vmem_limit_bytes=VMEM_ALL if mb is None else mb<<20)
ANY=pl.BlockSpec(memory_space=pl.ANY)
hs=jax.ShapeDtypeStruct
def stay(v):
    return pltpu.with_memory_space_constraint(v,pltpu.HBM)
def whole(a):
    z=(0,)*len(a.shape)
    return pl.BlockSpec(a.shape,lambda *_: z)
def lane_iota(shape):
    return lax.broadcasted_iota(jnp.int32,shape,len(shape)-1)
V_G1,V_B1,V_G2,V_B2,V_Q,V_KV,V_O,V_D,V_H=range(9)
def table_kernel(*refs):
    *vs,kb_ref,vb_ref,hb_ref,out_ref=refs
    D=out_ref.shape[1]
    for k,ref in zip((V_G1,V_B1,V_G2,V_B2,V_Q,V_O,V_D),vs):
        out_ref[k:k+1,:]=ref[...].astype(F32).reshape(1,D)
    n=kb_ref.shape[0]; h=vb_ref.shape[0]
    out_ref[V_KV:V_KV+1,:]=jnp.zeros((1,D),F32)
    out_ref[V_KV:V_KV+1,:n]=kb_ref[...].astype(F32).reshape(1,n)
    out_ref[V_KV:V_KV+1,h:2*h]=vb_ref[...].astype(F32).reshape(1,h)
    for i in range(4):
        out_ref[V_H+i:V_H+i+1,:]=hb_ref[i*D:(i+1)*D].astype(F32).reshape(1,D)
def table(*vs):
    return pl.pallas_call(table_kernel,out_shape=hs((V_H+4,vs[0].shape[0]),F32),compiler_params=params(0,None),name="table")(*vs)
def rope_apply(v,C,S,sign):
    l=lane_iota(v.shape)&63
    sh=jnp.where(l<8,pltpu.roll(v,120,1),jnp.where(l<16,pltpu.roll(v,8,1),0.0))
    return v*C+S*sh if sign>0 else v*C-S*sh
def rope_kv(v,C,S,sign):
    l=lane_iota(v.shape)
    return rope_apply(v,jnp.where(l<64,C,1.0),jnp.where(l<64,S,0.0),sign)
def pre_kernel(x_ref,g_ref,cs_ref,wq_ref,wk_ref,wv_ref,wo_ref,vec_ref,q_ref,kv_ref,do_ref,tab_ref,ai_ref):
    B=x_ref.shape[0]
    row=lambda k: vec_ref[k:k+1,:]
    n,_=ln(x_ref[...].astype(F32))
    ai=(n*row(V_G1)+row(V_B1)).astype(BF)
    ai_ref[...]=ai.T
    t=cs_ref[...]
    t=jnp.concatenate([t,jnp.zeros((128-t.shape[0],B),F32)],0).T
    l=lane_iota((B,128))
    co=jnp.where(l<8,t,0.0)
    c2=co+pltpu.roll(co,8,1)
    C=c2+pltpu.roll(c2,64,1)+jnp.where((l&63)>=16,1.0,0.0)
    sb=jnp.where((l>=8)&(l<16),t,0.0)
    s2=sb-pltpu.roll(sb,120,1)
    S=s2+pltpu.roll(s2,64,1)
    tab_ref[:,:128]=C
    tab_ref[:,128:]=jnp.where(l==127,pltpu.roll(t,111,1),S)
    q=dotf(ai,wq_ref[...])+row(V_Q)
    do=dotf(g_ref[...],wo_ref[...],NT)
    for k in range(q.shape[1]//128):
        c=slice(k*128,k*128+128)
        q_ref[k]=(rope_apply(q[:,c],C,S,1)*0.125).astype(BF)
        do_ref[k]=do[:,c].astype(BF)
    kv=jnp.concatenate([dotf(ai,wk_ref[...],NT),dotf(ai,wv_ref[...],NT)],1)+row(V_KV)[:,:128]
    kv_ref[...]=rope_kv(kv,C,S,1).astype(BF)
def pre(x,g,cs,wq,wk,wv,wo,vec,B=256):
    N,D=x.shape; NP=D//128
    row=lambda w: pl.BlockSpec((B,w),lambda j:(j,0))
    pair=pl.BlockSpec((NP,B,128),lambda j:(0,j,0)); col=lambda h: pl.BlockSpec((h,B),lambda j:(0,j))
    return pl.pallas_call(pre_kernel,grid=(N//B,),
      in_specs=[row(D),row(D),col(cs.shape[0])]+[whole(a) for a in (wq,wk,wv,wo,vec)],
      out_specs=[pair,row(128),pair,row(256),col(D)],
      out_shape=[hs((NP,N,128),BF),hs((N,128),BF),hs((NP,N,128),BF),hs((N,256),F32),hs((D,N),BF)],
      cost_estimate=cost(4e9,1e7),compiler_params=params(1,None),name="pre")(x,g,cs,wq,wk,wv,wo,vec)
def mlp_kernel(last,rows,*refs):
    if last:
        (sc,x_ref,g_ref,wa_ref,wb_ref,va_ref,vb_ref,vec_ref,r2_ref,r1_ref,dbs_ref,_a,_g,
         keep_ref,send_ref,act_hbm,gp_hbm,db_ref,w1_ref,w2_ref,b_ref,act_ref,gp_ref,sem)=refs
        mi_ref=x_ref
    else:
        (sc,x_ref,g_ref,wa_ref,wb_ref,va_ref,vb_ref,vec_ref,
         out_ref,act_hbm,gp_hbm,db_ref,mi_ref,w1_ref,w2_ref,b_ref,act_ref,gp_ref,sem)=refs
    j=pl.program_id(0); N,D=x_ref.shape; W=wa_ref.shape[1]
    h=sc[0]
    def copies(jj):
        out=[]
        for i,(scr,hbm) in enumerate(((act_ref,act_hbm),(gp_ref,gp_hbm))):
            for k in (0,1):
                off=pl.multiple_of((2*(2*jj+k)+h)*W,W)
                out.append(pltpu.make_async_copy(scr.at[:,k*W:(k+1)*W],hbm.at[:,pl.ds(off,W)],sem.at[i,k]))
        return out
    if not last:
        @pl.when(j==0)
        def _():
            def body(i,_):
                r=pl.ds(pl.multiple_of(i*256,256),256)
                n,_s=ln(x_ref[r,:].astype(F32))
                mi_ref[r,:]=(n*vec_ref[V_G2:V_G2+1,:]+vec_ref[V_B2:V_B2+1,:]).astype(BF)
                return 0
            lax.fori_loop(0,N//256,body,0)
    w1_ref[:,:W]=wa_ref[...]; w1_ref[:,W:]=wb_ref[...]
    w2_ref[:W,:]=va_ref[...]; w2_ref[W:,:]=vb_ref[...]
    lane=pl.ds(pl.multiple_of(h*W,128),W)
    b_ref[:,:W]=vec_ref[pl.ds(V_H+2*j,1),lane]; b_ref[:,W:]=vec_ref[pl.ds(V_H+2*j+1,1),lane]
    @pl.when(j>0)
    def _():
        for c in copies(j-1): c.wait()
    for r in range(0,N,rows):
        sl=slice(r,r+rows)
        pre_=dotf(mi_ref[sl,:],w1_ref[...])+b_ref[...]
        da=dotf(g_ref[sl,:],w2_ref[...],NT)
        phi=0.5*(1.0+lax.erf(pre_*C1))
        act_ref[sl,:]=(pre_*phi).astype(BF)
        gp_ref[sl,:]=(da*(phi+pre_*(jnp.exp(pre_*pre_*-0.5)*C2))).astype(BF)
    for c in copies(j): c.start()
    db=jnp.sum(gp_ref[...].astype(F32),0,keepdims=True)
    if last:
        other=pl.ds(pl.multiple_of((1-h)*W,128),W)
        for k in (0,1):
            db_ref[pl.ds(2*j+k,1),lane]=db[:,k*W:(k+1)*W]
            db_ref[pl.ds(2*j+k,1),other]=dbs_ref[j][:,k*W:(k+1)*W]
    else: db_ref[0]=db
    q=D//4
    to=pl.ds(pl.multiple_of(j*q,q),q)
    if last: bit=sc[1]
    def part(i,_):
        c=pl.ds(pl.multiple_of(i*256,256),256)
        d2=dotf(act_ref[...],g_ref[:,c],TN).reshape(2,W,256)
        d1=dotf(mi_ref[...],gp_ref[:,c],TN).reshape(4,q,256)
        if last:
            d2=(d2+r2_ref[:,:,c].astype(F32)).astype(BF)
            d1=(d1+r1_ref[:,:,c].astype(F32)).astype(BF)
            @pl.when(bit==0)
            def _():
                keep_ref[pl.ds(2*j,2),:,c]=d2; send_ref[:,to,c]=d1
            @pl.when(bit!=0)
            def _():
                send_ref[pl.ds(2*j,2),:,c]=d2; keep_ref[:,to,c]=d1
        else:
            out_ref[pl.ds(2*j,2),:W,c]=d2.astype(BF)
            out_ref[:,pl.ds(pl.multiple_of(W+j*q,q),q),c]=d1.astype(BF)
        return 0
    lax.fori_loop(0,2*W//256,part,0)
    @pl.when(j==pl.num_programs(0)-1)
    def _():
        for c in copies(j): c.wait()
def mlp_half(sc,x,g,w1,w2,vec,recv=None,dbs=None,act=None,gp=None,rows=256):
    N,D=x.shape; F=w1.shape[1]; W=F//8
    last=recv is not None
    cb=lambda sh,k,ax: pl.BlockSpec(sh,(lambda j,s:(0,2*(2*j+k)+s[0])) if ax else (lambda j,s:(2*(2*j+k)+s[0],0)))
    ins=[whole(x),whole(g),cb((D,W),0,1),cb((D,W),1,1),cb((W,D),0,0),cb((W,D),1,0),whole(vec)]
    args=[x,g,w1,w1,w2,w2,vec]
    ag=[hs((N,F),BF),hs((N,F),BF),hs((2,1,2*W),F32)]
    ags=[ANY,ANY,pl.BlockSpec((1,1,2*W),lambda j,s:(j,0,0))]
    alias={}; scr=[]
    if last:
        ins+=[pl.BlockSpec((2,W,D),lambda j,s:(j,0,0)),pl.BlockSpec((4,D//4,D),lambda j,s:(0,W//(D//4)+j,0)),whole(dbs),ANY,ANY]
        args+=[recv,recv,dbs,act,gp]
        outs=[hs((4,W,D),BF)]*2+ag[:2]+[hs((4,2*W),F32)]
        ospec=[whole(outs[0])]*2+ags[:2]+[whole(outs[-1])]
        alias={1+10:2,1+11:3}
    else:
        outs=[hs((4,2*W,D),BF)]+ag+[hs((N,D),BF)]
        ospec=[whole(outs[0])]+ags+[whole(outs[-1])]
    return pl.pallas_call(functools.partial(mlp_kernel,last,rows),
        grid_spec=pltpu.PrefetchScalarGridSpec(num_scalar_prefetch=1,grid=(2,),in_specs=ins,out_specs=ospec,
            scratch_shapes=[pltpu.VMEM((D,2*W),BF),pltpu.VMEM((2*W,D),BF),pltpu.VMEM((1,2*W),F32),
                            pltpu.VMEM((N,2*W),BF),pltpu.VMEM((N,2*W),BF),pltpu.SemaphoreType.DMA((2,2))]),
        out_shape=outs,input_output_aliases=alias,cost_estimate=cost(4*N*D*F*1.3,20e6),
        compiler_params=params(1,None),name="mlp_keep" if last else "mlp_send")(sc,*args)

def attn_kernel(base,per,RB,acc_in,q_ref,do_ref,kv_ref,kvp_ref,tab_ref,o_ref,dq_ref,own_ref,prev_ref,rest_ref,kx_ref,bias_ref,s_ref,d_ref,p_ref,ds_ref,acc_ref,qt_ref,oa_ref):
    first=pl.program_id(0)==0
    step=lax.rem(pl.program_id(0)+base,per)
    T=q_ref.shape[1]; QB=T//2
    @pl.when(first|(step==0))
    def _():
        for i,ref in enumerate((kvp_ref,kv_ref)):
            kv=ref[...].astype(F32)
            l=lane_iota(kv.shape)
            ke=jnp.where(l<64,kv,0.0); vo=jnp.where(l>=64,kv,0.0)
            sl=slice(i*T,(i+1)*T)
            kx_ref[0,sl,:]=ke.astype(BF)
            kx_ref[1,sl,:]=pltpu.roll(ke,64,1).astype(BF)
            kx_ref[2,sl,:]=pltpu.roll(vo,64,1).astype(BF)
            kx_ref[3,sl,:]=vo.astype(BF)
        def mask(i,_):
            r=pl.ds(pl.multiple_of(i*64,64),64)
            kk=lane_iota((64,2*T))-T
            qi=lax.broadcasted_iota(jnp.int32,(64,2*T),0)+i*64
            ok=(kk.astype(F32)>=tab_ref[r,255:256])&(kk<=qi)
            bias_ref[r,:]=jnp.where(ok,0.0,NEG)
            return 0
        lax.fori_loop(0,T//64,mask,0)
        if acc_in is None: acc_ref[...]=jnp.zeros_like(acc_ref)
        else: acc_ref[...]=acc_in[...]
    def run(lo):
        units=[(qb,e) for qb in (0,1) for e in (0,1)]
        rng=lambda qb: (lo,T+(qb+1)*QB)
        def mm1(u):
            qb,e=units[u]; a,b=rng(qb); n=b-a; z=u%2; rs=slice(qb*QB,(qb+1)*QB)
            qs=q_ref[:,rs,:].reshape(2*QB,128); dv=do_ref[:,rs,:].reshape(2*QB,128)
            if e==0:
                qt_ref[0,qb]=qs.T; qt_ref[1,qb]=dv.T
            s_ref[z,:,:n]=dotf(qs,kx_ref[e,a:b,:],NT)
            d_ref[z,:,:n]=dotf(dv,kx_ref[2+e,a:b,:],NT)
        def vp(u):
            qb,e=units[u]; a,b=rng(qb); n=b-a; z=u%2
            for r in range(0,2*QB,RB):
                rr=slice(r,r+RB); br=qb*QB+r%QB
                s=s_ref[z,rr,:n]+bias_ref[br:br+RB,a:b]
                m=jnp.max(s,-1,keepdims=True)
                p=jnp.exp(s-m)
                p=p*(1.0/jnp.sum(p,-1,keepdims=True))
                p_ref[z,rr,:n]=p.astype(BF)
                t=p*d_ref[z,rr,:n]
                ds_ref[z,rr,:n]=(t-p*jnp.sum(t,-1,keepdims=True)).astype(BF)
        def mm2(u):
            qb,e=units[u]; a,b=rng(qb); n=b-a; z=u%2; rs=slice(qb*QB,(qb+1)*QB)
            pb=p_ref[z,:,:n]; dsb=ds_ref[z,:,:n]
            o=dotf(pb,kx_ref[2+e,a:b,:]); dq=dotf(dsb,kx_ref[e,a:b,:])
            h=slice(e*64,e*64+64)
            acc_ref[:64,a:b]+=dotf(qt_ref[0,qb,h,:],dsb)
            acc_ref[64:,a:b]+=dotf(qt_ref[1,qb,h,:],pb)
            if e==0:
                oa_ref[0]=o; oa_ref[1]=dq
            else:
                oo=(oa_ref[0]+o).astype(BF)
                dq=((oa_ref[1]+dq)*0.125)
                C=tab_ref[rs,:128]; S=tab_ref[rs,128:]
                for k in (0,1):
                    o_ref[rs,k*128:(k+1)*128]=oo[k*QB:(k+1)*QB]
                    dq_ref[rs,k*128:(k+1)*128]=rope_apply(dq[k*QB:(k+1)*QB],C,S,-1).astype(BF)
        mm1(0)
        mm1(1); vp(0)
        mm2(0); mm1(2); vp(1)
        mm2(1); mm1(3); vp(2)
        mm2(2); vp(3)
        mm2(3)
    run(0)
    @pl.when(step==per-1)
    def _():
        prev_ref[...]=acc_ref[:,:T].astype(BF)
        own_ref[...]=acc_ref[:,T:]
    if rest_ref is not None:
        @pl.when(pl.program_id(0)==pl.num_programs(0)-1)
        def _(): rest_ref[...]=acc_ref[...]
def attn_part(base,count,q,do,kv,kvp,tab,prev=None,T=512,RB=32):
    NP,N,_=q.shape; QB=T//2; per=NP//2
    bf=BF; f=F32
    row=lambda h: lax.div(h+base,per); col=lambda h: lax.rem(h+base,per)
    hb=pl.BlockSpec((2,T,128),lambda h:(col(h),row(h),0)); rb=lambda w: pl.BlockSpec((T,w),lambda h:(row(h),0))
    c=lambda w: pl.BlockSpec((128,w),lambda h:(0,0)); ob=pl.BlockSpec((T,256),lambda h:(row(h),col(h)))
    more=prev is not None
    def body(q_ref,do_ref,kv_ref,kvp_ref,tab_ref,*refs):
        acc_in=None
        if more: acc_in=refs[0]; refs=refs[3:]
        o_ref,dq_ref,own_ref,prev_ref,*refs=refs
        rest_ref=None
        if not more: rest_ref,*refs=refs
        attn_kernel(base,per,RB,acc_in,q_ref,do_ref,kv_ref,kvp_ref,tab_ref,o_ref,dq_ref,own_ref,prev_ref,rest_ref,*refs)
    ins=[hb,hb,rb(128),rb(128),rb(256)]; args=[stay(v) for v in (q,do,kv,kvp,tab)]; alias={}
    outs=[hs((N,NP*128),bf)]*2+[hs((128,T),f),hs((128,T),bf)]; specs=[ob,ob,c(T),c(T)]
    if more:
        ins+=[c(2*T),ANY,ANY]; args+=[prev[2],prev[0],prev[1]]; alias={6:0,7:1}
    else:
        outs+=[hs((128,2*T),f)]; specs+=[c(2*T)]
    return pl.pallas_call(body,
      grid=(count,),in_specs=ins,out_specs=specs,
        scratch_shapes=[pltpu.VMEM((4,2*T,128),bf),pltpu.VMEM((T,2*T),f),pltpu.VMEM((2,2*QB,2*T),f),pltpu.VMEM((2,2*QB,2*T),f),
                        pltpu.VMEM((2,2*QB,2*T),bf),pltpu.VMEM((2,2*QB,2*T),bf),pltpu.VMEM((128,2*T),f),pltpu.VMEM((2,2,128,2*QB),bf),pltpu.VMEM((2,2*QB,128),f)],
      out_shape=outs,input_output_aliases=alias,cost_estimate=cost(8e9*count,1.4e6*count),
      compiler_params=params(1,28),name="attn_b" if more else "attn_a")(*args)
def wgrad_kernel(sc,g_ref,o_ref,dq_ref,ai_ref,keep_ref,send_ref,qb_ref,ot_ref,so_ref,sa_ref):
    N,D=o_ref.shape; hr=D//8
    def turn(i,_):
        r=pl.ds(pl.multiple_of(i*256,256),256); ot_ref[:,r]=o_ref[r,:].T
        return 0
    lax.fori_loop(0,N//256,turn,0)
    for i,c in enumerate((1-sc[0],sc[0])):
        def move(s,_):
            src=pl.ds(pl.multiple_of(s*2*hr+c*hr,hr),hr); to=pl.ds(pl.multiple_of((4*i+s)*hr,hr),hr)
            so_ref[to,:]=ot_ref[src,:]; sa_ref[to,:]=ai_ref[src,:]
            return 0
        lax.fori_loop(0,4,move,0)
    def part(i,_):
        c=pl.ds(pl.multiple_of(i*256,256),256)
        for k,(a,b) in enumerate(((so_ref,g_ref),(sa_ref,dq_ref))):
            w=dotf(a[...],b[:,c]).astype(BF).reshape(8,hr,256); to=pl.ds(pl.multiple_of(k*D+i*256,256),256)
            send_ref[:,:,to]=w[:4]; keep_ref[:,:,to]=w[4:]
        return 0
    lax.fori_loop(0,D//256,part,0)
    qb_ref[...]=jnp.sum(dq_ref[...].astype(F32),0,keepdims=True)
def wgrad(sc,g,o,dq,ai):
    N,D=g.shape
    args=(g,o,dq,ai)
    part=pl.BlockSpec((4,D//8,2*D),lambda j,s:(0,0,0)); out=hs((4,D//8,2*D+128),BF)
    return pl.pallas_call(wgrad_kernel,
        grid_spec=pltpu.PrefetchScalarGridSpec(num_scalar_prefetch=1,grid=(1,),in_specs=[whole(a) for a in args],out_specs=[part,part,pl.BlockSpec((1,D),lambda j,s:(0,0))],
            scratch_shapes=[pltpu.VMEM((D,N),BF)]*3),
        out_shape=[out,out,hs((1,D),F32)],cost_estimate=cost(2.6e9,9e6),compiler_params=params(1,30),name="wgrad")(sc,*args)
def kvgrad_kernel(sc,da_ref,db_ref,ra_ref,rb_ref,tab_ref,ai_ref,_k,_s,keep_ref,send_ref,dkv_ref,kvb_ref,w_ref):
    D,N=ai_ref.shape; T=N//2; hr=D//8
    for i,(ref,rr) in enumerate(((da_ref,ra_ref),(db_ref,rb_ref))):
        sl=slice(i*T,(i+1)*T)
        dkv_ref[sl,:]=rope_kv((ref[...]+rr[...].astype(F32)).T,tab_ref[sl,:128],tab_ref[sl,128:],-1).astype(BF)
    kvb_ref[...]=jnp.sum(dkv_ref[...].astype(F32),0,keepdims=True)
    w_ref[...]=dotf(ai_ref[...],dkv_ref[...])
    for dst,c in ((send_ref,1-sc[0]),(keep_ref,sc[0])):
        for s in range(4):
            dst[s]=w_ref[pl.ds(pl.multiple_of(s*2*hr+c*hr,hr),hr),:].astype(BF)
def kvgrad(sc,d0,d1,r0,r1,tab,ai,keep,send):
    D,N=ai.shape
    args=(d0,d1,r0,r1,tab,ai)
    col=pl.BlockSpec((4,D//8,128),lambda j,s:(0,0,2*D//128))
    outs=[hs(keep.shape,BF),hs(send.shape,BF),hs((N,128),BF),hs((1,128),F32)]
    return pl.pallas_call(kvgrad_kernel,
        grid_spec=pltpu.PrefetchScalarGridSpec(num_scalar_prefetch=1,grid=(1,),in_specs=[whole(a) for a in args]+[ANY,ANY],out_specs=[col,col,whole(outs[2]),whole(outs[3])],
            scratch_shapes=[pltpu.VMEM((D,128),F32)]),
        out_shape=outs,input_output_aliases={7:0,8:1},cost_estimate=cost(2e8,4e6),compiler_params=params(1,16),name="kvgrad")(sc,*args,keep,send)
def rows_of(w,B): return pl.BlockSpec((B,w),lambda j:(j,0))
def product_kernel(dims,a_ref,w_ref,out_ref):
    @pl.when(pl.program_id(0)==0)
    def _(): out_ref[...]=jnp.zeros_like(out_ref)
    out_ref[...]+=dotf(a_ref[...],w_ref[...],dims)
def product(a,w,across,name):
    N,F=a.shape; D=w.shape[0] if across else w.shape[1]
    ws=pl.BlockSpec((D,D),(lambda j:(0,j)) if across else (lambda j:(j,0)))
    return pl.pallas_call(functools.partial(product_kernel,NT if across else NN),grid=(F//D,),
      in_specs=[pl.BlockSpec((N,D),lambda j:(0,j)),ws],out_specs=pl.BlockSpec((N,D),lambda j:(0,0)),out_shape=hs((N,D),F32),
      cost_estimate=cost(4.8e9,1.4e7),compiler_params=params(1,26),name=name)(stay(a),stay(w))
def postb_kernel(x_ref,g_ref,dq_ref,dkv_ref,c2_ref,wq_ref,wk_ref,wv_ref,vec_ref,qb_ref,hb_ref,kvb_ref,ig_ref,sm_ref):
    j=pl.program_id(0)
    @pl.when(j==0)
    def _():
        sm_ref[...]=jnp.zeros_like(sm_ref)
        sm_ref[5:6,:]=qb_ref[...]; sm_ref[6:10,:]=hb_ref[...]; sm_ref[10:11,:kvb_ref.shape[1]]=kvb_ref[...]
    g=g_ref[...].astype(F32)
    n,s=ln(x_ref[...].astype(F32))
    dkv=dkv_ref[...]
    c1=dotf(dq_ref[...],wq_ref[...],NT)+dotf(dkv[:,:64],wk_ref[...])+dotf(dkv[:,64:],wv_ref[...])
    c2=c2_ref[...]
    u=c1*vec_ref[V_G1:V_G1+1,:]+c2*vec_ref[V_G2:V_G2+1,:]
    ig_ref[...]=g+s*(u-jnp.mean(u,-1,keepdims=True)-n*jnp.mean(u*n,-1,keepdims=True))
    for i,v in enumerate((c1*n,c1,c2*n,c2,g)):
        sm_ref[i:i+1,:]+=jnp.sum(v,0,keepdims=True)
def postb(x,g,dq,dkv,c2,wq,wk,wv,vec,qb,hb,kvb,B=256):
    N,D=x.shape
    return pl.pallas_call(postb_kernel,grid=(N//B,),
      in_specs=[rows_of(D,B)]*3+[rows_of(128,B),rows_of(D,B)]+[whole(a) for a in (wq,wk,wv,vec,qb,hb,kvb)],
      out_specs=[rows_of(D,B),pl.BlockSpec((16,D),lambda j:(0,0))],
      out_shape=[hs((N,D),F32),hs((16,D),F32)],
      cost_estimate=cost(2e9,1.2e7),compiler_params=params(1,26),name="postb")(*[stay(v) for v in (x,g,dq,dkv,c2,wq,wk,wv)],vec,qb,hb,kvb)
def posta_kernel(x_ref,o_ref,mb_ref,wo_ref,vec_ref,lo_ref):
    lo_ref[...]=(x_ref[...].astype(F32)+(dotf(o_ref[...],wo_ref[...])+vec_ref[V_O:V_O+1,:])+(mb_ref[...]+vec_ref[V_D:V_D+1,:])).astype(BF)
def posta(x,o,mb,wo,vec,B=256):
    N,D=x.shape
    return pl.pallas_call(posta_kernel,grid=(N//B,),
      in_specs=[rows_of(D,B)]*3+[whole(a) for a in (wo,vec)],
      out_specs=rows_of(D,B),out_shape=hs((N,D),BF),
      cost_estimate=cost(2e9,9e6),compiler_params=params(1,20),name="posta")(*[stay(v) for v in (x,o,mb,wo)],vec)
def final_kernel(sc,m_ref,mr_ref,a_ref,ar_ref,s_ref,sr_ref,w1_ref,w2_ref,wo_ref,wq_ref,wk_ref,wv_ref,
                 n1g_ref,n1b_ref,n2g_ref,n2b_ref,ob_ref,qb_ref,db_ref,hb_ref,kb_ref,vb_ref,kv_ref):
    W=w2_ref.shape[0]//2; D=m_ref.shape[1]; q=D//4; hr=a_ref.shape[0]; pr=hr//4; mr=m_ref.shape[0]//4
    for r0,(m,a) in enumerate(((m_ref,a_ref),(mr_ref,ar_ref))):
        h=sc[0]^r0
        def piece(k,_):
            i=sc[2+2*r0]^(k>>1); j=sc[3+2*r0]^(k&1)
            src=pl.ds(pl.multiple_of(k*mr,mr),mr)
            @pl.when(i==0)
            def _(): w2_ref[pl.ds(pl.multiple_of(h*W+j*mr,mr),mr),:]=m[src,:].astype(F32)
            @pl.when(i!=0)
            def _():
                for c in (0,1):
                    w1_ref[:,pl.ds(pl.multiple_of((2*j+c)*2*W+h*W,W),W)]=m[src,c*W:(c+1)*W].astype(F32)
            return 0
        lax.fori_loop(0,4,piece,0)
        for k in range(4):
            i=sc[2+2*r0]^(k>>1); j=sc[3+2*r0]^(k&1)
            to=pl.ds(pl.multiple_of(h*hr+i*2*pr+j*pr,pr),pr)
            wo_ref[to,:]=a[k*pr:(k+1)*pr,:D].astype(F32)
            wq_ref[to,:]=a[k*pr:(k+1)*pr,D:2*D].astype(F32)
            kv_ref[to,:]=a[k*pr:(k+1)*pr,2*D:].astype(F32)
    keys=kv_ref[...].T
    wk_ref[...]=keys[:64]; wv_ref[...]=keys[64:]
    t=s_ref[...]+sr_ref[...]
    for s in range(4):
        @pl.when(sc[1]==s)
        def _():
            for k,ref in enumerate((n1g_ref,n1b_ref,n2g_ref,n2b_ref,ob_ref,qb_ref)):
                ref[...]=t[k:k+1,s*q:(s+1)*q].reshape(q)
            db_ref[...]=t[4:5,s*q:(s+1)*q].reshape(q)
            hb_ref[...]=t[6+s:7+s,:].reshape(D)
            n=kb_ref.shape[0]; kb_ref[...]=t[10:11,s*n:(s+1)*n].reshape(n)
            n=vb_ref.shape[0]; vb_ref[...]=t[10:11,64+s*n:64+(s+1)*n].reshape(n)
def final(sc,m,mr,a,ar,s,sr,F,rotd):
    D=m.shape[1]; f=F32; v=hs((D//4,),f)
    outs=[hs((D//4,F),f),hs((F//4,D),f),hs((D//4,D),f),hs((D//4,D),f),hs((64,D//4),f),hs((64,D//4),f)]+[v]*7+[hs((D,),f),hs((rotd//4,),f),hs((16,),f)]
    return pl.pallas_call(final_kernel,
        grid_spec=pltpu.PrefetchScalarGridSpec(num_scalar_prefetch=1,grid=(1,),in_specs=[whole(u) for u in (m,mr,a,ar,s,sr)],out_specs=[whole(u) for u in outs],
            scratch_shapes=[pltpu.VMEM((D//4,128),F32)]),
        out_shape=outs,cost_estimate=cost(1e6,9e6),compiler_params=params(1,24),name="final")(sc,m,mr,a,ar,s,sr)
def bits_of(n):
    return n.bit_length()-1
def after(xs,*deps):
    out=lax.optimization_barrier(tuple(xs)+tuple(deps))
    return out[:len(xs)]
def dp_stages():
    dp=lax.axis_size("dp"); nb=bits_of(dp); i=lax.axis_index("dp")
    core=i&1
    st=[(core,[(k,k^1) for k in range(dp)],core)]
    for t in range(1,nb):
        up,down=t,nb-t
        a,b=(i>>up)&1,(i>>down)&1
        st.append((jnp.where(core==0,a,b),[(k,k^((1<<up) if k%2==0 else (1<<down))) for k in range(dp)],jnp.where(core==0,b,a)))
    return st
def pick(G,bit,ax): return lax.dynamic_index_in_dim(G,bit,ax,keepdims=False)
def add(a,b): return (a.astype(F32)+b.astype(F32)).astype(a.dtype)
class Stream:
    def __init__(self,stages,at,send,keep):
        self.st=stages; self.at=at; self.send=send; self.keep=keep; self.left=len(stages)
    def go(self):
        n=len(self.st)
        if self.at<n: axis,pairs="dp",self.st[self.at][1]
        else: axis="sp"; pairs=[(k,k^(1<<(self.at-n))) for k in range(lax.axis_size("sp"))]
        self.recv=lax.ppermute(self.send,axis,pairs)
        return self.recv
    def land(self):
        k,r=self.keep,self.recv; self.at+=1
        n=len(self.st); s=lax.axis_index("sp")
        if self.at<n:
            split=lambda t: t.reshape(t.shape[0],2,t.shape[1]//2,t.shape[2]); bit=self.st[self.at][0]; ax=1
        elif self.at==n:
            split=lambda t: t.reshape(2,2,t.shape[1],t.shape[2]); bit=s&1; ax=1
        elif self.at==n+1:
            split=lambda t: t; bit=s>>1; ax=0
        else:
            self.own=add(k,r); self.left=n
            return
        k,r=split(k),split(r)
        self.send=add(pick(k,1-bit,ax),pick(r,1-bit,ax))
        self.keep=add(pick(k,bit,ax),pick(r,bit,ax))
    def gather_go(self):
        self.left-=1
        self.recv=lax.ppermute(self.own,"dp",self.st[self.left][1])
        return self.recv
    def gather_land(self):
        self.own=jnp.concatenate([self.own,self.recv],0)
    def settle(self,x,of):
        n=len(self.st)
        if n<=3: return x
        g=x.reshape((4,)+(2,)*(n-3)+(-1,x.shape[1]))
        for t in range(3,n): g=jnp.where(self.st[t][of]==0,g,jnp.flip(g,t-2))
        return g.reshape(x.shape)
def on_device(inputs,out_grad,segment_ids,positions,norm1_gain,norm1_bias,norm2_gain,norm2_bias,query_weight,query_bias,key_weight,key_bias,value_weight,value_bias,output_weight,output_bias,hidden_weight,hidden_bias,down_weight,down_bias):
    sp=lax.axis_size("sp"); s=lax.axis_index("sp")
    R,T,D=inputs.shape; hd=key_weight.shape[1]; rotd=key_bias.shape[0]
    F=hidden_weight.shape[1]
    N=R*T
    x=inputs.reshape(N,D); g=out_grad.reshape(N,D)
    vec=table(norm1_gain,norm1_bias,norm2_gain,norm2_bias,query_bias,output_bias,down_bias,key_bias,value_bias,hidden_bias)
    pos=lax.dynamic_slice_in_dim(positions,s*T,T,1)
    st=dp_stages(); core=st[0][0]; bit1=st[1][0]
    both=[(i,i^1) for i in range(sp)]
    Ms,act,gp,dbs,mi=mlp_half(jnp.stack([1-core,bit1]),x,g,hidden_weight,down_weight,vec)
    Mr=lax.ppermute(Ms,"dp",st[0][1])
    pf=pos.astype(F32).reshape(N)
    freq=10000.0**(-(jnp.arange(rotd//2,dtype=F32)*2.0)/rotd)
    ang=pf[None,:]*freq[:,None]
    ds=(jnp.arange(T,dtype=F32)[None,:]-pos.astype(F32)).reshape(1,N)
    cs=jnp.concatenate([jnp.cos(ang),jnp.sin(ang),ds,jnp.zeros((7,N),F32)],0)
    xq,=after([x],dbs)
    q,kv,do,tab,ai=pre(xq,g,cs,query_weight,key_weight.T,value_weight.T,output_weight,vec)
    kv,Mr=after([kv,Mr],q)
    kvp=lax.ppermute(kv,"sp",both)
    mi,=after([mi],q)
    keep,send,act,gp,dbk=mlp_half(jnp.stack([core,bit1]),mi,g,hidden_weight,down_weight,vec,recv=Mr,dbs=dbs,act=act,gp=gp)
    M=Stream(st,1,send,keep)
    M.send,kvp=after([M.send,kvp],dbk)
    M.go()
    q,=after([q],dbk)
    o,dq,d0,k0,part=attn_part(0,2*(D//256)*2//3,q,do,kv,kvp,tab,T=T)
    M.recv,k0=after([M.recv,k0],dq)
    M.land()
    r0=lax.ppermute(k0,"sp",both); M.go()
    o,dq=after([o,dq],M.send,k0)
    o,dq,d1,k1=attn_part(2*(D//256)*2//3,2*(D//256)-2*(D//256)*2//3,q,do,kv,kvp,tab,prev=(o,dq,part),T=T)
    k1,M.recv,r0=after([k1,M.recv,r0],dq)
    r1=lax.ppermute(k1,"sp",both)
    while True:
        M.land()
        if M.at>=len(st): break
        M.go()
    o_,=after([o],M.send,k1)
    sc=core.reshape(1)
    wkeep,wsend,qb=wgrad(sc,g,o_,dq,ai)
    M.send,wkeep,wsend,r1=after([M.send,wkeep,wsend,r1],qb)
    M.send,=after([M.send],r1)
    M.go()
    r1,=after([r1],M.send)
    wkeep,wsend,dkv,kvb=kvgrad(sc,d0,d1,r0,r1,tab,ai,wkeep,wsend)
    A=Stream(st,0,wsend,wkeep)
    small=None
    todo=[("dp",p) for _,p,_o in st]+[("sp",[(i,i^(1<<k)) for i in range(sp)]) for k in range(bits_of(sp))]
    c2=mb=ig=lo=sm=None
    fill=["mb","c2","ig","lo"]
    held=1
    busy=True
    while True:
        rs=A.at<len(st)+2
        ag=not rs and A.left>1
        if not (rs or ag or busy or M.left>1 or len(todo)>1): break
        if rs: A.go(); moved=[A.send]
        elif ag: A.gather_go(); moved=[A.own]
        else: moved=[]
        if not busy:
            if M.at<len(st)+2: M.go(); busy=True; held=1; moved.append(M.send)
            elif M.left>1: moved.append(M.own); M.gather_go(); busy=True; held=0 if M.left>1 else 1
        sr=None
        if small is not None and len(todo)>1: axis,pairs=todo.pop(0); sr=lax.ppermute(small,axis,pairs); moved.append(small)
        deps=[]
        if fill:
            k=fill.pop(0)
            if k=="c2": gk,=after([gp],*moved); c2=product(gk,hidden_weight,True,"back"); deps=[c2]
            if k=="ig": xk,=after([x],*moved); ig,sm=postb(xk,g,dq,dkv,c2,query_weight,key_weight.T,value_weight.T,vec,qb,dbk,kvb); deps=[ig]
            if k=="mb": ak,=after([act],*moved); mb=product(ak,down_weight,False,"down"); deps=[mb]
            if k=="lo": xk,=after([x],*moved); lo=posta(xk,o,mb,output_weight,vec); deps=[lo]
        lands=busy and held==0
        got=([A.recv] if rs or ag else [])+([M.recv] if lands else [])+([sr] if sr is not None else [])
        got=list(after(got,*deps))
        if rs or ag: A.recv=got.pop(0)
        if lands: M.recv=got.pop(0)
        if sr is not None: small=small+got.pop(0)
        if rs: A.land()
        elif ag: A.gather_land()
        if lands:
            busy=False
            if M.at<len(st)+2: M.land()
            else: M.gather_land()
        held-=1
        if small is None and ig is not None:
            small=sm
    Mr=lax.ppermute(M.own,"dp",st[0][1])
    Ar=lax.ppermute(A.own,"dp",st[0][1])
    axis,pairs=todo.pop(0)
    sr=lax.ppermute(small,axis,pairs)
    zero=jnp.zeros_like(core)
    where=jnp.stack([core,s]+[st[t][of] if len(st)>t else zero for of in (0,2) for t in (1,2)])
    rw1,rw2,ro,rq,rk,rv,n1g,n1b,n2g,n2b,ob,qbg,db,hb,kb,vb=final(where,M.settle(M.own,0),M.settle(Mr,2),A.settle(A.own,0),A.settle(Ar,2),small,sr,F,rotd)
    return (lo.reshape(R,T,D),ig.reshape(R,T,D),n1g,n1b,n2g,n2b,rq,qbg,rk.T,kb,rv.T,vb,ro,ob,rw1,hb,rw2,db)
def solution(mesh):
    t=P("dp","sp",None); m=P("dp",None); w=P()
    v=P("sp"); v2=P("sp",None)
    return jax.shard_map(on_device,mesh=mesh,in_specs=(t,t,m,m)+(w,)*16,
        out_specs=(t,t,v,v,v,v,v2,v,v2,v,v2,v,v2,v,v2,v,v2,v),check_vma=False)
```

```python
import functools
import jax
import jax.numpy as jnp
from jax import lax
from jax.experimental import pallas as pl
from jax.experimental.pallas import tpu as pltpu
from jax.sharding import PartitionSpec as P
EPS=1e-5
VMEM_ALL=67043328
NN=(((1,),(0,)),((),()))
NT=(((1,),(1,)),((),()))
TN=(((0,),(0,)),((),()))
BF=jnp.bfloat16
F32=jnp.float32
NEG=-1e30
C1=0.7071067811865476
C2=0.3989422804014327
def dotf(a,b,dims=NN):
    return lax.dot_general(a,b,dims,preferred_element_type=F32)
def ln(xv):
    m=jnp.mean(xv,-1,keepdims=True); c=xv-m
    s=lax.rsqrt(jnp.mean(c*c,-1,keepdims=True)+EPS)
    return c*s,s
def cost(flops,bytes_):
    return pl.CostEstimate(flops=int(flops),bytes_accessed=int(bytes_),transcendentals=0)
def params(n,mb):
    return pltpu.CompilerParams(dimension_semantics=("arbitrary",)*n,vmem_limit_bytes=VMEM_ALL if mb is None else mb<<20)
ANY=pl.BlockSpec(memory_space=pl.ANY)
hs=jax.ShapeDtypeStruct
def stay(v):
    return pltpu.with_memory_space_constraint(v,pltpu.HBM)
def whole(a):
    z=(0,)*len(a.shape)
    return pl.BlockSpec(a.shape,lambda *_: z)
def lane_iota(shape):
    return lax.broadcasted_iota(jnp.int32,shape,len(shape)-1)
V_G1,V_B1,V_G2,V_B2,V_Q,V_KV,V_O,V_D,V_H=range(9)
def table_kernel(*refs):
    *vs,kb_ref,vb_ref,hb_ref,out_ref=refs
    D=out_ref.shape[1]
    for k,ref in zip((V_G1,V_B1,V_G2,V_B2,V_Q,V_O,V_D),vs):
        out_ref[k:k+1,:]=ref[...].astype(F32).reshape(1,D)
    n=kb_ref.shape[0]; h=vb_ref.shape[0]
    out_ref[V_KV:V_KV+1,:]=jnp.zeros((1,D),F32)
    out_ref[V_KV:V_KV+1,:n]=kb_ref[...].astype(F32).reshape(1,n)
    out_ref[V_KV:V_KV+1,h:2*h]=vb_ref[...].astype(F32).reshape(1,h)
    for i in range(4):
        out_ref[V_H+i:V_H+i+1,:]=hb_ref[i*D:(i+1)*D].astype(F32).reshape(1,D)
def table(*vs):
    return pl.pallas_call(table_kernel,out_shape=hs((V_H+4,vs[0].shape[0]),F32),compiler_params=params(0,None),name="table")(*vs)
def rope_apply(v,C,S,sign):
    l=lane_iota(v.shape)&63
    sh=jnp.where(l<8,pltpu.roll(v,120,1),jnp.where(l<16,pltpu.roll(v,8,1),0.0))
    return v*C+S*sh if sign>0 else v*C-S*sh
def rope_kv(v,C,S,sign):
    l=lane_iota(v.shape)
    return rope_apply(v,jnp.where(l<64,C,1.0),jnp.where(l<64,S,0.0),sign)
def pre_kernel(x_ref,g_ref,cs_ref,wq_ref,wk_ref,wv_ref,wo_ref,vec_ref,q_ref,kv_ref,do_ref,tab_ref,ai_ref):
    B=x_ref.shape[0]
    row=lambda k: vec_ref[k:k+1,:]
    n,_=ln(x_ref[...].astype(F32))
    ai=(n*row(V_G1)+row(V_B1)).astype(BF)
    ai_ref[...]=ai.T
    t=cs_ref[...]
    t=jnp.concatenate([t,jnp.zeros((128-t.shape[0],B),F32)],0).T
    l=lane_iota((B,128))
    co=jnp.where(l<8,t,0.0)
    c2=co+pltpu.roll(co,8,1)
    C=c2+pltpu.roll(c2,64,1)+jnp.where((l&63)>=16,1.0,0.0)
    sb=jnp.where((l>=8)&(l<16),t,0.0)
    s2=sb-pltpu.roll(sb,120,1)
    S=s2+pltpu.roll(s2,64,1)
    tab_ref[:,:128]=C
    tab_ref[:,128:]=jnp.where(l==127,pltpu.roll(t,111,1),S)
    q=dotf(ai,wq_ref[...])+row(V_Q)
    do=dotf(g_ref[...],wo_ref[...],NT)
    for k in range(q.shape[1]//128):
        c=slice(k*128,k*128+128)
        q_ref[k]=(rope_apply(q[:,c],C,S,1)*0.125).astype(BF)
        do_ref[k]=do[:,c].astype(BF)
    kv=jnp.concatenate([dotf(ai,wk_ref[...],NT),dotf(ai,wv_ref[...],NT)],1)+row(V_KV)[:,:128]
    kv_ref[...]=rope_kv(kv,C,S,1).astype(BF)
def pre(x,g,cs,wq,wk,wv,wo,vec,B=256):
    N,D=x.shape; NP=D//128
    row=lambda w: pl.BlockSpec((B,w),lambda j:(j,0))
    pair=pl.BlockSpec((NP,B,128),lambda j:(0,j,0)); col=lambda h: pl.BlockSpec((h,B),lambda j:(0,j))
    return pl.pallas_call(pre_kernel,grid=(N//B,),
      in_specs=[row(D),row(D),col(cs.shape[0])]+[whole(a) for a in (wq,wk,wv,wo,vec)],
      out_specs=[pair,row(128),pair,row(256),col(D)],
      out_shape=[hs((NP,N,128),BF),hs((N,128),BF),hs((NP,N,128),BF),hs((N,256),F32),hs((D,N),BF)],
      cost_estimate=cost(4e9,1e7),compiler_params=params(1,None),name="pre")(x,g,cs,wq,wk,wv,wo,vec)
def mlp_kernel(last,rows,*refs):
    if last:
        (sc,x_ref,g_ref,wa_ref,wb_ref,va_ref,vb_ref,vec_ref,r2_ref,r1_ref,dbs_ref,_a,_g,
         keep_ref,send_ref,act_hbm,gp_hbm,db_ref,w1_ref,w2_ref,b_ref,act_ref,gp_ref,sem)=refs
        mi_ref=x_ref
    else:
        (sc,x_ref,g_ref,wa_ref,wb_ref,va_ref,vb_ref,vec_ref,
         out_ref,act_hbm,gp_hbm,db_ref,mi_ref,w1_ref,w2_ref,b_ref,act_ref,gp_ref,sem)=refs
    j=pl.program_id(0); N,D=x_ref.shape; W=wa_ref.shape[1]
    h=sc[0]
    def copies(jj):
        out=[]
        for i,(scr,hbm) in enumerate(((act_ref,act_hbm),(gp_ref,gp_hbm))):
            for k in (0,1):
                off=pl.multiple_of((2*(2*jj+k)+h)*W,W)
                out.append(pltpu.make_async_copy(scr.at[:,k*W:(k+1)*W],hbm.at[:,pl.ds(off,W)],sem.at[i,k]))
        return out
    if not last:
        @pl.when(j==0)
        def _():
            def body(i,_):
                r=pl.ds(pl.multiple_of(i*256,256),256)
                n,_s=ln(x_ref[r,:].astype(F32))
                mi_ref[r,:]=(n*vec_ref[V_G2:V_G2+1,:]+vec_ref[V_B2:V_B2+1,:]).astype(BF)
                return 0
            lax.fori_loop(0,N//256,body,0)
    w1_ref[:,:W]=wa_ref[...]; w1_ref[:,W:]=wb_ref[...]
    w2_ref[:W,:]=va_ref[...]; w2_ref[W:,:]=vb_ref[...]
    lane=pl.ds(pl.multiple_of(h*W,128),W)
    b_ref[:,:W]=vec_ref[pl.ds(V_H+2*j,1),lane]; b_ref[:,W:]=vec_ref[pl.ds(V_H+2*j+1,1),lane]
    @pl.when(j>0)
    def _():
        for c in copies(j-1): c.wait()
    for r in range(0,N,rows):
        sl=slice(r,r+rows)
        pre_=dotf(mi_ref[sl,:],w1_ref[...])+b_ref[...]
        da=dotf(g_ref[sl,:],w2_ref[...],NT)
        phi=0.5*(1.0+lax.erf(pre_*C1))
        act_ref[sl,:]=(pre_*phi).astype(BF)
        gp_ref[sl,:]=(da*(phi+pre_*(jnp.exp(pre_*pre_*-0.5)*C2))).astype(BF)
    for c in copies(j): c.start()
    db=jnp.sum(gp_ref[...].astype(F32),0,keepdims=True)
    if last:
        other=pl.ds(pl.multiple_of((1-h)*W,128),W)
        for k in (0,1):
            db_ref[pl.ds(2*j+k,1),lane]=db[:,k*W:(k+1)*W]
            db_ref[pl.ds(2*j+k,1),other]=dbs_ref[j][:,k*W:(k+1)*W]
    else: db_ref[0]=db
    q=D//4
    to=pl.ds(pl.multiple_of(j*q,q),q)
    if last: bit=sc[1]
    def part(i,_):
        c=pl.ds(pl.multiple_of(i*256,256),256)
        d2=dotf(act_ref[...],g_ref[:,c],TN).reshape(2,W,256)
        d1=dotf(mi_ref[...],gp_ref[:,c],TN).reshape(4,q,256)
        if last:
            d2=(d2+r2_ref[:,:,c].astype(F32)).astype(BF)
            d1=(d1+r1_ref[:,:,c].astype(F32)).astype(BF)
            @pl.when(bit==0)
            def _():
                keep_ref[pl.ds(2*j,2),:,c]=d2; send_ref[:,to,c]=d1
            @pl.when(bit!=0)
            def _():
                send_ref[pl.ds(2*j,2),:,c]=d2; keep_ref[:,to,c]=d1
        else:
            out_ref[pl.ds(2*j,2),:W,c]=d2.astype(BF)
            out_ref[:,pl.ds(pl.multiple_of(W+j*q,q),q),c]=d1.astype(BF)
        return 0
    lax.fori_loop(0,2*W//256,part,0)
    @pl.when(j==pl.num_programs(0)-1)
    def _():
        for c in copies(j): c.wait()
def mlp_half(sc,x,g,w1,w2,vec,recv=None,dbs=None,act=None,gp=None,rows=256):
    N,D=x.shape; F=w1.shape[1]; W=F//8
    last=recv is not None
    cb=lambda sh,k,ax: pl.BlockSpec(sh,(lambda j,s:(0,2*(2*j+k)+s[0])) if ax else (lambda j,s:(2*(2*j+k)+s[0],0)))
    ins=[whole(x),whole(g),cb((D,W),0,1),cb((D,W),1,1),cb((W,D),0,0),cb((W,D),1,0),whole(vec)]
    args=[x,g,w1,w1,w2,w2,vec]
    ag=[hs((N,F),BF),hs((N,F),BF),hs((2,1,2*W),F32)]
    ags=[ANY,ANY,pl.BlockSpec((1,1,2*W),lambda j,s:(j,0,0))]
    alias={}; scr=[]
    if last:
        ins+=[pl.BlockSpec((2,W,D),lambda j,s:(j,0,0)),pl.BlockSpec((4,D//4,D),lambda j,s:(0,W//(D//4)+j,0)),whole(dbs),ANY,ANY]
        args+=[recv,recv,dbs,act,gp]
        outs=[hs((4,W,D),BF)]*2+ag[:2]+[hs((4,2*W),F32)]
        ospec=[whole(outs[0])]*2+ags[:2]+[whole(outs[-1])]
        alias={1+10:2,1+11:3}
    else:
        outs=[hs((4,2*W,D),BF)]+ag+[hs((N,D),BF)]
        ospec=[whole(outs[0])]+ags+[whole(outs[-1])]
    return pl.pallas_call(functools.partial(mlp_kernel,last,rows),
        grid_spec=pltpu.PrefetchScalarGridSpec(num_scalar_prefetch=1,grid=(2,),in_specs=ins,out_specs=ospec,
            scratch_shapes=[pltpu.VMEM((D,2*W),BF),pltpu.VMEM((2*W,D),BF),pltpu.VMEM((1,2*W),F32),
                            pltpu.VMEM((N,2*W),BF),pltpu.VMEM((N,2*W),BF),pltpu.SemaphoreType.DMA((2,2))]),
        out_shape=outs,input_output_aliases=alias,cost_estimate=cost(4*N*D*F*1.3,20e6),
        compiler_params=params(1,None),name="mlp_keep" if last else "mlp_send")(sc,*args)

def attn_kernel(base,per,RB,acc_in,q_ref,do_ref,kv_ref,kvp_ref,tab_ref,o_ref,dq_ref,own_ref,prev_ref,rest_ref,kx_ref,bias_ref,s_ref,d_ref,p_ref,ds_ref,acc_ref,qt_ref,oa_ref):
    first=pl.program_id(0)==0
    step=lax.rem(pl.program_id(0)+base,per)
    T=q_ref.shape[1]; QB=T//2
    @pl.when(first|(step==0))
    def _():
        for i,ref in enumerate((kvp_ref,kv_ref)):
            kv=ref[...].astype(F32)
            l=lane_iota(kv.shape)
            ke=jnp.where(l<64,kv,0.0); vo=jnp.where(l>=64,kv,0.0)
            sl=slice(i*T,(i+1)*T)
            kx_ref[0,sl,:]=ke.astype(BF)
            kx_ref[1,sl,:]=pltpu.roll(ke,64,1).astype(BF)
            kx_ref[2,sl,:]=pltpu.roll(vo,64,1).astype(BF)
            kx_ref[3,sl,:]=vo.astype(BF)
        def mask(i,_):
            r=pl.ds(pl.multiple_of(i*64,64),64)
            kk=lane_iota((64,2*T))-T
            qi=lax.broadcasted_iota(jnp.int32,(64,2*T),0)+i*64
            ok=(kk.astype(F32)>=tab_ref[r,255:256])&(kk<=qi)
            bias_ref[r,:]=jnp.where(ok,0.0,NEG)
            return 0
        lax.fori_loop(0,T//64,mask,0)
        if acc_in is None: acc_ref[...]=jnp.zeros_like(acc_ref)
        else: acc_ref[...]=acc_in[...]
    def run(lo):
        units=[(qb,e) for qb in (0,1) for e in (0,1)]
        rng=lambda qb: (lo,T+(qb+1)*QB)
        def mm1(u):
            qb,e=units[u]; a,b=rng(qb); n=b-a; z=u%2; rs=slice(qb*QB,(qb+1)*QB)
            qs=q_ref[:,rs,:].reshape(2*QB,128); dv=do_ref[:,rs,:].reshape(2*QB,128)
            if e==0:
                qt_ref[0,qb]=qs.T; qt_ref[1,qb]=dv.T
            s_ref[z,:,:n]=dotf(qs,kx_ref[e,a:b,:],NT)
            d_ref[z,:,:n]=dotf(dv,kx_ref[2+e,a:b,:],NT)
        def vp(u):
            qb,e=units[u]; a,b=rng(qb); n=b-a; z=u%2
            for r in range(0,2*QB,RB):
                rr=slice(r,r+RB); br=qb*QB+r%QB
                s=s_ref[z,rr,:n]+bias_ref[br:br+RB,a:b]
                m=jnp.max(s,-1,keepdims=True)
                p=jnp.exp(s-m)
                p=p*(1.0/jnp.sum(p,-1,keepdims=True))
                p_ref[z,rr,:n]=p.astype(BF)
                t=p*d_ref[z,rr,:n]
                ds_ref[z,rr,:n]=(t-p*jnp.sum(t,-1,keepdims=True)).astype(BF)
        def mm2(u):
            qb,e=units[u]; a,b=rng(qb); n=b-a; z=u%2; rs=slice(qb*QB,(qb+1)*QB)
            pb=p_ref[z,:,:n]; dsb=ds_ref[z,:,:n]
            o=dotf(pb,kx_ref[2+e,a:b,:]); dq=dotf(dsb,kx_ref[e,a:b,:])
            h=slice(e*64,e*64+64)
            acc_ref[:64,a:b]+=dotf(qt_ref[0,qb,h,:],dsb)
            acc_ref[64:,a:b]+=dotf(qt_ref[1,qb,h,:],pb)
            if e==0:
                oa_ref[0]=o; oa_ref[1]=dq
            else:
                oo=(oa_ref[0]+o).astype(BF)
                dq=((oa_ref[1]+dq)*0.125)
                C=tab_ref[rs,:128]; S=tab_ref[rs,128:]
                for k in (0,1):
                    o_ref[rs,k*128:(k+1)*128]=oo[k*QB:(k+1)*QB]
                    dq_ref[rs,k*128:(k+1)*128]=rope_apply(dq[k*QB:(k+1)*QB],C,S,-1).astype(BF)
        mm1(0)
        mm1(1); vp(0)
        mm2(0); mm1(2); vp(1)
        mm2(1); mm1(3); vp(2)
        mm2(2); vp(3)
        mm2(3)
    run(0)
    @pl.when(step==per-1)
    def _():
        prev_ref[...]=acc_ref[:,:T].astype(BF)
        own_ref[...]=acc_ref[:,T:]
    if rest_ref is not None:
        @pl.when(pl.program_id(0)==pl.num_programs(0)-1)
        def _(): rest_ref[...]=acc_ref[...]
def attn_part(base,count,q,do,kv,kvp,tab,prev=None,T=512,RB=32):
    NP,N,_=q.shape; QB=T//2; per=NP//2
    bf=BF; f=F32
    row=lambda h: lax.div(h+base,per); col=lambda h: lax.rem(h+base,per)
    hb=pl.BlockSpec((2,T,128),lambda h:(col(h),row(h),0)); rb=lambda w: pl.BlockSpec((T,w),lambda h:(row(h),0))
    c=lambda w: pl.BlockSpec((128,w),lambda h:(0,0)); ob=pl.BlockSpec((T,256),lambda h:(row(h),col(h)))
    more=prev is not None
    def body(q_ref,do_ref,kv_ref,kvp_ref,tab_ref,*refs):
        acc_in=None
        if more: acc_in=refs[0]; refs=refs[3:]
        o_ref,dq_ref,own_ref,prev_ref,*refs=refs
        rest_ref=None
        if not more: rest_ref,*refs=refs
        attn_kernel(base,per,RB,acc_in,q_ref,do_ref,kv_ref,kvp_ref,tab_ref,o_ref,dq_ref,own_ref,prev_ref,rest_ref,*refs)
    ins=[hb,hb,rb(128),rb(128),rb(256)]; args=[stay(v) for v in (q,do,kv,kvp,tab)]; alias={}
    outs=[hs((N,NP*128),bf)]*2+[hs((128,T),f),hs((128,T),bf)]; specs=[ob,ob,c(T),c(T)]
    if more:
        ins+=[c(2*T),ANY,ANY]; args+=[prev[2],prev[0],prev[1]]; alias={6:0,7:1}
    else:
        outs+=[hs((128,2*T),f)]; specs+=[c(2*T)]
    return pl.pallas_call(body,
      grid=(count,),in_specs=ins,out_specs=specs,
        scratch_shapes=[pltpu.VMEM((4,2*T,128),bf),pltpu.VMEM((T,2*T),f),pltpu.VMEM((2,2*QB,2*T),f),pltpu.VMEM((2,2*QB,2*T),f),
                        pltpu.VMEM((2,2*QB,2*T),bf),pltpu.VMEM((2,2*QB,2*T),bf),pltpu.VMEM((128,2*T),f),pltpu.VMEM((2,2,128,2*QB),bf),pltpu.VMEM((2,2*QB,128),f)],
      out_shape=outs,input_output_aliases=alias,cost_estimate=cost(8e9*count,1.4e6*count),
      compiler_params=params(1,28),name="attn_b" if more else "attn_a")(*args)
def wgrad_kernel(sc,g_ref,o_ref,dq_ref,ai_ref,keep_ref,send_ref,qb_ref,ot_ref,so_ref,sa_ref):
    N,D=o_ref.shape; hr=D//8
    def turn(i,_):
        r=pl.ds(pl.multiple_of(i*256,256),256); ot_ref[:,r]=o_ref[r,:].T
        return 0
    lax.fori_loop(0,N//256,turn,0)
    for i,c in enumerate((1-sc[0],sc[0])):
        def move(s,_):
            src=pl.ds(pl.multiple_of(s*2*hr+c*hr,hr),hr); to=pl.ds(pl.multiple_of((4*i+s)*hr,hr),hr)
            so_ref[to,:]=ot_ref[src,:]; sa_ref[to,:]=ai_ref[src,:]
            return 0
        lax.fori_loop(0,4,move,0)
    def part(i,_):
        c=pl.ds(pl.multiple_of(i*256,256),256)
        for k,(a,b) in enumerate(((so_ref,g_ref),(sa_ref,dq_ref))):
            w=dotf(a[...],b[:,c]).astype(BF).reshape(8,hr,256); to=pl.ds(pl.multiple_of(k*D+i*256,256),256)
            send_ref[:,:,to]=w[:4]; keep_ref[:,:,to]=w[4:]
        return 0
    lax.fori_loop(0,D//256,part,0)
    qb_ref[...]=jnp.sum(dq_ref[...].astype(F32),0,keepdims=True)
def wgrad(sc,g,o,dq,ai):
    N,D=g.shape
    args=(g,o,dq,ai)
    part=pl.BlockSpec((4,D//8,2*D),lambda j,s:(0,0,0)); out=hs((4,D//8,2*D+128),BF)
    return pl.pallas_call(wgrad_kernel,
        grid_spec=pltpu.PrefetchScalarGridSpec(num_scalar_prefetch=1,grid=(1,),in_specs=[whole(a) for a in args],out_specs=[part,part,pl.BlockSpec((1,D),lambda j,s:(0,0))],
            scratch_shapes=[pltpu.VMEM((D,N),BF)]*3),
        out_shape=[out,out,hs((1,D),F32)],cost_estimate=cost(2.6e9,9e6),compiler_params=params(1,30),name="wgrad")(sc,*args)
def kvgrad_kernel(sc,da_ref,db_ref,ra_ref,rb_ref,tab_ref,ai_ref,_k,_s,keep_ref,send_ref,dkv_ref,kvb_ref,w_ref):
    D,N=ai_ref.shape; T=N//2; hr=D//8
    for i,(ref,rr) in enumerate(((da_ref,ra_ref),(db_ref,rb_ref))):
        sl=slice(i*T,(i+1)*T)
        dkv_ref[sl,:]=rope_kv((ref[...]+rr[...].astype(F32)).T,tab_ref[sl,:128],tab_ref[sl,128:],-1).astype(BF)
    kvb_ref[...]=jnp.sum(dkv_ref[...].astype(F32),0,keepdims=True)
    w_ref[...]=dotf(ai_ref[...],dkv_ref[...])
    for dst,c in ((send_ref,1-sc[0]),(keep_ref,sc[0])):
        for s in range(4):
            dst[s]=w_ref[pl.ds(pl.multiple_of(s*2*hr+c*hr,hr),hr),:].astype(BF)
def kvgrad(sc,d0,d1,r0,r1,tab,ai,keep,send):
    D,N=ai.shape
    args=(d0,d1,r0,r1,tab,ai)
    col=pl.BlockSpec((4,D//8,128),lambda j,s:(0,0,2*D//128))
    outs=[hs(keep.shape,BF),hs(send.shape,BF),hs((N,128),BF),hs((1,128),F32)]
    return pl.pallas_call(kvgrad_kernel,
        grid_spec=pltpu.PrefetchScalarGridSpec(num_scalar_prefetch=1,grid=(1,),in_specs=[whole(a) for a in args]+[ANY,ANY],out_specs=[col,col,whole(outs[2]),whole(outs[3])],
            scratch_shapes=[pltpu.VMEM((D,128),F32)]),
        out_shape=outs,input_output_aliases={7:0,8:1},cost_estimate=cost(2e8,4e6),compiler_params=params(1,16),name="kvgrad")(sc,*args,keep,send)
def rows_of(w,B): return pl.BlockSpec((B,w),lambda j:(j,0))
def product_kernel(dims,a_ref,w_ref,out_ref):
    @pl.when(pl.program_id(0)==0)
    def _(): out_ref[...]=jnp.zeros_like(out_ref)
    out_ref[...]+=dotf(a_ref[...],w_ref[...],dims)
def product(a,w,across,name):
    N,F=a.shape; D=w.shape[0] if across else w.shape[1]
    ws=pl.BlockSpec((D,D),(lambda j:(0,j)) if across else (lambda j:(j,0)))
    return pl.pallas_call(functools.partial(product_kernel,NT if across else NN),grid=(F//D,),
      in_specs=[pl.BlockSpec((N,D),lambda j:(0,j)),ws],out_specs=pl.BlockSpec((N,D),lambda j:(0,0)),out_shape=hs((N,D),F32),
      cost_estimate=cost(4.8e9,1.4e7),compiler_params=params(1,26),name=name)(stay(a),stay(w))
def postb_kernel(x_ref,g_ref,dq_ref,dkv_ref,c2_ref,wq_ref,wk_ref,wv_ref,vec_ref,qb_ref,hb_ref,kvb_ref,ig_ref,sm_ref):
    j=pl.program_id(0)
    @pl.when(j==0)
    def _():
        sm_ref[...]=jnp.zeros_like(sm_ref)
        sm_ref[5:6,:]=qb_ref[...]; sm_ref[6:10,:]=hb_ref[...]; sm_ref[10:11,:kvb_ref.shape[1]]=kvb_ref[...]
    g=g_ref[...].astype(F32)
    n,s=ln(x_ref[...].astype(F32))
    dkv=dkv_ref[...]
    c1=dotf(dq_ref[...],wq_ref[...],NT)+dotf(dkv[:,:64],wk_ref[...])+dotf(dkv[:,64:],wv_ref[...])
    c2=c2_ref[...]
    u=c1*vec_ref[V_G1:V_G1+1,:]+c2*vec_ref[V_G2:V_G2+1,:]
    ig_ref[...]=g+s*(u-jnp.mean(u,-1,keepdims=True)-n*jnp.mean(u*n,-1,keepdims=True))
    for i,v in enumerate((c1*n,c1,c2*n,c2,g)):
        sm_ref[i:i+1,:]+=jnp.sum(v,0,keepdims=True)
def postb(x,g,dq,dkv,c2,wq,wk,wv,vec,qb,hb,kvb,B=256):
    N,D=x.shape
    return pl.pallas_call(postb_kernel,grid=(N//B,),
      in_specs=[rows_of(D,B)]*3+[rows_of(128,B),rows_of(D,B)]+[whole(a) for a in (wq,wk,wv,vec,qb,hb,kvb)],
      out_specs=[rows_of(D,B),pl.BlockSpec((16,D),lambda j:(0,0))],
      out_shape=[hs((N,D),F32),hs((16,D),F32)],
      cost_estimate=cost(2e9,1.2e7),compiler_params=params(1,26),name="postb")(*[stay(v) for v in (x,g,dq,dkv,c2,wq,wk,wv)],vec,qb,hb,kvb)
def posta_kernel(x_ref,o_ref,mb_ref,wo_ref,vec_ref,lo_ref):
    lo_ref[...]=(x_ref[...].astype(F32)+(dotf(o_ref[...],wo_ref[...])+vec_ref[V_O:V_O+1,:])+(mb_ref[...]+vec_ref[V_D:V_D+1,:])).astype(BF)
def posta(x,o,mb,wo,vec,B=256):
    N,D=x.shape
    return pl.pallas_call(posta_kernel,grid=(N//B,),
      in_specs=[rows_of(D,B)]*3+[whole(a) for a in (wo,vec)],
      out_specs=rows_of(D,B),out_shape=hs((N,D),BF),
      cost_estimate=cost(2e9,9e6),compiler_params=params(1,20),name="posta")(*[stay(v) for v in (x,o,mb,wo)],vec)
def final_kernel(sc,m_ref,mr_ref,a_ref,ar_ref,s_ref,sr_ref,w1_ref,w2_ref,wo_ref,wq_ref,wk_ref,wv_ref,
                 n1g_ref,n1b_ref,n2g_ref,n2b_ref,ob_ref,qb_ref,db_ref,hb_ref,kb_ref,vb_ref,kv_ref):
    W=w2_ref.shape[0]//2; D=m_ref.shape[1]; q=D//4; hr=a_ref.shape[0]; pr=hr//4; mr=m_ref.shape[0]//4
    for r0,(m,a) in enumerate(((m_ref,a_ref),(mr_ref,ar_ref))):
        h=sc[0]^r0
        def piece(k,_):
            i=sc[2+2*r0]^(k>>1); j=sc[3+2*r0]^(k&1)
            src=pl.ds(pl.multiple_of(k*mr,mr),mr)
            @pl.when(i==0)
            def _(): w2_ref[pl.ds(pl.multiple_of(h*W+j*mr,mr),mr),:]=m[src,:].astype(F32)
            @pl.when(i!=0)
            def _():
                for c in (0,1):
                    w1_ref[:,pl.ds(pl.multiple_of((2*j+c)*2*W+h*W,W),W)]=m[src,c*W:(c+1)*W].astype(F32)
            return 0
        lax.fori_loop(0,4,piece,0)
        for k in range(4):
            i=sc[2+2*r0]^(k>>1); j=sc[3+2*r0]^(k&1)
            to=pl.ds(pl.multiple_of(h*hr+i*2*pr+j*pr,pr),pr)
            wo_ref[to,:]=a[k*pr:(k+1)*pr,:D].astype(F32)
            wq_ref[to,:]=a[k*pr:(k+1)*pr,D:2*D].astype(F32)
            kv_ref[to,:]=a[k*pr:(k+1)*pr,2*D:].astype(F32)
    keys=kv_ref[...].T
    wk_ref[...]=keys[:64]; wv_ref[...]=keys[64:]
    t=s_ref[...]+sr_ref[...]
    for s in range(4):
        @pl.when(sc[1]==s)
        def _():
            for k,ref in enumerate((n1g_ref,n1b_ref,n2g_ref,n2b_ref,ob_ref,qb_ref)):
                ref[...]=t[k:k+1,s*q:(s+1)*q].reshape(q)
            db_ref[...]=t[4:5,s*q:(s+1)*q].reshape(q)
            hb_ref[...]=t[6+s:7+s,:].reshape(D)
            n=kb_ref.shape[0]; kb_ref[...]=t[10:11,s*n:(s+1)*n].reshape(n)
            n=vb_ref.shape[0]; vb_ref[...]=t[10:11,64+s*n:64+(s+1)*n].reshape(n)
def final(sc,m,mr,a,ar,s,sr,F,rotd):
    D=m.shape[1]; f=F32; v=hs((D//4,),f)
    outs=[hs((D//4,F),f),hs((F//4,D),f),hs((D//4,D),f),hs((D//4,D),f),hs((64,D//4),f),hs((64,D//4),f)]+[v]*7+[hs((D,),f),hs((rotd//4,),f),hs((16,),f)]
    return pl.pallas_call(final_kernel,
        grid_spec=pltpu.PrefetchScalarGridSpec(num_scalar_prefetch=1,grid=(1,),in_specs=[whole(u) for u in (m,mr,a,ar,s,sr)],out_specs=[whole(u) for u in outs],
            scratch_shapes=[pltpu.VMEM((D//4,128),F32)]),
        out_shape=outs,cost_estimate=cost(1e6,9e6),compiler_params=params(1,24),name="final")(sc,m,mr,a,ar,s,sr)
def bits_of(n):
    return n.bit_length()-1
def after(xs,*deps):
    out=lax.optimization_barrier(tuple(xs)+tuple(deps))
    return out[:len(xs)]
def dp_stages():
    dp=lax.axis_size("dp"); nb=bits_of(dp); i=lax.axis_index("dp")
    core=i&1
    st=[(core,[(k,k^1) for k in range(dp)],core)]
    for t in range(1,nb):
        up,down=t,nb-t
        a,b=(i>>up)&1,(i>>down)&1
        st.append((jnp.where(core==0,a,b),[(k,k^((1<<up) if k%2==0 else (1<<down))) for k in range(dp)],jnp.where(core==0,b,a)))
    return st
def pick(G,bit,ax): return lax.dynamic_index_in_dim(G,bit,ax,keepdims=False)
def add(a,b): return (a.astype(F32)+b.astype(F32)).astype(a.dtype)
class Stream:
    def __init__(self,stages,at,send,keep):
        self.st=stages; self.at=at; self.send=send; self.keep=keep; self.left=len(stages)
    def go(self):
        n=len(self.st)
        if self.at<n: axis,pairs="dp",self.st[self.at][1]
        else: axis="sp"; pairs=[(k,k^(1<<(self.at-n))) for k in range(lax.axis_size("sp"))]
        self.recv=lax.ppermute(self.send,axis,pairs)
        return self.recv
    def land(self):
        k,r=self.keep,self.recv; self.at+=1
        n=len(self.st); s=lax.axis_index("sp")
        if self.at<n:
            split=lambda t: t.reshape(t.shape[0],2,t.shape[1]//2,t.shape[2]); bit=self.st[self.at][0]; ax=1
        elif self.at==n:
            split=lambda t: t.reshape(2,2,t.shape[1],t.shape[2]); bit=s&1; ax=1
        elif self.at==n+1:
            split=lambda t: t; bit=s>>1; ax=0
        else:
            self.own=add(k,r); self.left=n
            return
        k,r=split(k),split(r)
        self.send=add(pick(k,1-bit,ax),pick(r,1-bit,ax))
        self.keep=add(pick(k,bit,ax),pick(r,bit,ax))
    def gather_go(self):
        self.left-=1
        self.recv=lax.ppermute(self.own,"dp",self.st[self.left][1])
        return self.recv
    def gather_land(self):
        self.own=jnp.concatenate([self.own,self.recv],0)
    def settle(self,x,of):
        n=len(self.st)
        if n<=3: return x
        g=x.reshape((4,)+(2,)*(n-3)+(-1,x.shape[1]))
        for t in range(3,n): g=jnp.where(self.st[t][of]==0,g,jnp.flip(g,t-2))
        return g.reshape(x.shape)
def on_device(inputs,out_grad,segment_ids,positions,norm1_gain,norm1_bias,norm2_gain,norm2_bias,query_weight,query_bias,key_weight,key_bias,value_weight,value_bias,output_weight,output_bias,hidden_weight,hidden_bias,down_weight,down_bias):
    sp=lax.axis_size("sp"); s=lax.axis_index("sp")
    R,T,D=inputs.shape; hd=key_weight.shape[1]; rotd=key_bias.shape[0]
    F=hidden_weight.shape[1]
    N=R*T
    x=inputs.reshape(N,D); g=out_grad.reshape(N,D)
    vec=table(norm1_gain,norm1_bias,norm2_gain,norm2_bias,query_bias,output_bias,down_bias,key_bias,value_bias,hidden_bias)
    pos=lax.dynamic_slice_in_dim(positions,s*T,T,1)
    st=dp_stages(); core=st[0][0]; bit1=st[1][0]
    both=[(i,i^1) for i in range(sp)]
    Ms,act,gp,dbs,mi=mlp_half(jnp.stack([1-core,bit1]),x,g,hidden_weight,down_weight,vec)
    Mr=lax.ppermute(Ms,"dp",st[0][1])
    pf=pos.astype(F32).reshape(N)
    freq=10000.0**(-(jnp.arange(rotd//2,dtype=F32)*2.0)/rotd)
    ang=pf[None,:]*freq[:,None]
    ds=(jnp.arange(T,dtype=F32)[None,:]-pos.astype(F32)).reshape(1,N)
    cs=jnp.concatenate([jnp.cos(ang),jnp.sin(ang),ds,jnp.zeros((7,N),F32)],0)
    xq,=after([x],dbs)
    q,kv,do,tab,ai=pre(xq,g,cs,query_weight,key_weight.T,value_weight.T,output_weight,vec)
    kv,Mr=after([kv,Mr],q)
    kvp=lax.ppermute(kv,"sp",both)
    mi,=after([mi],q)
    keep,send,act,gp,dbk=mlp_half(jnp.stack([core,bit1]),mi,g,hidden_weight,down_weight,vec,recv=Mr,dbs=dbs,act=act,gp=gp)
    M=Stream(st,1,send,keep)
    M.send,kvp=after([M.send,kvp],dbk)
    M.go()
    q,=after([q],dbk)
    o,dq,d0,k0,part=attn_part(0,2*(D//256)*2//3,q,do,kv,kvp,tab,T=T)
    M.recv,k0=after([M.recv,k0],dq)
    M.land()
    r0=lax.ppermute(k0,"sp",both); M.go()
    o,dq=after([o,dq],M.send,k0)
    o,dq,d1,k1=attn_part(2*(D//256)*2//3,2*(D//256)-2*(D//256)*2//3,q,do,kv,kvp,tab,prev=(o,dq,part),T=T)
    k1,M.recv,r0=after([k1,M.recv,r0],dq)
    r1=lax.ppermute(k1,"sp",both)
    while True:
        M.land()
        if M.at>=len(st): break
        M.go()
    o_,=after([o],M.send,k1)
    sc=core.reshape(1)
    wkeep,wsend,qb=wgrad(sc,g,o_,dq,ai)
    M.send,wkeep,wsend,r1=after([M.send,wkeep,wsend,r1],qb)
    M.send,=after([M.send],r1)
    M.go()
    r1,=after([r1],M.send)
    wkeep,wsend,dkv,kvb=kvgrad(sc,d0,d1,r0,r1,tab,ai,wkeep,wsend)
    A=Stream(st,0,wsend,wkeep)
    small=None
    todo=[("dp",p) for _,p,_o in st]+[("sp",[(i,i^(1<<k)) for i in range(sp)]) for k in range(bits_of(sp))]
    c2=mb=ig=lo=sm=None
    fill=["","c2","ig","mb","lo"]
    held=1
    busy=True
    while True:
        rs=A.at<len(st)+2
        ag=not rs and A.left>1
        if not (rs or ag or busy or M.left>1 or len(todo)>1): break
        if rs: A.go(); moved=[A.send]
        elif ag: A.gather_go(); moved=[A.own]
        else: moved=[]
        if not busy:
            if M.at<len(st)+2: M.go(); busy=True; held=1; moved.append(M.send)
            elif M.left>1: moved.append(M.own); M.gather_go(); busy=True; held=0 if M.left>1 else 1
        sr=None
        if small is not None and len(todo)>1: axis,pairs=todo.pop(0); sr=lax.ppermute(small,axis,pairs); moved.append(small)
        deps=[]
        if fill:
            k=fill.pop(0)
            if k=="c2": gk,=after([gp],*moved); c2=product(gk,hidden_weight,True,"back"); deps=[c2]
            if k=="ig": xk,=after([x],*moved); ig,sm=postb(xk,g,dq,dkv,c2,query_weight,key_weight.T,value_weight.T,vec,qb,dbk,kvb); deps=[ig]
            if k=="mb": ak,=after([act],*moved); mb=product(ak,down_weight,False,"down"); deps=[mb]
            if k=="lo": xk,=after([x],*moved); lo=posta(xk,o,mb,output_weight,vec); deps=[lo]
        lands=busy and held==0
        got=([A.recv] if rs or ag else [])+([M.recv] if lands else [])+([sr] if sr is not None else [])
        got=list(after(got,*deps))
        if rs or ag: A.recv=got.pop(0)
        if lands: M.recv=got.pop(0)
        if sr is not None: small=small+got.pop(0)
        if rs: A.land()
        elif ag: A.gather_land()
        if lands:
            busy=False
            if M.at<len(st)+2: M.land()
            else: M.gather_land()
        held-=1
        if small is None and ig is not None:
            small=sm
    Mr=lax.ppermute(M.own,"dp",st[0][1])
    Ar=lax.ppermute(A.own,"dp",st[0][1])
    axis,pairs=todo.pop(0)
    sr=lax.ppermute(small,axis,pairs)
    zero=jnp.zeros_like(core)
    where=jnp.stack([core,s]+[st[t][of] if len(st)>t else zero for of in (0,2) for t in (1,2)])
    rw1,rw2,ro,rq,rk,rv,n1g,n1b,n2g,n2b,ob,qbg,db,hb,kb,vb=final(where,M.settle(M.own,0),M.settle(Mr,2),A.settle(A.own,0),A.settle(Ar,2),small,sr,F,rotd)
    return (lo.reshape(R,T,D),ig.reshape(R,T,D),n1g,n1b,n2g,n2b,rq,qbg,rk.T,kb,rv.T,vb,ro,ob,rw1,hb,rw2,db)
def solution(mesh):
    t=P("dp","sp",None); m=P("dp",None); w=P()
    v=P("sp"); v2=P("sp",None)
    return jax.shard_map(on_device,mesh=mesh,in_specs=(t,t,m,m)+(w,)*16,
        out_specs=(t,t,v,v,v,v,v2,v,v2,v,v2,v,v2,v,v2,v,v2,v),check_vma=False)
```
